32 devices in a mesh: replica: 4 (over x, core), fsdp: 8 (over z, y).
Axes of the slice: x: 2, y: 2, z: 4, core: 2. Of those that a mesh axis runs over, the one named last changes fastest.
Arguments:
- tokens: bfloat16 [32768, 768], P(('replica', 'fsdp')), may hold values from -6 to 6
- lengths: int32 [32], P(('replica', 'fsdp')), may hold values from 513 to 1024, as said below
- random_blocks: int32 [32, 16, 3], P(('replica', 'fsdp')), may hold values from 0 to 15, as said below
- qkv_weight: bfloat16 [768, 2304], P('fsdp'), may hold values from -0.21875 to 0.21875
- out_weight: bfloat16 [768, 768], P('fsdp'), may hold values from -1.75 to 1.75
- up_weight: bfloat16 [768, 3072], P('fsdp'), may hold values from -0.21875 to 0.21875
- down_weight: bfloat16 [3072, 768], P('fsdp'), may hold values from -0.109375 to 0.109375
- proj_bias: bfloat16 [4, 768], P(None, 'fsdp'), may hold values from -3 to 3
- up_bias: bfloat16 [3072], P('fsdp'), may hold values from -3 to 3
- norm_gain: bfloat16 [2, 768], P(None, 'fsdp'), may hold values from 0.5 to 1.5
- norm_bias: bfloat16 [2, 768], P(None, 'fsdp'), may hold values from -3 to 3
- cotangent: bfloat16 [32768, 768], P(('replica', 'fsdp')), may hold values from -6 to 6
Outputs:
- out: bfloat16 [32768, 768], P(('replica', 'fsdp'))
- input_grad: float32 [32768, 768], P(('replica', 'fsdp'))
- qkv_grad: float32 [768, 2304], P('fsdp')
- out_weight_grad: float32 [768, 768], P('fsdp')
- up_grad: float32 [768, 3072], P('fsdp')
- down_grad: float32 [3072, 768], P('fsdp')
- proj_bias_grad: float32 [4, 768], P(None, 'fsdp')
- up_bias_grad: float32 [3072], P('fsdp')
- gain_grad: float32 [2, 768], P(None, 'fsdp')
- norm_bias_grad: float32 [2, 768], P(None, 'fsdp')
The draws below stay inside these ranges and needn't reach their ends.
Inputs may be any that keep to these rules, and one draw needn't show every extreme that they name: Slot s holds one sequence of lengths[s] positions from its start; the rest is padding. Each entry of random_blocks[s] is below ceil(lengths[s] / 64), so random blocks lie inside the sequence.
All inputs are finite; a program needn't handle non-finite values.
Results may differ from the reference program's by a relative error of at most 0.017.
Values may be sent and summed in bfloat16 or wider, within the bound.
No kernel may reach another device: no remote copies, remote signals or barrier semaphores. Data moves between devices by JAX's collectives and lax.ppermute only.
A program may use at most 256 MiB of HBM per device.

```python
import math
import jax
import jax.numpy as jnp
from jax import lax

D = 768
H = 12
HD = 64
FF = 3072
BLK = 64
NR = 3
TOK_DEV = 1024
NB = 16
MIN_LEN = 513
SLOTS = 32
TOKENS = 32768


def slot_draw(key):
    base_key = jax.random.fold_in(key, 7)
    length_key, block_key = jax.random.split(base_key)
    lengths = jax.random.randint(length_key, (SLOTS,), MIN_LEN, TOK_DEV + 1, dtype=jnp.int32)
    lengths = lengths.at[0].set(TOK_DEV).at[SLOTS - 1].set(MIN_LEN)
    counts = (lengths + BLK - 1) // BLK
    raw_bits = jax.random.randint(block_key, (SLOTS, NB, NR), 0, 1 << 20, dtype=jnp.int32)
    chosen = raw_bits % counts[:, None, None]
    chosen = chosen.at[0, 0, 0].set(NB - 1)
    return (lengths, chosen)


def draw_lengths(key, part):
    return slot_draw(key)[0]


def draw_random_blocks(key, part):
    return slot_draw(key)[1]


def raised(values, stream_key, source, target, parts, factor):
    def block_of(dim):
        return (jnp.arange(values.shape[dim]) // (values.shape[dim] // parts)).reshape((-1,) + (1,) * (values.ndim - 1 - dim))

    near = jax.random.permutation(stream_key, parts)[block_of(target)]
    far = (block_of(target) + parts // 2) % parts
    return jnp.where((block_of(source) == near) | (block_of(source) == far), factor * values, values)


def block_levels(own_key, dims, cuts, low, high):
    loudness, own = 1.0, jax.random.fold_in(own_key, 6)
    for dim, parts in cuts:
        steps = jnp.exp(jax.random.uniform(jax.random.fold_in(own, dim), (parts,), jnp.float32, low / len(cuts), high / len(cuts)))
        loudness = loudness * jnp.repeat(steps, dims[dim] // parts).reshape([-1 if axis == dim else 1 for axis in range(len(dims))])
    return loudness


def centred(stream_key, extent, scale, most, cuts=(), kind=jnp.bfloat16):
    factor_of = block_levels(stream_key, extent, cuts, -0.22, 0.18) if cuts else 1.0
    values = jax.random.normal(stream_key, extent, jnp.float32) * scale * factor_of
    return jnp.minimum(jnp.maximum(values, -most), most).astype(kind)


def noise_with(stream_key, dims, deviation, bound, shards, heavy, kind=jnp.bfloat16):
    entries = deviation * jax.random.normal(stream_key, dims, jnp.float32)
    if shards:
        entries = entries * block_levels(stream_key, dims, shards, -0.22, 0.18)
    return jnp.clip(raised(entries, jax.random.fold_in(stream_key, 3), *heavy), -bound, bound).astype(kind)


def setup_inputs(seed: int = 0) -> dict:
    key_list = jax.random.split(jax.random.key(seed), 13)
    tokens = noise_with(key_list[0], (TOKENS, D), 1.0, 6.0, ((0, 32),), (0, 1, 32, 2.75))
    lengths = draw_lengths(jax.random.fold_in(key_list[12], 71), 0)
    random_blocks = draw_random_blocks(jax.random.fold_in(key_list[12], 71), 0)
    qkv_weight = centred(key_list[3], (D, 3 * D), D ** -0.5, 0.21875, ((0, 8),))
    out_weight = centred(key_list[4], (D, D), (D // 64) ** -0.5, 1.75, ((0, 8),))
    up_weight = centred(key_list[5], (D, FF), D ** -0.5, 0.21875, ((0, 8),))
    down_weight = centred(key_list[6], (FF, D), FF ** -0.5, 0.109375, ((0, 8),))
    proj_bias = centred(key_list[7], (4, D), 0.5, 3.0, ((1, 8),))
    up_bias = centred(key_list[8], (FF,), 0.5, 3.0, ((0, 8),))
    norm_gain = jnp.clip(1.0 + 0.1 * jax.random.normal(key_list[9], (2, D), jnp.float32), 0.5, 1.5).astype(jnp.bfloat16)
    norm_bias = centred(key_list[10], (2, D), 0.5, 3.0, ((1, 8),))
    cotangent = centred(key_list[11], (TOKENS, D), 1.0, 6.0, ((0, 32),))
    return {"tokens": tokens, "lengths": lengths, "random_blocks": random_blocks, "qkv_weight": qkv_weight, "out_weight": out_weight, "up_weight": up_weight, "down_weight": down_weight, "proj_bias": proj_bias, "up_bias": up_bias, "norm_gain": norm_gain, "norm_bias": norm_bias, "cotangent": cotangent}


@jax.custom_vjp
def low(v):
    return lax.optimization_barrier(v.astype(jnp.bfloat16)).astype(jnp.float32)

@jax.custom_vjp
def low_back(v):
    return v

def low_keep(v):
    return (low(v), None)

def low_pass(kept, grad):
    return (grad,)

def back_keep(v):
    return (v, None)

def back_low(kept, grad):
    return (low(grad),)
low.defvjp(low_keep, low_pass)
low_back.defvjp(back_keep, back_low)
norm_eps = 1e-06
highest = lax.Precision.HIGHEST

def rounded(values):
    return low(low_back(values))

def matmul(left, right):
    return jnp.dot(left, right, precision=highest)

def layer_norm(hidden, factor, offset):
    centre = hidden - lax.optimization_barrier(jnp.mean(hidden, axis=-1, keepdims=True))
    variance = lax.optimization_barrier(jnp.mean(centre * centre, axis=-1, keepdims=True))
    return centre * lax.rsqrt(variance + norm_eps) * factor + offset

def block_mask(length, chosen, seq_len, block_size):
    block_count = chosen.shape[0]
    blocks_used = (length + block_size - 1) // block_size
    query_block = jnp.arange(block_count, dtype=jnp.int32)[:, None]
    key_block = jnp.arange(block_count, dtype=jnp.int32)[None, :]
    nearby = jnp.abs(query_block - key_block) <= 1
    global_key = (key_block == 0) | (key_block == blocks_used - 1)
    global_query = (query_block == 0) | (query_block == blocks_used - 1)
    picked = jnp.any(chosen[:, None, :] == key_block[:, :, None], axis=2)
    allowed = (nearby | global_key | global_query | picked) & (key_block < blocks_used)
    spread_mask = jnp.repeat(jnp.repeat(allowed, block_size, axis=0), block_size, axis=1)
    key_pos = jnp.arange(seq_len, dtype=jnp.int32)[None, :]
    return spread_mask & (key_pos < length)

def slot_forward(params, inputs, mask, valid):
    qkv_weight, out_weight, up_weight, down_weight, proj_bias, up_bias, norm_gain, norm_bias = params
    seq_len = inputs.shape[0]
    scale = 1.0 / math.sqrt(HD)
    mixed = matmul(inputs, qkv_weight)
    queries = rounded(mixed[:, :D] + proj_bias[0])
    keys = rounded(mixed[:, D:2 * D]).reshape(seq_len, H, HD)
    values = rounded(mixed[:, 2 * D:] + proj_bias[1]).reshape(seq_len, H, HD)
    query_rows = min(512, seq_len)

    def attend(begin_row):
        query_block = lax.dynamic_slice_in_dim(queries, begin_row, query_rows, 0).reshape(query_rows, H, HD)
        mask_block = lax.dynamic_slice_in_dim(mask, begin_row, query_rows, 0)
        scores = jnp.einsum('qhd,khd->hqk', query_block, keys, precision=highest)
        scores = low_back(scores * scale)
        scores = jnp.where(mask_block[None], scores, -1000000000.0)
        probs = jax.nn.softmax(scores, axis=-1)
        context = jnp.einsum('hqk,khd->qhd', low(probs), values, precision=highest)
        return context.reshape(query_rows, D)
    starts = jnp.arange(seq_len // query_rows, dtype=jnp.int32) * query_rows
    attended = lax.map(jax.checkpoint(attend), starts).reshape(seq_len, D)
    attended = rounded(attended)
    branch = low_back(matmul(attended, out_weight) + proj_bias[2])
    normed = layer_norm(inputs + branch, norm_gain[0], norm_bias[0])
    upward = low_back(matmul(low(normed), up_weight) + up_bias)
    activated = low(jax.nn.gelu(upward, approximate=True))
    downward = low_back(matmul(activated, down_weight) + proj_bias[3])
    result = layer_norm(normed + downward, norm_gain[1], norm_bias[1])
    return result * valid[:, None]

def reference(tokens, lengths, random_blocks, qkv_weight, out_weight, up_weight, down_weight, proj_bias, up_bias, norm_gain, norm_bias, cotangent):
    params = tuple((matrix.astype(jnp.float32) for matrix in (qkv_weight, out_weight, up_weight, down_weight, proj_bias, up_bias, norm_gain, norm_bias)))
    inputs_all = tokens.astype(jnp.float32).reshape(SLOTS, TOK_DEV, D)
    cot_all = cotangent.astype(jnp.float32).reshape(SLOTS, TOK_DEV, D)

    def one_slot(totals, slot):
        inputs, cot_slot, length, chosen = slot
        mask = block_mask(length, chosen, TOK_DEV, BLK)
        valid = (jnp.arange(TOK_DEV, dtype=jnp.int32) < length).astype(jnp.float32)

        def forward(weights, layer_input):
            return slot_forward(weights, layer_input, mask, valid)
        result, pullback = jax.vjp(forward, params, inputs)
        grad_params, grad_inputs = pullback(cot_slot)
        totals = tuple((total + grad for total, grad in zip(totals, grad_params)))
        return (totals, (result.astype(jnp.bfloat16), grad_inputs))
    zeros = tuple((jnp.zeros(matrix.shape, jnp.float32) for matrix in params))
    totals, (outputs, grads) = lax.scan(one_slot, zeros, (inputs_all, cot_all, lengths, random_blocks))
    return (outputs.reshape(TOKENS, D), grads.reshape(TOKENS, D), totals[0], totals[1], totals[2], totals[3], totals[4], totals[5], totals[6], totals[7])
```

```python
import functools

import jax
import jax.numpy as jnp
from jax import lax
from jax.experimental import pallas as pl
from jax.experimental.pallas import tpu as pltpu
from jax.sharding import PartitionSpec as P

D = 768
HD = 64
BLK = 64
GROUPS = 3
EPS = 1e-06
BF = jnp.bfloat16
F32 = jnp.float32
ANY = pl.BlockSpec(memory_space=pl.ANY)
VM = pl.BlockSpec(memory_space=pltpu.VMEM)
SM = pl.BlockSpec(memory_space=pltpu.SMEM)


def dotf(a, b, ca, cb):
    return lax.dot_general(a, b, (((ca,), (cb,)), ((), ())), preferred_element_type=F32)


def lane_iota(shape):
    return lax.broadcasted_iota(jnp.int32, shape, 1)


def mult(v, m):
    return pl.multiple_of(v, m)


def piece_slot(me, cr, xr, yr, zr, rows, cols):
    z = lax.bitwise_xor(me[0], zr)
    y = lax.bitwise_xor(me[1], yr)
    x = lax.bitwise_xor(me[2], xr)
    c = lax.bitwise_xor(me[3], cr)
    r = mult(((z * 2 + y) * 2 + x) * rows, rows)
    return pl.ds(r, rows), pl.ds(mult(c * cols, cols), cols)


def load_pieces(me_ref, pieces, dst, sem):
    me = [me_ref[i] for i in range(4)]
    for k, ref in enumerate(pieces):
        cr, xr, yr = k // 4, (k // 2) % 2, k % 2
        for zr in range(4):
            rs, cs = piece_slot(me, cr, xr, yr, zr, ref.shape[1], ref.shape[2])
            pltpu.make_async_copy(ref.at[zr], dst.at[rs, cs], sem).start()


def store_pieces(me_ref, src, keep, send, sem):
    me = [me_ref[i] for i in range(4)]
    for cr, ref in ((1, send), (0, keep)):
        for xr in range(2):
            for yr in range(2):
                for zr in range(4):
                    rs, cs = piece_slot(me, cr, xr, yr, zr, ref.shape[3], ref.shape[4])
                    pltpu.make_async_copy(src.at[rs, cs], ref.at[xr, yr, zr], sem).start()


def wait_all(ref, sem):
    pltpu.make_async_copy(ref, ref, sem).wait()


def piece_shape(rows, cols):
    return jax.ShapeDtypeStruct((2, 2, 4, rows // 16, cols // 2), BF)


def attn_fwd_kernel(rt, me_ref, x_ref, bq_ref, bv_ref, qm_ref, km_ref, *refs):
    pieces, refs = refs[:8], refs[8:]
    q_ref, k_ref, v_ref, c_ref, lse_ref, wf_ref, w_ref, kx_ref, vx_ref, sem, sem2 = refs
    seq, gw = q_ref.shape
    load_pieces(me_ref, pieces, w_ref, sem)
    low = lane_iota((seq, 128)) < HD
    wait_all(w_ref, sem)
    out = pltpu.make_async_copy(w_ref, wf_ref, sem2)
    out.start()
    x = x_ref[...]
    q = dotf(x, w_ref[:, :gw], 1, 0) + bq_ref[...]
    q_ref[...] = (q * (HD**-0.5)).astype(BF)
    k_ref[...] = dotf(x, w_ref[:, gw : 2 * gw], 1, 0).astype(BF)
    v_ref[...] = (dotf(x, w_ref[:, 2 * gw :], 1, 0) + bv_ref[...]).astype(BF)

    def pair_body(pair, carry):
        sl = pl.ds(mult(pair * 128, 128), 128)
        kp = k_ref[:, sl]
        vp = v_ref[:, sl]
        for h in range(2):
            sel = low if h == 0 else jnp.logical_not(low)
            kx_ref[h, :, :128] = jnp.where(sel, kp, jnp.zeros_like(kp))
            kx_ref[h, :, 128:] = km_ref[...]
            vx_ref[h] = jnp.where(sel, vp, jnp.ones_like(vp))
        for i in range(seq // rt):
            rows = pl.ds(i * rt, rt)
            qx = jnp.concatenate([q_ref[rows, sl], qm_ref[rows, :]], axis=1)
            outs, lses = [], []
            for h in range(2):
                s = dotf(qx, kx_ref[h], 1, 1)
                m = jnp.max(s, axis=1, keepdims=True)
                p = jnp.exp(s - m).astype(BF)
                c = dotf(p, vx_ref[h], 1, 0)
                t = pltpu.roll(c, HD, 1)
                outs.append(c / t)
                lses.append(m + jnp.log(t))
            lo = lane_iota((rt, 128)) < HD
            c_ref[rows, sl] = jnp.where(lo, outs[0], outs[1]).astype(BF)
            lse_ref[rows, sl] = jnp.where(lo, lses[0], lses[1])
        return carry

    lax.fori_loop(0, gw // 128, pair_body, 0)
    out.wait()


def attn_fwd(me, x, bq, bv, qm, km, pieces):
    seq, d = x.shape
    gw = bq.shape[1]
    b = jax.ShapeDtypeStruct((seq, gw), BF)
    rt = min(1024, seq)
    return pl.pallas_call(
        functools.partial(attn_fwd_kernel, rt),
        in_specs=[SM] + [VM] * 5 + [ANY] * 8,
        out_specs=[VM] * 5 + [ANY],
        out_shape=[b, b, b, b, jax.ShapeDtypeStruct((seq, gw), F32), jax.ShapeDtypeStruct((d, 3 * gw), BF)],
        scratch_shapes=[
            pltpu.VMEM((d, 3 * gw), BF),
            pltpu.VMEM((2, seq, 256), BF),
            pltpu.VMEM((2, seq, 128), BF),
            pltpu.SemaphoreType.DMA,
            pltpu.SemaphoreType.DMA,
        ],
        compiler_params=pltpu.CompilerParams(vmem_limit_bytes=56 << 20),
        cost_estimate=pl.CostEstimate(flops=10_000_000_000, bytes_accessed=8 << 20, transcendentals=seq * seq * 4),
        name="attn_fwd",
    )(me, x, bq, bv, qm, km, *pieces)


def split3(t):
    hi = t.astype(BF).astype(F32)
    r = t - hi
    mid = r.astype(BF).astype(F32)
    return hi, mid, r - mid


def attn_bwd_kernel(me_ref, xt_ref, q_ref, k_ref, v_ref, c_ref, lse_ref, dc_ref, qm_ref, km_ref, *refs):
    dm_ref, keep_ref, send_ref, db_ref, kx, vx, qx, cx, pt, dst, dw, sem = refs
    seq, gw = q_ref.shape
    lane = lane_iota((seq, 128))
    low = lane < HD

    def pair_body(pair, carry):
        sl = pl.ds(mult(pair * 128, 128), 128)
        kp = k_ref[:, sl]
        vp = v_ref[:, sl]
        qp = q_ref[:, sl]
        dcp = dc_ref[:, sl]
        prod = dcp.astype(F32) * c_ref[:, sl].astype(F32)
        lsep = lse_ref[:, sl]
        zero = jnp.zeros_like(kp)
        one = jnp.ones_like(kp)
        qm = qm_ref[...].astype(F32)
        qx[:, :128] = qp
        cx[:, :128] = dcp
        for h in range(2):
            sel = low if h == 0 else jnp.logical_not(low)
            lse = jnp.max(jnp.where(sel, lsep, -3e38), axis=1, keepdims=True)
            delta = jnp.sum(jnp.where(sel, prod, 0.0), axis=1, keepdims=True)
            a, b, c = split3(-lse)
            qext = jnp.where(lane == 16, a, jnp.where(lane == 17, b, jnp.where(lane == 18, c, qm)))
            a, b, c = split3(-delta)
            cext = jnp.where(lane == 0, a, jnp.where(lane == 1, b, jnp.where(lane == 2, c, 0.0)))
            kx[h, :, :128] = jnp.where(sel, kp, zero)
            kx[h, :, 128:] = jnp.where((lane >= 16) & (lane < 19), one, km_ref[...])
            vx[h, :, :128] = jnp.where(sel, vp, zero)
            vx[h, :, 128:] = jnp.where(lane < 3, one, zero)
            qx[:, 128:] = qext.astype(BF)
            cx[:, 128:] = cext.astype(BF)
            p = jnp.exp(dotf(kx[h], qx[...], 1, 1))
            dp = dotf(vx[h], cx[...], 1, 1)
            pt[:, h * seq : (h + 1) * seq] = p.astype(BF)
            dst[:, h * seq : (h + 1) * seq] = (p * dp).astype(BF)
        qz = jnp.concatenate([jnp.where(low, qp, zero), jnp.where(low, zero, qp)], axis=0)
        cz = jnp.concatenate([jnp.where(low, dcp, zero), jnp.where(low, zero, dcp)], axis=0)
        dv = dotf(pt[...], cz, 1, 0)
        dk = dotf(dst[...], qz, 1, 0)
        dq = dotf(kx[0, :, :128], dst[:, :seq], 0, 0) + dotf(kx[1, :, :128], dst[:, seq:], 0, 0)
        dq = dq.T * (HD**-0.5)
        db_ref[0:1, sl] = jnp.sum(dq, axis=0, keepdims=True)
        db_ref[1:2, sl] = jnp.sum(dv, axis=0, keepdims=True)
        dm_ref[:, sl] = dq.astype(BF)
        dm_ref[:, pl.ds(mult(gw + pair * 128, 128), 128)] = dk.astype(BF)
        dm_ref[:, pl.ds(mult(2 * gw + pair * 128, 128), 128)] = dv.astype(BF)
        return carry

    lax.fori_loop(0, gw // 128, pair_body, 0)
    dw[...] = dotf(xt_ref[...], dm_ref[...], 1, 0).astype(BF)
    store_pieces(me_ref, dw, keep_ref, send_ref, sem)
    wait_all(dw, sem)


def attn_bwd(me, xt, q, k, v, c, lse, dc, qm, km):
    seq, gw = q.shape
    d = xt.shape[0]
    ps = piece_shape(d, 3 * gw)
    return pl.pallas_call(
        attn_bwd_kernel,
        in_specs=[SM] + [VM] * 9,
        out_specs=[VM, ANY, ANY, VM],
        out_shape=[jax.ShapeDtypeStruct((seq, 3 * gw), BF), ps, ps, jax.ShapeDtypeStruct((2, gw), F32)],
        scratch_shapes=[
            pltpu.VMEM((2, seq, 256), BF),
            pltpu.VMEM((2, seq, 256), BF),
            pltpu.VMEM((seq, 256), BF),
            pltpu.VMEM((seq, 256), BF),
            pltpu.VMEM((seq, 2 * seq), BF),
            pltpu.VMEM((seq, 2 * seq), BF),
            pltpu.VMEM((d, 3 * gw), BF),
            pltpu.SemaphoreType.DMA,
        ],
        compiler_params=pltpu.CompilerParams(vmem_limit_bytes=58 << 20),
        cost_estimate=pl.CostEstimate(flops=17_000_000_000, bytes_accessed=10 << 20, transcendentals=seq * seq * 4),
        name="attn_bwd",
    )(me, xt, q, k, v, c, lse, dc, qm, km)


def mid_a_kernel(rt, ft, me_ref, x_ref, c0_ref, c1_ref, c2_ref, bo_ref, g0_ref, b0_ref, ub_ref, *refs):
    wo_p, wu_p, refs = refs[:8], refs[8:16], refs[16:]
    g_ref, gp_ref, y_ref, yb_ref, n1_ref, r1_ref, wof_ref, wuf_ref, wo, wu, sem = refs
    load_pieces(me_ref, wo_p, wo, sem.at[0])
    load_pieces(me_ref, wu_p, wu, sem.at[1])
    seq, d = x_ref.shape
    gw = c0_ref.shape[1]
    wait_all(wo, sem.at[0])
    out_o = pltpu.make_async_copy(wo, wof_ref, sem.at[2])
    out_o.start()

    def rows_body(i, carry):
        rows = pl.ds(mult(i * rt, rt), rt)
        a = dotf(c0_ref[rows, :], wo[:gw], 1, 0)
        a += dotf(c1_ref[rows, :], wo[gw : 2 * gw], 1, 0)
        a += dotf(c2_ref[rows, :], wo[2 * gw :], 1, 0)
        h = x_ref[rows, :].astype(F32) + (a + bo_ref[...])
        cen = h - jnp.mean(h, axis=1, keepdims=True)
        r = lax.rsqrt(jnp.mean(cen * cen, axis=1, keepdims=True) + EPS)
        n = cen * r
        y = n * g0_ref[...] + b0_ref[...]
        n1_ref[rows, :] = n
        r1_ref[rows, :] = jnp.broadcast_to(r, (rt, 128))
        y_ref[rows, :] = y
        yb_ref[rows, :] = y.astype(BF)
        return carry

    lax.fori_loop(0, seq // rt, rows_body, 0)
    wait_all(wu, sem.at[1])
    out_u = pltpu.make_async_copy(wu, wuf_ref, sem.at[3])
    out_u.start()

    def cols_body(i, carry):
        cs = pl.ds(mult(i * ft, ft), ft)
        u = dotf(yb_ref[...], wu[:, cs], 1, 0) + ub_ref[:, cs]
        u2 = u * u
        k1 = 0.7978845608028654
        k2 = k1 * 0.044715
        h = 0.5 + 0.5 * jnp.tanh(u * (k1 + k2 * u2))
        g = u * h
        g_ref[:, cs] = g.astype(BF)
        gp_ref[:, cs] = (h + g * (1.0 - h) * (2 * k1 + (6 * k2) * u2)).astype(BF)
        return carry

    lax.fori_loop(0, wu.shape[1] // ft, cols_body, 0)
    out_o.wait()
    out_u.wait()


def mid_a(me, x, cs, bo, g0, b0, ub, wo_p, wu_p):
    seq, d = x.shape
    ff = ub.shape[1]
    S = jax.ShapeDtypeStruct
    return pl.pallas_call(
        functools.partial(mid_a_kernel, 256, 512),
        in_specs=[SM] + [VM] * 8 + [ANY] * 16,
        out_specs=[VM] * 6 + [ANY] * 2,
        out_shape=[
            S((seq, ff), BF),
            S((seq, ff), BF),
            S((seq, d), F32),
            S((seq, d), BF),
            S((seq, d), F32),
            S((seq, 128), F32),
            S((d, d), BF),
            S((d, ff), BF),
        ],
        scratch_shapes=[pltpu.VMEM((d, d), BF), pltpu.VMEM((d, ff), BF), pltpu.SemaphoreType.DMA((4,))],
        compiler_params=pltpu.CompilerParams(vmem_limit_bytes=58 << 20),
        cost_estimate=pl.CostEstimate(
            flops=2 * seq * d * (d + ff), bytes_accessed=20 << 20, transcendentals=seq * ff
        ),
        name="mid_a",
    )(me, x, *cs, bo, g0, b0, ub, *wo_p, *wu_p)


def mid_b_kernel(rt, ft, me_ref, len_ref, y_ref, cot_ref, bd_ref, g1_ref, b1_ref, g_hbm, gp_hbm, *refs):
    wd_p, refs = refs[:8], refs[8:]
    out_ref, dh2_ref, du_hbm, keep_ref, send_ref, sm_ref, ubg_ref, g, gp, wd, dz, dw, sem = refs
    load_pieces(me_ref, wd_p, wd, sem.at[0])
    cg = pltpu.make_async_copy(g_hbm, g, sem.at[1])
    cg.start()
    cgp = pltpu.make_async_copy(gp_hbm, gp, sem.at[2])
    cgp.start()
    seq, d = y_ref.shape
    ff = g.shape[1]
    length = len_ref[0]
    cg.wait()
    wait_all(wd, sem.at[0])
    sm_ref[...] = jnp.zeros_like(sm_ref)

    def rows_body(i, carry):
        rows = pl.ds(mult(i * rt, rt), rt)
        z = dotf(g[rows, :], wd[...], 1, 0) + bd_ref[...]
        h = y_ref[rows, :] + z
        cen = h - jnp.mean(h, axis=1, keepdims=True)
        r = lax.rsqrt(jnp.mean(cen * cen, axis=1, keepdims=True) + EPS)
        n = cen * r
        pos = lax.broadcasted_iota(jnp.int32, (rt, 1), 0) + i * rt
        valid = pos < length
        res = n * g1_ref[...] + b1_ref[...]
        out_ref[rows, :] = jnp.where(valid, res, 0.0).astype(BF)
        do = jnp.where(valid, cot_ref[rows, :].astype(F32), 0.0)
        e = do * g1_ref[...]
        me_ = jnp.mean(e, axis=1, keepdims=True)
        men = jnp.mean(e * n, axis=1, keepdims=True)
        dh = r * (e - me_ - n * men)
        dh2_ref[rows, :] = dh
        dzt = dh.astype(BF)
        dz[rows, :] = dzt
        sm_ref[0:1, :] += jnp.sum(do * n, axis=0, keepdims=True)
        sm_ref[1:2, :] += jnp.sum(do, axis=0, keepdims=True)
        sm_ref[2:3, :] += jnp.sum(dh, axis=0, keepdims=True)
        return carry

    lax.fori_loop(0, seq // rt, rows_body, 0)

    def dw_body(i, carry):
        cs = pl.ds(mult(i * ft, ft), ft)
        dw[cs, :] = dotf(g[:, cs], dz[...], 0, 0).astype(BF)
        return carry

    lax.fori_loop(0, ff // ft, dw_body, 0)
    store_pieces(me_ref, dw, keep_ref, send_ref, sem.at[3])
    cgp.wait()

    def du_body(i, carry):
        cs = pl.ds(mult(i * ft, ft), ft)
        dg = dotf(dz[...], wd[cs, :], 1, 1)
        du = dg * gp[:, cs].astype(F32)
        ubg_ref[:, cs] = jnp.sum(du, axis=0, keepdims=True)
        gp[:, cs] = du.astype(BF)
        return carry

    lax.fori_loop(0, ff // ft, du_body, 0)
    out = pltpu.make_async_copy(gp, du_hbm, sem.at[4])
    out.start()
    wait_all(dw, sem.at[3])
    out.wait()


def mid_b(me, length, y, cot, bd, g1, b1, g, gp, wd_p):
    seq, d = y.shape
    ff = g.shape[1]
    S = jax.ShapeDtypeStruct
    ps = piece_shape(ff, d)
    return pl.pallas_call(
        functools.partial(mid_b_kernel, 256, 512),
        in_specs=[SM] * 2 + [VM] * 5 + [ANY] * 10,
        out_specs=[VM, VM, ANY, ANY, ANY, VM, VM],
        out_shape=[
            S((seq, d), BF),
            S((seq, d), F32),
            S((seq, ff), BF),
            ps,
            ps,
            S((8, d), F32),
            S((1, ff), F32),
        ],
        scratch_shapes=[
            pltpu.VMEM((seq, ff), BF),
            pltpu.VMEM((seq, ff), BF),
            pltpu.VMEM((ff, d), BF),
            pltpu.VMEM((seq, d), BF),
            pltpu.VMEM((ff, d), BF),
            pltpu.SemaphoreType.DMA((5,)),
        ],
        compiler_params=pltpu.CompilerParams(vmem_limit_bytes=58 << 20),
        cost_estimate=pl.CostEstimate(flops=6 * seq * d * ff, bytes_accessed=20 << 20, transcendentals=seq),
        name="mid_b",
    )(me, length, y, cot, bd, g1, b1, g, gp, *wd_p)


def mid_c_kernel(rt, ft, me_ref, n1_ref, r1_ref, dh2_ref, yb_ref, c0_ref, c1_ref, c2_ref, g0_ref, wo_ref, *refs):
    du_hbm, wu_hbm, refs = refs[0], refs[1], refs[2:]
    dh1_ref, d0_ref, d1_ref, d2_ref, sm_ref = refs[:5]
    ukeep, usend, okeep, osend, du, wu, dwu, dwo, da, sem = refs[5:]
    cdu = pltpu.make_async_copy(du_hbm, du, sem.at[0])
    cdu.start()
    cwu = pltpu.make_async_copy(wu_hbm, wu, sem.at[1])
    cwu.start()
    seq, d = n1_ref.shape
    ff = du.shape[1]
    gw = c0_ref.shape[1]
    sm_ref[...] = jnp.zeros_like(sm_ref)
    cdu.wait()

    def dwu_body(i, carry):
        cs = pl.ds(mult(i * ft, ft), ft)
        dwu[:, cs] = dotf(yb_ref[...], du[:, cs], 0, 0).astype(BF)
        return carry

    lax.fori_loop(0, ff // ft, dwu_body, 0)
    store_pieces(me_ref, dwu, ukeep, usend, sem.at[2])
    cwu.wait()

    def rows_body(i, carry):
        rows = pl.ds(mult(i * rt, rt), rt)
        dy = dh2_ref[rows, :] + dotf(du[rows, :], wu[...], 1, 1)
        n = n1_ref[rows, :]
        e = dy * g0_ref[...]
        me_ = jnp.mean(e, axis=1, keepdims=True)
        men = jnp.mean(e * n, axis=1, keepdims=True)
        dh = r1_ref[rows, 0:1] * (e - me_ - n * men)
        dh1_ref[rows, :] = dh
        dat = dh.astype(BF)
        da[rows, :] = dat
        sm_ref[0:1, :] += jnp.sum(dy * n, axis=0, keepdims=True)
        sm_ref[1:2, :] += jnp.sum(dy, axis=0, keepdims=True)
        sm_ref[2:3, :] += jnp.sum(dh, axis=0, keepdims=True)
        dc = dotf(dat, wo_ref[...], 1, 1).astype(BF)
        d0_ref[rows, :] = dc[:, :gw]
        d1_ref[rows, :] = dc[:, gw : 2 * gw]
        d2_ref[rows, :] = dc[:, 2 * gw :]
        return carry

    lax.fori_loop(0, seq // rt, rows_body, 0)
    for i, c in enumerate((c0_ref, c1_ref, c2_ref)):
        dwo[i * gw : (i + 1) * gw, :] = dotf(c[...], da[...], 0, 0).astype(BF)
    store_pieces(me_ref, dwo, okeep, osend, sem.at[3])
    wait_all(dwu, sem.at[2])
    wait_all(dwo, sem.at[3])


def mid_c(me, n1, r1, dh2, yb, cs, g0, wo, du, wu):
    seq, d = n1.shape
    ff = du.shape[1]
    gw = cs[0].shape[1]
    S = jax.ShapeDtypeStruct
    pu, po = piece_shape(d, ff), piece_shape(d, d)
    dc = S((seq, gw), BF)
    return pl.pallas_call(
        functools.partial(mid_c_kernel, 256, 512),
        in_specs=[SM] + [VM] * 9 + [ANY] * 2,
        out_specs=[VM] * 5 + [ANY] * 4,
        out_shape=[S((seq, d), F32), dc, dc, dc, S((8, d), F32), pu, pu, po, po],
        scratch_shapes=[
            pltpu.VMEM((seq, ff), BF),
            pltpu.VMEM((d, ff), BF),
            pltpu.VMEM((d, ff), BF),
            pltpu.VMEM((d, d), BF),
            pltpu.VMEM((seq, d), BF),
            pltpu.SemaphoreType.DMA((4,)),
        ],
        compiler_params=pltpu.CompilerParams(vmem_limit_bytes=58 << 20),
        cost_estimate=pl.CostEstimate(flops=4 * seq * d * (ff + d), bytes_accessed=20 << 20, transcendentals=seq),
        name="mid_c",
    )(me, n1, r1, dh2, yb, *cs, g0, wo, du, wu)


def input_grad_kernel(dh1_ref, m0, m1, m2, w0, w1, w2, out_ref):
    acc = dh1_ref[...]
    for m, w in ((m0, w0), (m1, w1), (m2, w2)):
        acc += dotf(m[...], w[...], 1, 1)
    out_ref[...] = acc


def input_grad(dh1, dms, ws):
    seq, d = dh1.shape
    n = dms[0].shape[1]
    rt = 256
    row = lambda cols: pl.BlockSpec((rt, cols), lambda i: (i, 0))
    full = pl.BlockSpec((d, n), lambda i: (0, 0))
    return pl.pallas_call(
        input_grad_kernel,
        grid=(seq // rt,),
        in_specs=[row(d), row(n), row(n), row(n), full, full, full],
        out_specs=row(d),
        out_shape=jax.ShapeDtypeStruct((seq, d), F32),
        compiler_params=pltpu.CompilerParams(vmem_limit_bytes=40 << 20),
        cost_estimate=pl.CostEstimate(flops=6 * seq * d * n, bytes_accessed=15 << 20, transcendentals=0),
        name="input_grad",
    )(dh1, *dms, *ws)


class Links:
    def __init__(self, mesh):
        r, f = mesh.shape["replica"], mesh.shape["fsdp"]
        self.direct = (r, f) == (4, 8)
        if self.direct:
            fi, ri = lax.axis_index("fsdp"), lax.axis_index("replica")
            self.me = jnp.stack([fi // 2, fi % 2, ri // 2, ri % 2]).astype(jnp.int32)
        else:
            self.me = jnp.zeros((4,), jnp.int32)

    def core(self, a):
        return lax.ppermute(a, "replica", [(i, i ^ 1) for i in range(4)])

    def x(self, a):
        return lax.ppermute(a, "replica", [(i, i ^ 2) for i in range(4)])

    def y(self, a):
        return lax.ppermute(a, "fsdp", [(i, i ^ 1) for i in range(8)])

    def z(self, a, d):
        return lax.ppermute(a, "fsdp", [(i, i ^ (2 * d)) for i in range(8)])

    def gather(self, shard, x_last):
        if not self.direct:
            full = lax.all_gather(shard, "fsdp", axis=0, tiled=True)
            rows, cols = full.shape
            cut = full.reshape(4, 2, 2, rows // 16, 2, cols // 2)
            return [cut[:, y, x, :, c] for c in range(2) for x in range(2) for y in range(2)]
        rows, cols = shard.shape[0] // 2, shard.shape[1] // 2
        own = lax.dynamic_slice(shard, (self.me[2] * rows, self.me[3] * cols), (rows, cols))
        b = jnp.stack([own] + [self.z(own, d) for d in (1, 2, 3)])
        if x_last:
            by = self.y(b)
            bx, bxy = self.x(b), self.x(by)
        else:
            bx = self.x(b)
            by, bxy = self.y(b), self.y(bx)
        near = [b, by, bx, bxy]
        return near + [self.core(a) for a in near]

    def small_gather(self, rows):
        if not self.direct:
            every = lax.all_gather(rows, "fsdp", axis=0)
            return every
        b = jnp.stack([rows] + [self.z(rows, d) for d in (1, 2, 3)])
        both = jnp.stack([b, self.y(b)], axis=1).reshape((8,) + rows.shape)
        fi = lax.axis_index("fsdp")
        return jnp.stack([lax.dynamic_index_in_dim(both, fi ^ i, 0, keepdims=False) for i in range(8)])

    def reduce(self, keep, send, x_first):
        if not self.direct:
            both = jnp.stack([keep, send])
            c, x, y, z, r, n = both.shape
            full = both.transpose(3, 2, 1, 4, 0, 5).reshape(z * y * x * r, c * n)
            part = lax.psum_scatter(full.astype(F32), "fsdp", scatter_dimension=0, tiled=True)
            return lax.psum(part.astype(BF), "replica").astype(F32)
        r1 = self.core(send)
        up = lambda *parts: sum(p.astype(F32) for p in parts)
        if x_first:
            r2 = self.x(up(keep[1], r1[1]).astype(BF))
            r3 = self.y(up(keep[0, 1], r1[0, 1], r2[1]).astype(BF))
        else:
            r2 = self.y(up(keep[:, 1], r1[:, 1]).astype(BF))
            r3 = self.x(up(keep[1, 0], r1[1, 0], r2[1]).astype(BF))
        base = lambda d: up(keep[0, 0, d], r1[0, 0, d], r2[0, d], r3[d])
        r4 = [self.z(base(d).astype(BF), d) for d in (1, 2, 3)]
        fin = up(base(0), *r4).astype(BF)
        fx = self.x(fin)
        fc, fxc = self.core(fin), self.core(fx)
        c0, x0 = self.me[3] == 0, self.me[2] == 0
        wide = lambda a, b: jnp.concatenate([jnp.where(c0, a, b), jnp.where(c0, b, a)], axis=1)
        mine, theirs = wide(fin, fc), wide(fx, fxc)
        out = jnp.concatenate([jnp.where(x0, mine, theirs), jnp.where(x0, theirs, mine)], axis=0)
        return out.astype(F32)

    def small_reduce(self, rows):
        if not self.direct:
            return lax.psum(rows, ("replica", "fsdp"))
        s = rows + self.core(rows)
        s = s + self.x(s)
        s = s + self.y(s)
        s = s + self.z(s, 1)
        return s + self.z(s, 2)


def masks(length, chosen, seq):
    nb = chosen.shape[0]
    used = (length + BLK - 1) // BLK
    lane = jnp.arange(128, dtype=jnp.int32)[None, :]
    pos = jnp.arange(seq, dtype=jnp.int32)[:, None]
    kb = pos // BLK
    onehot = (kb == lane).astype(BF)
    picks = jnp.pad(chosen, ((0, 128 - nb), (0, 0)), constant_values=-1)
    allowed = (jnp.abs(lane - kb) <= 1) | (kb == 0) | (kb == used - 1) | (lane == 0) | (lane == used - 1)
    for i in range(chosen.shape[1]):
        allowed |= picks[:, i][None, :] == kb
    bias = jnp.where(allowed & (pos < length), 0.0, -1e9)
    return onehot, jnp.where(lane < nb, bias, 0.0).astype(BF)


def shards(mesh, tokens, lengths, random_blocks, qkv_weight, out_weight, up_weight, down_weight, proj_bias,
           up_bias, norm_gain, norm_bias, cotangent):
    links = Links(mesh)
    me = links.me
    seq, d = tokens.shape
    gw = d // GROUPS
    f_size = mesh.shape["fsdp"]
    dl = proj_bias.shape[1]
    ul = up_bias.shape[0]
    small = jnp.concatenate(
        [proj_bias, up_bias.reshape(ul // dl, dl), norm_gain, norm_bias], axis=0
    )
    small = links.small_gather(small)
    n_up = ul // dl
    ff = ul * f_size

    def row(i):
        return small[:, i].reshape(1, d).astype(F32)

    ub = small[:, 4 : 4 + n_up].reshape(1, ff).astype(F32)
    pb = [row(i) for i in range(4)]
    ng = [row(4 + n_up + i) for i in range(2)]
    nbias = [row(6 + n_up + i) for i in range(2)]
    onehot, bias = masks(lengths[0], random_blocks[0], seq)
    qkv_parts = []
    for g in range(GROUPS):
        cut = [qkv_weight[:, j * d + g * gw : j * d + (g + 1) * gw] for j in range(3)]
        qkv_parts.append(links.gather(jnp.concatenate(cut, axis=1), g % 2 == 0))
    wo_p = links.gather(out_weight, False)
    wu_p = links.gather(up_weight, True)
    wd_p = links.gather(down_weight, False)
    xt = tokens.T
    fwd = []
    for g in range(GROUPS):
        sl = slice(g * gw, (g + 1) * gw)
        fwd.append(attn_fwd(me, tokens, pb[0][:, sl], pb[1][:, sl], onehot, bias, qkv_parts[g]))
    cs = [o[3] for o in fwd]
    gact, gp, y, yb, n1, r1, wo, wu = mid_a(me, tokens, cs, pb[2], ng[0], nbias[0], ub, wo_p, wu_p)
    result, dh2, du, dkeep, dsend, sm2, ubg = mid_b(
        me, lengths, y, cotangent, pb[3], ng[1], nbias[1], gact, gp, wd_p
    )
    down_grad = links.reduce(dkeep, dsend, False)
    dh1, dc0, dc1, dc2, sm1, ukeep, usend, okeep, osend = mid_c(me, n1, r1, dh2, yb, cs, ng[0], wo, du, wu)
    up_grad = links.reduce(ukeep, usend, True)
    out_grad = links.reduce(okeep, osend, False)
    dms, dbs, qkv_cols = [], [], []
    for g, dc in enumerate((dc0, dc1, dc2)):
        q, k, v, c, lse, _ = fwd[g]
        dm, keep, send, db = attn_bwd(me, xt, q, k, v, c, lse, dc, onehot, bias)
        dms.append(dm)
        dbs.append(db)
        qkv_cols.append(links.reduce(keep, send, g % 2 == 0))
    grad_in = input_grad(dh1, dms, [o[5] for o in fwd])
    qkv_grad = jnp.concatenate(
        [qkv_cols[g][:, j * gw : (j + 1) * gw] for j in range(3) for g in range(GROUPS)], axis=1
    )
    db = jnp.concatenate(dbs, axis=1)
    rows = jnp.stack([db[0], db[1], sm1[2], sm2[2], sm1[0], sm2[0], sm1[1], sm2[1]])
    rows = rows.reshape(8, f_size, dl).transpose(1, 0, 2)
    every = jnp.concatenate([rows, ubg.reshape(f_size, n_up, dl)], axis=1)
    every = links.small_reduce(every)
    own = lax.dynamic_index_in_dim(every, lax.axis_index("fsdp"), 0, keepdims=False)
    return (
        result,
        grad_in,
        qkv_grad,
        out_grad,
        up_grad,
        down_grad,
        own[:4],
        own[8:].reshape(ul),
        own[4:6],
        own[6:8],
    )


def solution(mesh):
    both = ("replica", "fsdp")
    return jax.shard_map(
        functools.partial(shards, mesh),
        mesh=mesh,
        in_specs=(
            P(both, None),
            P(both),
            P(both, None, None),
            P("fsdp", None),
            P("fsdp", None),
            P("fsdp", None),
            P("fsdp", None),
            P(None, "fsdp"),
            P("fsdp"),
            P(None, "fsdp"),
            P(None, "fsdp"),
            P(both, None),
        ),
        out_specs=(
            P(both, None),
            P(both, None),
            P("fsdp", None),
            P("fsdp", None),
            P("fsdp", None),
            P("fsdp", None),
            P(None, "fsdp"),
            P("fsdp"),
            P(None, "fsdp"),
            P(None, "fsdp"),
        ),
        check_vma=False,
    )
```

```python
import functools

import jax
import jax.numpy as jnp
from jax import lax
from jax.experimental import pallas as pl
from jax.experimental.pallas import tpu as pltpu
from jax.sharding import PartitionSpec as P

D = 768
HD = 64
BLK = 64
GROUPS = 3
EPS = 1e-06
BF = jnp.bfloat16
F32 = jnp.float32
ANY = pl.BlockSpec(memory_space=pl.ANY)
VM = pl.BlockSpec(memory_space=pltpu.VMEM)
SM = pl.BlockSpec(memory_space=pltpu.SMEM)


def dotf(a, b, ca, cb):
    return lax.dot_general(a, b, (((ca,), (cb,)), ((), ())), preferred_element_type=F32)


def lane_iota(shape):
    return lax.broadcasted_iota(jnp.int32, shape, 1)


def mult(v, m):
    return pl.multiple_of(v, m)


def columns(me, cr, cols):
    return pl.ds(mult(lax.bitwise_xor(me[3], cr) * cols, cols), cols)


def load_rows(me, refs, dst, sem):
    for k, (ref, rows) in enumerate(refs):
        cols = ref.shape[-1]
        for zr in range(4):
            f = lax.bitwise_xor(me[0], zr) * 2 + lax.bitwise_xor(me[1], k % 2)
            at = dst.at[pl.ds(mult(f * rows, rows), rows), columns(me, k // 2, cols)]
            pltpu.make_async_copy(ref.at[zr, pl.ds(0, rows)], at, sem).start()


def piece_rows(me, xr, yr, zr, rows):
    z = lax.bitwise_xor(me[0], zr)
    y = lax.bitwise_xor(me[1], yr)
    x = lax.bitwise_xor(me[2], xr)
    return pl.ds(mult(((z * 2 + y) * 2 + x) * rows, rows), rows)


def load_pieces(me, refs, dst, sem):
    for k, ref in enumerate(refs):
        cr, xr, yr = k // 4, (k // 2) % 2, k % 2
        rows, cols = ref.shape[1:]
        for zr in range(4):
            at = dst.at[piece_rows(me, xr, yr, zr, rows), columns(me, cr, cols)]
            pltpu.make_async_copy(ref.at[zr], at, sem).start()


def store_pieces(me, src, keep, send, sem):
    for cr, ref in ((1, send), (0, keep)):
        rows, cols = ref.shape[3:]
        for xr in range(2):
            for yr in range(2):
                for zr in range(4):
                    at = src.at[piece_rows(me, xr, yr, zr, rows), columns(me, cr, cols)]
                    pltpu.make_async_copy(at, ref.at[xr, yr, zr], sem).start()


def wait_all(ref, sem):
    pltpu.make_async_copy(ref, ref, sem).wait()


def read_me(me_ref):
    return [me_ref[i] for i in range(4)]


def piece_shape(rows, cols):
    return jax.ShapeDtypeStruct((2, 2, 4, rows // 16, cols // 2), BF)


def attn_fwd_kernel(rt, g, group, me_ref, x_ref, par_ref, qm_ref, km_ref, *refs):
    pieces, refs = refs[:4], refs[4:]
    q_ref, k_ref, v_ref, c_ref, lse_ref, wf_ref, w_ref, kx_ref, vx_ref, sem, sem2 = refs
    seq, gw = q_ref.shape
    rows = w_ref.shape[0] // 8
    pieces = [ref if group is None else ref.at[:, group] for ref in pieces]
    load_rows(read_me(me_ref), [(ref, rows) for ref in pieces], w_ref, sem)
    low = lane_iota((seq, 128)) < HD
    wait_all(w_ref, sem)
    out = pltpu.make_async_copy(w_ref, wf_ref, sem2)
    out.start()
    x = x_ref[...]
    q = dotf(x, w_ref[:, :gw], 1, 0) + par_ref[0:1, g * gw : (g + 1) * gw]
    q_ref[...] = (q * (HD**-0.5)).astype(BF)
    k_ref[...] = dotf(x, w_ref[:, gw : 2 * gw], 1, 0).astype(BF)
    v_ref[...] = (dotf(x, w_ref[:, 2 * gw :], 1, 0) + par_ref[1:2, g * gw : (g + 1) * gw]).astype(BF)

    def pair_body(pair, carry):
        sl = pl.ds(mult(pair * 128, 128), 128)
        kp = k_ref[:, sl]
        vp = v_ref[:, sl]
        for h in range(2):
            sel = low if h == 0 else jnp.logical_not(low)
            kx_ref[h, :, :128] = jnp.where(sel, kp, jnp.zeros_like(kp))
            kx_ref[h, :, 128:] = km_ref[...]
            vx_ref[h] = jnp.where(sel, vp, jnp.ones_like(vp))
        for i in range(seq // rt):
            rows = pl.ds(i * rt, rt)
            qx = jnp.concatenate([q_ref[rows, sl], qm_ref[rows, :]], axis=1)
            outs, lses = [], []
            for h in range(2):
                s = dotf(qx, kx_ref[h], 1, 1)
                m = jnp.max(s, axis=1, keepdims=True)
                p = jnp.exp(s - m).astype(BF)
                c = dotf(p, vx_ref[h], 1, 0)
                t = pltpu.roll(c, HD, 1)
                outs.append(c / t)
                lses.append(m + jnp.log(t))
            lo = lane_iota((rt, 128)) < HD
            c_ref[rows, sl] = jnp.where(lo, outs[0], outs[1]).astype(BF)
            lse_ref[rows, sl] = jnp.where(lo, lses[0], lses[1])
        return carry

    lax.fori_loop(0, gw // 128, pair_body, 0)
    out.wait()


def attn_fwd(me, x, par, qm, km, pieces, g, group):
    seq, d = x.shape
    gw = d // GROUPS
    b = jax.ShapeDtypeStruct((seq, gw), BF)
    rt = min(1024, seq)
    return pl.pallas_call(
        functools.partial(attn_fwd_kernel, rt, g, group),
        in_specs=[SM] + [VM] * 4 + [ANY] * 4,
        out_specs=[VM] * 5 + [ANY],
        out_shape=[b, b, b, b, jax.ShapeDtypeStruct((seq, gw), F32), jax.ShapeDtypeStruct((d, 3 * gw), BF)],
        scratch_shapes=[
            pltpu.VMEM((d, 3 * gw), BF),
            pltpu.VMEM((2, seq, 256), BF),
            pltpu.VMEM((2, seq, 128), BF),
            pltpu.SemaphoreType.DMA,
            pltpu.SemaphoreType.DMA,
        ],
        compiler_params=pltpu.CompilerParams(vmem_limit_bytes=56 << 20),
        cost_estimate=pl.CostEstimate(flops=10_000_000_000, bytes_accessed=8 << 20, transcendentals=seq * seq * 4),
        name="attn_fwd",
    )(me, x, par, qm, km, *pieces)


def split3(t):
    hi = t.astype(BF).astype(F32)
    r = t - hi
    mid = r.astype(BF).astype(F32)
    return hi, mid, r - mid


def attn_bwd_kernel(me_ref, xt_ref, q_ref, k_ref, v_ref, c_ref, lse_ref, dc_ref, qm_ref, km_ref, *refs):
    dm_ref, keep_ref, send_ref, db_ref, kx, vx, qx, cx, pt, dst, dw, sem = refs
    seq, gw = q_ref.shape
    lane = lane_iota((seq, 128))
    low = lane < HD

    def pair_body(pair, carry):
        sl = pl.ds(mult(pair * 128, 128), 128)
        kp = k_ref[:, sl]
        vp = v_ref[:, sl]
        qp = q_ref[:, sl]
        dcp = dc_ref[:, sl]
        prod = dcp.astype(F32) * c_ref[:, sl].astype(F32)
        lsep = lse_ref[:, sl]
        zero = jnp.zeros_like(kp)
        one = jnp.ones_like(kp)
        qm = qm_ref[...].astype(F32)
        qx[:, :128] = qp
        cx[:, :128] = dcp
        for h in range(2):
            sel = low if h == 0 else jnp.logical_not(low)
            lse = jnp.max(jnp.where(sel, lsep, -3e38), axis=1, keepdims=True)
            delta = jnp.sum(jnp.where(sel, prod, 0.0), axis=1, keepdims=True)
            a, b, c = split3(-lse)
            qext = jnp.where(lane == 16, a, jnp.where(lane == 17, b, jnp.where(lane == 18, c, qm)))
            a, b, c = split3(-delta)
            cext = jnp.where(lane == 0, a, jnp.where(lane == 1, b, jnp.where(lane == 2, c, 0.0)))
            kx[h, :, :128] = jnp.where(sel, kp, zero)
            kx[h, :, 128:] = jnp.where((lane >= 16) & (lane < 19), one, km_ref[...])
            vx[h, :, :128] = jnp.where(sel, vp, zero)
            vx[h, :, 128:] = jnp.where(lane < 3, one, zero)
            qx[:, 128:] = qext.astype(BF)
            cx[:, 128:] = cext.astype(BF)
            p = jnp.exp(dotf(kx[h], qx[...], 1, 1))
            dp = dotf(vx[h], cx[...], 1, 1)
            pt[:, h * seq : (h + 1) * seq] = p.astype(BF)
            dst[:, h * seq : (h + 1) * seq] = (p * dp).astype(BF)
        qz = jnp.concatenate([jnp.where(low, qp, zero), jnp.where(low, zero, qp)], axis=0)
        cz = jnp.concatenate([jnp.where(low, dcp, zero), jnp.where(low, zero, dcp)], axis=0)
        dv = dotf(pt[...], cz, 1, 0)
        dk = dotf(dst[...], qz, 1, 0)
        dq = dotf(kx[0, :, :128], dst[:, :seq], 0, 0) + dotf(kx[1, :, :128], dst[:, seq:], 0, 0)
        dq = dq.T * (HD**-0.5)
        db_ref[0:1, sl] = jnp.sum(dq, axis=0, keepdims=True)
        db_ref[1:2, sl] = jnp.sum(dv, axis=0, keepdims=True)
        dm_ref[:, sl] = dq.astype(BF)
        dm_ref[:, pl.ds(mult(gw + pair * 128, 128), 128)] = dk.astype(BF)
        dm_ref[:, pl.ds(mult(2 * gw + pair * 128, 128), 128)] = dv.astype(BF)
        return carry

    lax.fori_loop(0, gw // 128, pair_body, 0)
    dw[...] = dotf(xt_ref[...], dm_ref[...], 1, 0).astype(BF)
    store_pieces(read_me(me_ref), dw, keep_ref, send_ref, sem)
    wait_all(dw, sem)


def attn_bwd(me, xt, q, k, v, c, lse, dc, qm, km):
    seq, gw = q.shape
    d = xt.shape[0]
    ps = piece_shape(d, 3 * gw)
    return pl.pallas_call(
        attn_bwd_kernel,
        in_specs=[SM] + [VM] * 9,
        out_specs=[VM, ANY, ANY, VM],
        out_shape=[jax.ShapeDtypeStruct((seq, 3 * gw), BF), ps, ps, jax.ShapeDtypeStruct((2, gw), F32)],
        scratch_shapes=[
            pltpu.VMEM((2, seq, 256), BF),
            pltpu.VMEM((2, seq, 256), BF),
            pltpu.VMEM((seq, 256), BF),
            pltpu.VMEM((seq, 256), BF),
            pltpu.VMEM((seq, 2 * seq), BF),
            pltpu.VMEM((seq, 2 * seq), BF),
            pltpu.VMEM((d, 3 * gw), BF),
            pltpu.SemaphoreType.DMA,
        ],
        compiler_params=pltpu.CompilerParams(vmem_limit_bytes=58 << 20),
        cost_estimate=pl.CostEstimate(flops=17_000_000_000, bytes_accessed=10 << 20, transcendentals=seq * seq * 4),
        name="attn_bwd",
    )(me, xt, q, k, v, c, lse, dc, qm, km)


def copies(pairs, sem):
    for src, dst in pairs:
        pltpu.make_async_copy(src, dst, sem).start()


def gelu_parts(u):
    u2 = u * u
    k1 = 0.7978845608028654
    k2 = k1 * 0.044715
    h = 0.5 + 0.5 * jnp.tanh(u * (k1 + k2 * u2))
    g = u * h
    return g, h + g * (1.0 - h) * (2 * k1 + (6 * k2) * u2)


def mid_a_kernel(rt, ft, me_ref, par_ref, ub_ref, x_hbm, c0_hbm, c1_hbm, c2_hbm, *refs):
    pieces, refs = refs[:2], refs[2:]
    g, gp, y, yb, n1, r1, wo, wu, us, x_ref, c0_ref, c1_ref, c2_ref, sem = refs
    me = read_me(me_ref)
    loads = ((c0_hbm, c0_ref, 2), (c1_hbm, c1_ref, 3), (c2_hbm, c2_ref, 4), (x_hbm, x_ref, 5))
    for src, dst, k in loads:
        pltpu.make_async_copy(src, dst, sem.at[k]).start()
    nu, no = wu.shape[1] // 2, wo.shape[1] // 2
    for cr, ref in enumerate(pieces):
        pltpu.make_async_copy(ref.at[:, pl.ds(nu, no)], wo.at[:, columns(me, cr, no)], sem.at[0]).start()
    for cr, ref in enumerate(pieces):
        pltpu.make_async_copy(ref.at[:, pl.ds(0, nu)], wu.at[:, columns(me, cr, nu)], sem.at[1]).start()
    seq, d = x_ref.shape
    ff = wu.shape[1]
    gw = c0_ref.shape[1]
    for src, dst, k in loads:
        pltpu.make_async_copy(src, dst, sem.at[k]).wait()
    wait_all(wo, sem.at[0])

    def rows_body(i, carry):
        rows = pl.ds(mult(i * rt, rt), rt)
        a = dotf(c0_ref[rows, :], wo[:gw], 1, 0)
        a += dotf(c1_ref[rows, :], wo[gw : 2 * gw], 1, 0)
        a += dotf(c2_ref[rows, :], wo[2 * gw :], 1, 0)
        h = x_ref[rows, :].astype(F32) + (a + par_ref[2:3, :])
        cen = h - jnp.mean(h, axis=1, keepdims=True)
        r = lax.rsqrt(jnp.mean(cen * cen, axis=1, keepdims=True) + EPS)
        n = cen * r
        yt = n * par_ref[4:5, :] + par_ref[6:7, :]
        n1[rows, :] = n
        r1[rows, :] = jnp.broadcast_to(r, (rt, 128))
        y[rows, :] = yt
        yb[rows, :] = yt.astype(BF)
        return carry

    lax.fori_loop(0, seq // rt, rows_body, 0)
    wait_all(wu, sem.at[1])

    def product(i, slot):
        cs = pl.ds(mult(i * ft, ft), ft)
        us[slot] = dotf(yb[...], wu[:, cs], 1, 0)

    def finish(i, slot):
        cs = pl.ds(mult(i * ft, ft), ft)
        gt, gpt = gelu_parts(us[slot] + ub_ref[:, cs])
        g[:, cs] = gt.astype(BF)
        gp[:, cs] = gpt.astype(BF)

    last = ff // ft - 1
    product(0, 0)

    def cols_body(i, carry):
        product(2 * i + 1, 1)
        finish(2 * i, 0)
        product(lax.min(2 * i + 2, last), 0)
        finish(2 * i + 1, 1)
        return carry

    lax.fori_loop(0, ff // ft // 2, cols_body, 0)


def in_vmem(*arrays):
    return [pltpu.with_memory_space_constraint(a, pltpu.VMEM) for a in arrays]


def in_hbm(*arrays):
    return [pltpu.with_memory_space_constraint(a, pltpu.HBM) for a in arrays]


def mid_a(me, x, cs, par, ub, pieces):
    seq, d = x.shape
    ff = ub.shape[1]
    ft = 512
    shapes = [((seq, ff), BF), ((seq, ff), BF), ((seq, d), F32), ((seq, d), BF), ((seq, d), F32), ((seq, 128), F32)]
    shapes += [((d, d), BF), ((d, ff), BF)]
    return pl.pallas_call(
        functools.partial(mid_a_kernel, 256, ft),
        in_specs=[SM] + [VM] * 2 + [ANY] * 6,
        out_specs=[VM] * 8,
        out_shape=[pltpu.VMEM(*sh) for sh in shapes],
        scratch_shapes=[pltpu.VMEM((2, seq, ft), F32), pltpu.VMEM((seq, d), BF)]
        + [pltpu.VMEM((seq, d // GROUPS), BF)] * GROUPS
        + [pltpu.SemaphoreType.DMA((6,))],
        compiler_params=pltpu.CompilerParams(vmem_limit_bytes=15 << 20),
        cost_estimate=pl.CostEstimate(
            flops=2 * seq * d * (d + ff), bytes_accessed=20 << 20, transcendentals=seq * ff
        ),
        name="mid_a",
    )(me, par, ub, *in_hbm(x, *cs, *pieces))


def mid_b_kernel(rt, ft, me_ref, len_ref, par_ref, y, g, gp, cot_hbm, *refs):
    wd_p, refs = refs[:8], refs[8:]
    out_hbm, dh2, du, keep_ref, send_ref, sm_ref, ubg_ref, cot, wd, dz, dw, sem, tsem = refs
    me = read_me(me_ref)
    load_pieces(me, wd_p, wd, sem.at[0])
    pltpu.make_async_copy(cot_hbm, cot, sem.at[1]).start()
    seq, d = y.shape
    ff = g.shape[1]
    tiles = seq // rt
    length = len_ref[0]
    sm_ref[...] = jnp.zeros_like(sm_ref)
    wait_all(wd, sem.at[0])
    pltpu.make_async_copy(cot_hbm, cot, sem.at[1]).wait()

    def rows_body(i, carry):
        rows = pl.ds(mult(i * rt, rt), rt)
        z = dotf(g[rows, :], wd[...], 1, 0) + par_ref[3:4, :]
        h = y[rows, :] + z
        cen = h - jnp.mean(h, axis=1, keepdims=True)
        r = lax.rsqrt(jnp.mean(cen * cen, axis=1, keepdims=True) + EPS)
        n = cen * r
        pos = lax.broadcasted_iota(jnp.int32, (rt, 1), 0) + i * rt
        valid = pos < length
        do = jnp.where(valid, cot[rows, :].astype(F32), 0.0)
        res = n * par_ref[5:6, :] + par_ref[7:8, :]
        cot[rows, :] = jnp.where(valid, res, 0.0).astype(BF)
        e = do * par_ref[5:6, :]
        me_ = jnp.mean(e, axis=1, keepdims=True)
        men = jnp.mean(e * n, axis=1, keepdims=True)
        dh = r * (e - me_ - n * men)
        dh2[rows, :] = dh
        dz[rows, :] = dh.astype(BF)
        sm_ref[0:1, :] += jnp.sum(do * n, axis=0, keepdims=True)
        sm_ref[1:2, :] += jnp.sum(do, axis=0, keepdims=True)
        sm_ref[2:3, :] += jnp.sum(dh, axis=0, keepdims=True)
        return carry

    lax.fori_loop(0, tiles, rows_body, 0)
    pltpu.make_async_copy(cot, out_hbm, sem.at[2]).start()
    n = d // 2
    part = ff // 32

    def dw_body(f, carry):
        rows = pl.ds(mult(f * 4 * part, part), 4 * part)
        dw[rows, :] = dotf(g[:, rows], dz[...], 0, 0).astype(BF)
        for cr, ref in ((1, send_ref), (0, keep_ref)):
            for j in range(4):
                at = dw.at[pl.ds(mult((f * 4 + j) * part, part), part), columns(me, cr, n)]
                to = ref.at[pl.ds(mult(f * part, part), part), pl.ds(j * n, n)]
                pltpu.make_async_copy(at, to, sem.at[3]).start()
        return carry

    lax.fori_loop(0, 8, dw_body, 0)

    def du_body(i, carry):
        cs = pl.ds(mult(i * ft, ft), ft)
        dg = dotf(dz[...], wd[cs, :], 1, 1)
        dut = dg * gp[:, cs].astype(F32)
        ubg_ref[:, cs] = jnp.sum(dut, axis=0, keepdims=True)
        du[:, cs] = dut.astype(BF)
        return carry

    lax.fori_loop(0, ff // ft, du_body, 0)
    pltpu.make_async_copy(cot, out_hbm, sem.at[2]).wait()
    wait_all(dw, sem.at[3])


def mid_b(me, length, y, cot, par, g, gp, wd_p):
    seq, d = y.shape
    ff = g.shape[1]
    rt = 256
    S = jax.ShapeDtypeStruct
    ps = pltpu.HBM((ff // 4, 2 * d), BF)
    return pl.pallas_call(
        functools.partial(mid_b_kernel, rt, 512),
        in_specs=[SM] * 2 + [VM] * 4 + [ANY] * 9,
        out_specs=[ANY] + [VM] * 2 + [ANY] * 2 + [VM] * 2,
        out_shape=[
            pltpu.HBM((seq, d), BF),
            pltpu.VMEM((seq, d), F32),
            pltpu.VMEM((seq, ff), BF),
            ps,
            ps,
            S((8, d), F32),
            S((1, ff), F32),
        ],
        input_output_aliases={3: 1, 5: 2},
        scratch_shapes=[
            pltpu.VMEM((seq, d), BF),
            pltpu.VMEM((ff, d), BF),
            pltpu.VMEM((seq, d), BF),
            pltpu.VMEM((ff, d), BF),
            pltpu.SemaphoreType.DMA((4,)),
            pltpu.SemaphoreType.DMA((3, seq // rt)),
        ],
        compiler_params=pltpu.CompilerParams(vmem_limit_bytes=17 << 20),
        cost_estimate=pl.CostEstimate(flops=6 * seq * d * ff, bytes_accessed=20 << 20, transcendentals=seq),
        name="mid_b",
    )(me, length, par, *in_vmem(y, g, gp), *in_hbm(cot, *wd_p))


def mid_c_kernel(rt, ft, me_ref, par_ref, n1, r1, dh2, yb, wo, du, wu, *refs):
    c0_h, c1_h, c2_h = refs[:3]
    dh1_h, d0_h, d1_h, d2_h, keep, send, sm_ref = refs[3:10]
    cs_, dwu, dwo, da, dc, dh1, sem = refs[10:]
    me = read_me(me_ref)
    seq, d = n1.shape
    ff = du.shape[1]
    gw = d // 3
    nu, no = ff // 2, d // 2
    steps = nu // ft
    for i, ref in enumerate((c0_h, c1_h, c2_h)):
        pltpu.make_async_copy(ref, cs_.at[:, i * gw : (i + 1) * gw], sem.at[0]).start()
    sm_ref[...] = jnp.zeros_like(sm_ref)
    for cr, ref in ((1, send), (0, keep)):

        def dwu_body(j, carry):
            at = pl.ds(mult(lax.bitwise_xor(me[3], cr) * nu + j * ft, ft), ft)
            dwu[:, at] = dotf(yb[...], du[:, at], 0, 0).astype(BF)
            pltpu.make_async_copy(dwu.at[:, at], ref.at[:, pl.ds(mult(j * ft, ft), ft)], sem.at[1]).start()
            return carry

        lax.fori_loop(0, steps, dwu_body, 0)

    def rows_body(i, carry):
        rows = pl.ds(mult(i * rt, rt), rt)
        dy = dh2[rows, :] + dotf(du[rows, :], wu[...], 1, 1)
        n = n1[rows, :]
        e = dy * par_ref[4:5, :]
        me_ = jnp.mean(e, axis=1, keepdims=True)
        men = jnp.mean(e * n, axis=1, keepdims=True)
        dh = r1[rows, 0:1] * (e - me_ - n * men)
        dh1[rows, :] = dh
        dat = dh.astype(BF)
        da[rows, :] = dat
        sm_ref[0:1, :] += jnp.sum(dy * n, axis=0, keepdims=True)
        sm_ref[1:2, :] += jnp.sum(dy, axis=0, keepdims=True)
        sm_ref[2:3, :] += jnp.sum(dh, axis=0, keepdims=True)
        dc[rows, :] = dotf(dat, wo[...], 1, 1).astype(BF)
        return carry

    lax.fori_loop(0, seq // rt, rows_body, 0)
    pltpu.make_async_copy(dh1, dh1_h, sem.at[2]).start()
    for i, ref in enumerate((d0_h, d1_h, d2_h)):
        pltpu.make_async_copy(dc.at[:, i * gw : (i + 1) * gw], ref, sem.at[3]).start()
    wait_all(cs_, sem.at[0])
    for cr, ref in ((1, send), (0, keep)):
        at = columns(me, cr, no)
        dwo[:, at] = dotf(cs_[...], da[:, at], 0, 0).astype(BF)
        pltpu.make_async_copy(dwo.at[:, at], ref.at[:, pl.ds(nu, no)], sem.at[4]).start()
    pltpu.make_async_copy(dh1, dh1_h, sem.at[2]).wait()
    wait_all(dc, sem.at[3])
    wait_all(dwu, sem.at[1])
    wait_all(dwo, sem.at[4])


def mid_c(me, n1, r1, dh2, yb, cs, par, wo, du, wu):
    seq, d = n1.shape
    ff = du.shape[1]
    gw = cs[0].shape[1]
    S = jax.ShapeDtypeStruct
    ps = pltpu.HBM((d, (ff + d) // 2), BF)
    dc = pltpu.HBM((seq, gw), BF)
    ft = 512
    return pl.pallas_call(
        functools.partial(mid_c_kernel, 256, ft),
        in_specs=[SM] + [VM] * 8 + [ANY] * 3,
        out_specs=[ANY] * 6 + [VM],
        out_shape=[pltpu.HBM((seq, d), F32), dc, dc, dc, ps, ps, S((8, d), F32)],
        scratch_shapes=[
            pltpu.VMEM((seq, d), BF),
            pltpu.VMEM((d, ff), BF),
            pltpu.VMEM((d, d), BF),
            pltpu.VMEM((seq, d), BF),
            pltpu.VMEM((seq, d), BF),
            pltpu.VMEM((seq, d), F32),
            pltpu.SemaphoreType.DMA((5,)),
        ],
        compiler_params=pltpu.CompilerParams(vmem_limit_bytes=18 << 20),
        cost_estimate=pl.CostEstimate(flops=4 * seq * d * (ff + d), bytes_accessed=20 << 20, transcendentals=seq),
        name="mid_c",
    )(me, par, *in_vmem(n1, r1, dh2, yb, wo, du, wu), *in_hbm(*cs))


def input_grad_kernel(dh1_ref, m0, m1, m2, w0, w1, w2, out_ref):
    acc = dh1_ref[...]
    for m, w in ((m0, w0), (m1, w1), (m2, w2)):
        acc += dotf(m[...], w[...], 1, 1)
    out_ref[...] = acc


def input_grad(dh1, dms, ws):
    seq, d = dh1.shape
    n = dms[0].shape[1]
    rt = 256
    row = lambda cols: pl.BlockSpec((rt, cols), lambda i: (i, 0))
    full = pl.BlockSpec((d, n), lambda i: (0, 0))
    return pl.pallas_call(
        input_grad_kernel,
        grid=(seq // rt,),
        in_specs=[row(d), row(n), row(n), row(n), full, full, full],
        out_specs=row(d),
        out_shape=jax.ShapeDtypeStruct((seq, d), F32),
        compiler_params=pltpu.CompilerParams(vmem_limit_bytes=60 << 20),
        cost_estimate=pl.CostEstimate(flops=6 * seq * d * n, bytes_accessed=15 << 20, transcendentals=0),
        name="input_grad",
    )(dh1, *dms, *ws)


def sum_kernel(*refs):
    out = refs[-1]
    first = 0
    for a, b in zip(refs[0:-1:2], refs[1:-1:2]):
        w = a.shape[1]
        out[:, first : first + w] = (a[...].astype(F32) + b[...].astype(F32)).astype(BF)
        first += w


def summed(*pairs):
    rows = pairs[0][0].shape[0]
    rt = rows // 8
    width = sum(a.shape[1] for a, _ in pairs)
    one = lambda w: pl.BlockSpec((rt, w), lambda i: (i, 0))
    arrays = [a for pair in pairs for a in pair]
    return pl.pallas_call(
        sum_kernel,
        grid=(8,),
        in_specs=[one(a.shape[1]) for a in arrays],
        out_specs=one(width),
        out_shape=jax.ShapeDtypeStruct((rows, width), BF),
        compiler_params=pltpu.CompilerParams(vmem_limit_bytes=60 << 20),
        cost_estimate=pl.CostEstimate(flops=rows * width, bytes_accessed=6 * rows * width, transcendentals=0),
        name="summed",
    )(*arrays)


def small_kernel(d0_ref, d1_ref, d2_ref, s1_ref, s2_ref, ub_ref, me_ref, out_ref):
    gw = d0_ref.shape[1]
    d = s1_ref.shape[1]
    dl = d // 8
    rows = [jnp.concatenate([r[i : i + 1, :] for r in (d0_ref, d1_ref, d2_ref)], axis=1) for i in range(2)]
    rows += [s1_ref[2:3, :], s2_ref[2:3, :], s1_ref[0:1, :], s2_ref[0:1, :], s1_ref[1:2, :], s2_ref[1:2, :]]
    table = jnp.concatenate(rows, axis=0).astype(BF)
    ub = ub_ref[...].astype(BF)
    me = read_me(me_ref)
    out_ref[...] = jnp.zeros_like(out_ref)

    def pick(n, first):
        j = lax.broadcasted_iota(jnp.int32, (n, 128), 0)
        lane = lane_iota((n, 128))
        return ((j == lane + first) & (lane < dl)).astype(BF)

    ups = [dotf(ub, pick(ub.shape[1], k * dl), 1, 0) for k in range(4)]
    for f in range(8):
        top = dotf(table, pick(d, f * dl), 1, 0)
        both = jnp.concatenate([top] + [u[f : f + 1] for u in ups] + [jnp.zeros((4, 128), F32)], axis=0).astype(BF)
        for xr in range(2):
            out_ref[xr, lax.bitwise_xor(me[1], f % 2), lax.bitwise_xor(me[0], f // 2), 0:16, :] = both


def small_pieces(dbs, s1, s2, ub, me, rows):
    return pl.pallas_call(
        small_kernel,
        in_specs=[VM] * 6 + [SM],
        out_specs=VM,
        out_shape=jax.ShapeDtypeStruct((2, 2, 4, rows, 128), BF),
        compiler_params=pltpu.CompilerParams(vmem_limit_bytes=60 << 20),
        cost_estimate=pl.CostEstimate(flops=1 << 20, bytes_accessed=1 << 20, transcendentals=0),
        name="small_pieces",
    )(*dbs, s1, s2, ub, me)


def parts_of(arrays, lower):
    k0, k1, k2, e = arrays
    n = k1.shape[-1] // 3
    if lower:
        return [(k1, 2 * n, n), (k2, 0, 3 * n), (e, 0, 128)]
    return [(k0, 0, 3 * n), (k1, 0, 2 * n)]


def fill(out, index, keeps, recvs, lower, at, more=()):
    first = 0
    for (k, c, w), (r, _, _) in zip(parts_of(keeps, lower), parts_of(recvs, lower)):
        total = k[at + (slice(c, c + w),)].astype(F32) + r[at + (slice(c, c + w),)].astype(F32)
        for m, m_at in more:
            total += m[m_at + (slice(first, first + w),)].astype(F32)
        out[index + (slice(first, first + w),)] = total.astype(out.dtype)
        first += w


ALL3 = (slice(None),) * 3


def stage1_kernel(*refs):
    keeps, recvs, (ta, tb) = refs[:4], refs[4:8], refs[8:]
    for i in range(2):
        fill(ta, (i, slice(None), slice(None)), keeps, recvs, False, (1, i, slice(None), slice(None)))
        fill(tb, (i, slice(None), slice(None)), keeps, recvs, True, (i, 1, slice(None), slice(None)))


def stage2_kernel(*refs):
    keeps, recvs, (ra, rb), (ta, tb) = refs[:4], refs[4:8], refs[8:10], refs[10:]
    every = (slice(None), slice(None))
    fill(ta, every, keeps, recvs, False, (0, 1) + every, [(ra, (1,) + every)])
    fill(tb, every, keeps, recvs, True, (1, 0) + every, [(rb, (1,) + every)])


def stage3_kernel(*refs):
    keeps, recvs, (ra, rb, sa, sb), outs = refs[:4], refs[4:8], refs[8:12], refs[12:]
    half = sa.shape[-1]
    for zr, out in enumerate(outs):
        at = (0, 0, zr, slice(None))
        for lower, r, t in ((False, ra, sa), (True, rb, sb)):
            view = out.at[:, pl.ds(half * lower, half)]
            fill(view, (slice(None),), keeps, recvs, lower, at, [(r, (0, zr, slice(None))), (t, (zr, slice(None)))])


def stage(kernel, arrays, shapes):
    nbytes = sum(a.size * 2 for a in arrays)
    return pl.pallas_call(
        kernel,
        in_specs=[VM] * len(arrays),
        out_specs=[VM] * len(shapes),
        out_shape=[jax.ShapeDtypeStruct(sh, dt) for sh, dt in shapes],
        compiler_params=pltpu.CompilerParams(vmem_limit_bytes=60 << 20),
        cost_estimate=pl.CostEstimate(flops=nbytes, bytes_accessed=nbytes, transcendentals=0),
        name=kernel.__name__[:6],
    )(*arrays)


def after(value, *others):
    return lax.optimization_barrier((value, *others))[0]


def added(*parts):
    return sum(p.astype(F32) for p in parts)


def flipped(array, bits, axes):
    for bit, axis in zip(bits, axes):
        array = jnp.where(bit == 1, jnp.flip(array, axis), array)
    return array


class Links:
    def __init__(self, mesh):
        r, f = mesh.shape["replica"], mesh.shape["fsdp"]
        self.direct = (r, f) == (4, 8)
        if self.direct:
            fi, ri = lax.axis_index("fsdp"), lax.axis_index("replica")
            self.me = jnp.stack([fi // 2, fi % 2, ri // 2, ri % 2]).astype(jnp.int32)
        else:
            self.me = jnp.zeros((4,), jnp.int32)

    def core(self, a):
        return lax.ppermute(a, "replica", [(i, i ^ 1) for i in range(4)])

    def x(self, a):
        return lax.ppermute(a, "replica", [(i, i ^ 2) for i in range(4)])

    def y(self, a):
        return lax.ppermute(a, "fsdp", [(i, i ^ 1) for i in range(8)])

    def z(self, a, d):
        return lax.ppermute(a, "fsdp", [(i, i ^ (2 * d)) for i in range(8)])

    def to_z(self, own):
        return [self.z(own, d) for d in (1, 2, 3)]

    def half(self, shard):
        n = shard.shape[-1] // 2
        return lax.dynamic_slice_in_dim(shard, self.me[3] * n, n, shard.ndim - 1)

    def quarter(self, shard):
        r = shard.shape[0] // 2
        return lax.dynamic_slice_in_dim(self.half(shard), self.me[2] * r, r, 0)

    def bits(self):
        z, y, x, c = (self.me[i] for i in range(4))
        return z // 2, z % 2, y, x, c

    def wide(self, own, other):
        c0 = self.me[3] == 0
        return jnp.concatenate([jnp.where(c0, own, other), jnp.where(c0, other, own)], axis=1)


def masks(length, chosen, seq):
    nb = chosen.shape[0]
    used = (length + BLK - 1) // BLK
    lane = jnp.arange(128, dtype=jnp.int32)[None, :]
    pos = jnp.arange(seq, dtype=jnp.int32)[:, None]
    kb = pos // BLK
    onehot = (kb == lane).astype(BF)
    picks = jnp.pad(chosen, ((0, 128 - nb), (0, 0)), constant_values=-1)
    allowed = (jnp.abs(lane - kb) <= 1) | (kb == 0) | (kb == used - 1) | (lane == 0) | (lane == used - 1)
    for i in range(chosen.shape[1]):
        allowed |= picks[:, i][None, :] == kb
    bias = jnp.where(allowed & (pos < length), 0.0, -1e9)
    return onehot, jnp.where(lane < nb, bias, 0.0).astype(BF)


def shards(mesh, tokens, lengths, random_blocks, qkv_weight, out_weight, up_weight, down_weight, proj_bias,
           up_bias, norm_gain, norm_bias, cotangent):
    links = Links(mesh)
    me = links.me
    direct = links.direct
    seq, d = tokens.shape
    gw = d // GROUPS
    hw = 3 * gw // 2
    f_size = mesh.shape["fsdp"]
    dl = proj_bias.shape[1]
    ul = up_bias.shape[0]
    n_up = ul // dl
    ff = ul * f_size
    nu, no = ff // 2, d // 2
    small = jnp.concatenate([proj_bias, norm_gain, norm_bias, up_bias.reshape(n_up, dl)], axis=0)

    groups = []
    for g in range(GROUPS):
        cut = [qkv_weight[:, j * d + g * gw : j * d + (g + 1) * gw] for j in range(3)]
        groups.append(jnp.concatenate(cut, axis=1))
    if direct:
        own0 = jnp.concatenate([links.half(groups[0]), jnp.pad(small.reshape(-1, hw), ((0, 8 - small.size // hw), (0, 0)))])
        own12 = after(links.half(jnp.stack(groups[1:])), own0)
        own_m = jnp.concatenate([links.half(up_weight), links.half(out_weight)], axis=1)
        m_own = lax.all_gather(own_m, "fsdp", axis=0, tiled=True)
        own_d = links.quarter(down_weight)
        z0 = links.to_z(own0)
        z12 = links.to_z(own12)
        b0 = jnp.stack([own0] + z0)
        by0 = links.y(b0)
        own_d = after(own_d, by0)
        z_d = links.to_z(own_d)
        q0 = [b0, by0, links.core(b0), links.core(by0)]
        small = jnp.stack([b0[:, -8:], by0[:, -8:]], axis=1)
        small = small.reshape(2, 2, 2, -1)[..., : (8 + n_up) * dl]
        small = flipped(small, links.bits()[:3], (0, 1, 2)).reshape(f_size, 8 + n_up, dl)
    else:
        small = lax.all_gather(small, "fsdp", axis=0)
        every = [lax.all_gather(w, "fsdp", axis=0, tiled=True) for w in groups]
        every = [w.reshape(4, 2, d // 8, 2, hw) for w in every]
        q0 = [every[0][:, y, :, c] for c in range(2) for y in range(2)]
        stacked = jnp.stack(every[1:])
        q12 = [stacked[:, :, y, :, c].transpose(1, 0, 2, 3) for c in range(2) for y in range(2)]
        up_all = lax.all_gather(up_weight, "fsdp", axis=0, tiled=True)
        out_all = lax.all_gather(out_weight, "fsdp", axis=0, tiled=True)
        m_parts = [
            jnp.concatenate([up_all[:, c * nu : (c + 1) * nu], out_all[:, c * no : (c + 1) * no]], axis=1)
            for c in range(2)
        ]
        every = lax.all_gather(down_weight, "fsdp", axis=0, tiled=True).reshape(4, 2, 2, ff // 16, 2, d // 2)
        d_parts = [every[:, y, x, :, c] for c in range(2) for x in range(2) for y in range(2)]

    ub = small[:, 8:].reshape(1, ff).astype(F32)
    par = small[:, :8].transpose(1, 0, 2).reshape(8, d).astype(F32)
    onehot, bias = masks(lengths[0], random_blocks[0], seq)
    xt = tokens.T

    def forward(g, pieces, index, tok):
        return attn_fwd(me, tok, par, onehot, bias, pieces, g, index)

    if direct:
        b12 = jnp.stack([own12] + z12)
        by12 = links.y(b12)
        f0 = forward(0, q0, None, after(tokens, b12))
        by12, *z_d = after((by12, *z_d), f0[3])
        q12 = [b12, by12, links.core(b12), links.core(by12)]
        b_d = jnp.stack([own_d] + z_d)
        by_d = links.y(b_d)
        f1 = forward(1, q12, 0, after(tokens, b_d))
        by_d = after(by_d, f1[3])
        near = [b_d, by_d]
        far = [links.x(a) for a in near]
        near_c = [links.core(a) for a in near]
        m_own = after(m_own, f1[3])
        m_other = links.core(m_own)
        f2 = forward(2, q12, 1, after(tokens, by_d))
        near_c, m_other = after((near_c, m_other), f2[3])
        m_parts = [m_own, m_other]
    else:
        f0 = forward(0, q0, None, tokens)
        f1 = forward(1, q12, 0, tokens)
        f2 = forward(2, q12, 1, tokens)
    fwd = [f0, f1, f2]
    cs = [o[3] for o in fwd]
    gact, gp, y, yb, n1, r1, wo, wu = mid_a(me, tokens, cs, par, ub, m_parts)
    if direct:
        far = after(far, y)
        d_parts = near + far + near_c + [links.core(a) for a in far]
    result, dh2, du, dkeep, dsend, sm2, ubg = mid_b(me, lengths, y, cotangent, par, gact, gp, d_parts)
    dh1, dc0, dc1, dc2, mkeep, msend, sm1 = mid_c(me, n1, r1, dh2, yb, cs, par, wo, du, wu)

    def backward(g, dc):
        q, k, v, c, lse, _ = fwd[g]
        return attn_bwd(me, xt, q, k, v, c, lse, dc, onehot, bias)

    if direct:
        dwid, mwid = dkeep.shape[1], mkeep.shape[1]
        drecv = after(links.core(dsend), dc0)
        mrecv = links.core(after(msend, drecv))
        total = summed((dkeep, drecv), (mkeep, mrecv))
        part = lax.psum_scatter(total, "fsdp", scatter_dimension=0, tiled=True)
        dm0, keep0, send0, db0 = backward(0, after(dc0, total))
        recv0 = links.core(send0)
        dm1, keep1, send1, db1 = backward(1, dc1)
        recv0 = after(recv0, db1)
        recv1 = links.core(send1)
        dm2, keep2, send2, db2 = backward(2, dc2)
        recv1 = after(recv1, db2)
        recv2 = links.core(send2)
        rows = keep0.shape[3]
        e = small_pieces([db0, db1, db2], sm1, sm2, ubg.reshape(8, ff // 8), me, rows)
        keeps = [keep0, keep1, keep2, e]
        recvs = [recv0, recv1, recv2, links.core(e)]
        hq = (3 * hw + 128) // 2
        ta, tb = stage(stage1_kernel, keeps + recvs, [((2, 4, rows, hq), BF)] * 2)
        ra, rb = links.x(ta), links.y(tb)
        grad_in = input_grad(after(dh1, ta, tb), [dm0, dm1, dm2], [o[5] for o in fwd])
        ra, rb = after((ra, rb), grad_in)
        ta, tb = stage(stage2_kernel, keeps + recvs + [ra, rb], [((4, rows, hq), BF)] * 2)
        sa, sb = links.y(ta), links.x(tb)
        base, *sends = stage(
            stage3_kernel, keeps + recvs + [ra, rb, sa, sb], [((rows, 2 * hq), F32)] + [((rows, 2 * hq), BF)] * 3
        )
        last = [links.z(t, i + 1) for i, t in enumerate(sends)]
        part = after(part, base)
        part_x = links.x(part)
        fin = added(base, *last).astype(BF)
        fx = links.x(fin)
        fc, fxc = links.core(fin), links.core(fx)
        part = added(part, part_x).astype(BF)
        part_c = links.core(part)
        fourth = part.shape[1] * 4 // 9
        down = [p[:, :fourth].reshape(-1, 4, no).transpose(1, 0, 2).reshape(-1, no) for p in (part, part_c)]
        down_grad = links.wide(*down).astype(F32)
        up_grad = links.wide(*(p[:, dwid : dwid + nu] for p in (part, part_c))).astype(F32)
        out_grad = links.wide(*(p[:, dwid + nu :] for p in (part, part_c))).astype(F32)
        x0, c0 = me[2] == 0, me[3] == 0
        qkv_cols = []
        for g in range(GROUPS):
            cut = [q[:, g * hw : (g + 1) * hw] for q in (fin, fc, fx, fxc)]
            m, t = links.wide(*cut[:2]), links.wide(*cut[2:])
            qkv_cols.append(
                jnp.concatenate([jnp.where(x0, m, t), jnp.where(x0, t, m)], axis=0).astype(F32)
            )
        cut = [q[: 8 + n_up, GROUPS * hw : GROUPS * hw + dl] for q in (fin, fc, fx, fxc)]
        own = jnp.where(x0, jnp.where(c0, cut[0], cut[1]), jnp.where(c0, cut[2], cut[3])).astype(F32)
    else:

        def total(full):
            part = lax.psum_scatter(full.astype(F32), "fsdp", scatter_dimension=0, tiled=True)
            return lax.psum(part.astype(BF), "replica").astype(F32)

        def pieces_total(keep, send):
            full = jnp.stack([keep, send])
            c, x, y_, z, r, n = full.shape
            return total(full.transpose(3, 2, 1, 4, 0, 5).reshape(z * y_ * x * r, c * n))

        backs = [backward(g, dc) for g, dc in enumerate((dc0, dc1, dc2))]
        grad_in = input_grad(dh1, [b[0] for b in backs], [o[5] for o in fwd])
        downs = jnp.stack([p.reshape(8, -1, 4, no).transpose(0, 2, 1, 3).reshape(ff, no) for p in (dkeep, dsend)], axis=1)
        down_grad = total(downs.reshape(ff, d))
        up_grad = total(jnp.concatenate([mkeep[:, :nu], msend[:, :nu]], axis=1))
        out_grad = total(jnp.concatenate([mkeep[:, nu:], msend[:, nu:]], axis=1))
        qkv_cols = [pieces_total(b[1], b[2]) for b in backs]
        db = jnp.concatenate([b[3] for b in backs], axis=1)
        rows = jnp.stack([db[0], db[1], sm1[2], sm2[2], sm1[0], sm2[0], sm1[1], sm2[1]])
        rows = rows.reshape(8, f_size, dl).transpose(1, 0, 2)
        every = jnp.concatenate([rows, ubg.reshape(f_size, n_up, dl)], axis=1)
        every = lax.psum(every, ("replica", "fsdp"))
        own = lax.dynamic_index_in_dim(every, lax.axis_index("fsdp"), 0, keepdims=False)
    qkv_grad = jnp.concatenate(
        [qkv_cols[g][:, j * gw : (j + 1) * gw] for j in range(3) for g in range(GROUPS)], axis=1
    )
    return (
        result,
        grad_in,
        qkv_grad,
        out_grad,
        up_grad,
        down_grad,
        own[:4],
        own[8:].reshape(ul),
        own[4:6],
        own[6:8],
    )


def solution(mesh):
    both = ("replica", "fsdp")
    return jax.shard_map(
        functools.partial(shards, mesh),
        mesh=mesh,
        in_specs=(
            P(both, None),
            P(both),
            P(both, None, None),
            P("fsdp", None),
            P("fsdp", None),
            P("fsdp", None),
            P("fsdp", None),
            P(None, "fsdp"),
            P("fsdp"),
            P(None, "fsdp"),
            P(None, "fsdp"),
            P(both, None),
        ),
        out_specs=(
            P(both, None),
            P(both, None),
            P("fsdp", None),
            P("fsdp", None),
            P("fsdp", None),
            P("fsdp", None),
            P(None, "fsdp"),
            P("fsdp"),
            P(None, "fsdp"),
            P(None, "fsdp"),
        ),
        check_vma=False,
    )
```

```python
import functools

import jax
import jax.numpy as jnp
from jax import lax
from jax.experimental import pallas as pl
from jax.experimental.pallas import tpu as pltpu
from jax.sharding import PartitionSpec as P

D = 768
HD = 64
BLK = 64
GROUPS = 3
EPS = 1e-06
BF = jnp.bfloat16
F32 = jnp.float32
ANY = pl.BlockSpec(memory_space=pl.ANY)
VM = pl.BlockSpec(memory_space=pltpu.VMEM)
SM = pl.BlockSpec(memory_space=pltpu.SMEM)


def dotf(a, b, ca, cb):
    return lax.dot_general(a, b, (((ca,), (cb,)), ((), ())), preferred_element_type=F32)


def lane_iota(shape):
    return lax.broadcasted_iota(jnp.int32, shape, 1)


def mult(v, m):
    return pl.multiple_of(v, m)


def columns(me, cr, cols):
    return pl.ds(mult(lax.bitwise_xor(me[3], cr) * cols, cols), cols)


def load_rows(me, refs, dst, sem):
    for k, (ref, rows) in enumerate(refs):
        cols = ref.shape[-1]
        for zr in range(4):
            f = lax.bitwise_xor(me[0], zr) * 2 + lax.bitwise_xor(me[1], k % 2)
            at = dst.at[pl.ds(mult(f * rows, rows), rows), columns(me, k // 2, cols)]
            pltpu.make_async_copy(ref.at[zr, pl.ds(0, rows)], at, sem).start()


def piece_rows(me, xr, yr, zr, rows):
    z = lax.bitwise_xor(me[0], zr)
    y = lax.bitwise_xor(me[1], yr)
    x = lax.bitwise_xor(me[2], xr)
    return pl.ds(mult(((z * 2 + y) * 2 + x) * rows, rows), rows)


def load_pieces(me, refs, dst, sem):
    for k, ref in enumerate(refs):
        cr, xr, yr = k // 4, (k // 2) % 2, k % 2
        rows, cols = ref.shape[1:]
        for zr in range(4):
            at = dst.at[piece_rows(me, xr, yr, zr, rows), columns(me, cr, cols)]
            pltpu.make_async_copy(ref.at[zr], at, sem).start()


def store_pieces(me, src, keep, send, sem):
    for cr, ref in ((1, send), (0, keep)):
        rows, cols = ref.shape[3:]
        for xr in range(2):
            for yr in range(2):
                for zr in range(4):
                    at = src.at[piece_rows(me, xr, yr, zr, rows), columns(me, cr, cols)]
                    pltpu.make_async_copy(at, ref.at[xr, yr, zr], sem).start()


def wait_all(ref, sem):
    pltpu.make_async_copy(ref, ref, sem).wait()


def read_me(me_ref):
    return [me_ref[i] for i in range(4)]


def piece_shape(rows, cols):
    return jax.ShapeDtypeStruct((2, 2, 4, rows // 16, cols // 2), BF)


def attn_fwd_kernel(first, n, load, me_ref, par_ref, x_hbm, qm_hbm, km_hbm, *refs):
    pieces, refs = refs[: len(refs) - 19], refs[len(refs) - 19 :]
    outs, refs = refs[:6], refs[6:]
    x_ref, qm_ref, km_ref, q_ref, k_ref, v_ref, c_ref, lse_ref, w_ref, kx_ref, vx_ref, sem, gsem = refs
    seq, gw = q_ref.shape[1:]
    me = read_me(me_ref)

    def fetch(g):
        load(me, [ref if n == 1 else ref.at[:, g] for ref in pieces], w_ref.at[g], gsem.at[g, 0])

    fetch(0)
    loads = ((x_hbm, x_ref, 0), (qm_hbm, qm_ref, 1), (km_hbm, km_ref, 2))
    for src, dst, i in loads:
        pltpu.make_async_copy(src, dst, sem.at[i]).start()
    for g in range(1, n):
        fetch(g)
    low = lane_iota((seq, 128)) < HD
    for src, dst, i in loads:
        pltpu.make_async_copy(src, dst, sem.at[i]).wait()

    def out_copies(g):
        whole = ((q_ref, 0), (k_ref, 1), (v_ref, 2), (w_ref, 5), (c_ref, 3), (lse_ref, 4))
        return [pltpu.make_async_copy(src.at[g], outs[i].at[g], gsem.at[g, i + 1]) for src, i in whole]

    def group_body(g, carry):
        wait_all(w_ref.at[g], gsem.at[g, 0])
        x = x_ref[...]
        w = w_ref.at[g]
        par = par_ref.at[first + g]
        q = dotf(x, w[:, :gw], 1, 0) + par[0:1, :]
        q_ref[g] = (q * (HD**-0.5)).astype(BF)
        k_ref[g] = dotf(x, w[:, gw : 2 * gw], 1, 0).astype(BF)
        v_ref[g] = (dotf(x, w[:, 2 * gw :], 1, 0) + par[1:2, :]).astype(BF)
        started = out_copies(g)
        for copy in started[:4]:
            copy.start()

        def pair_body(pair, carry):
            sl = pl.ds(mult(pair * 128, 128), 128)
            kp = k_ref[g, :, sl]
            vp = v_ref[g, :, sl]
            qx = jnp.concatenate([q_ref[g, :, sl], qm_ref[...]], axis=1)
            sums, lses = [], []
            for h in range(2):
                sel = low if h == 0 else jnp.logical_not(low)
                kx_ref[h, :, :128] = jnp.where(sel, kp, jnp.zeros_like(kp))
                kx_ref[h, :, 128:] = km_ref[...]
                vx_ref[h] = jnp.where(sel, vp, jnp.ones_like(vp))
            for h in range(2):
                s = dotf(qx, kx_ref[h], 1, 1)
                m = jnp.max(s, axis=1, keepdims=True)
                p = jnp.exp(s - m).astype(BF)
                c = dotf(p, vx_ref[h], 1, 0)
                t = pltpu.roll(c, HD, 1)
                sums.append(c / t)
                lses.append(m + jnp.log(t))
            c_ref[g, :, sl] = jnp.where(low, sums[0], sums[1]).astype(BF)
            lse_ref[g, :, sl] = jnp.where(low, lses[0], lses[1])
            return carry

        lax.fori_loop(0, gw // 128, pair_body, 0)
        for copy in started[4:]:
            copy.start()
        return carry

    lax.fori_loop(0, n, group_body, 0)
    for g in range(n):
        for copy in out_copies(g):
            copy.wait()


def attn_fwd(me, x, par, qm, km, pieces, first, n, load):
    seq, d = x.shape
    gw = d // GROUPS
    b = ((n, seq, gw), BF)
    shapes = [b, b, b, b, ((n, seq, gw), F32), ((n, d, 3 * gw), BF)]
    loaded = [((seq, d), BF), ((seq, 128), BF), ((seq, 128), BF)]
    return pl.pallas_call(
        functools.partial(attn_fwd_kernel, first, n, load),
        in_specs=[SM, VM] + [ANY] * (3 + len(pieces)),
        out_specs=[ANY] * 6,
        out_shape=[pltpu.HBM(*sh) for sh in shapes],
        scratch_shapes=[pltpu.VMEM(*sh) for sh in loaded + shapes]
        + [
            pltpu.VMEM((2, seq, 256), BF),
            pltpu.VMEM((2, seq, 128), BF),
            pltpu.SemaphoreType.DMA((3,)),
            pltpu.SemaphoreType.DMA((n, 7)),
        ],
        compiler_params=pltpu.CompilerParams(vmem_limit_bytes=38 << 20),
        cost_estimate=pl.CostEstimate(flops=n * 10_000_000_000, bytes_accessed=8 << 20, transcendentals=seq * seq * 4),
        name="attn_fwd",
    )(me, par, *in_hbm(x, qm, km), *pieces)


def split3(t):
    hi = t.astype(BF).astype(F32)
    r = t - hi
    mid = r.astype(BF).astype(F32)
    return hi, mid, r - mid


def small_rows(me, db, s1, s2, ub, out_ref):
    d = s1.shape[1]
    dl = d // 8
    rows = [db[0:1], db[1:2], s1[2:3], s2[2:3], s1[0:1], s2[0:1], s1[1:2], s2[1:2]]
    table = jnp.concatenate(rows, axis=0).astype(BF)
    out_ref[...] = jnp.zeros_like(out_ref)

    def pick(n, first):
        j = lax.broadcasted_iota(jnp.int32, (n, 128), 0)
        lane = lane_iota((n, 128))
        return ((j == lane + first) & (lane < dl)).astype(BF)

    ups = [dotf(ub.astype(BF), pick(ub.shape[1], k * dl), 1, 0) for k in range(4)]
    for f in range(8):
        top = dotf(table, pick(d, f * dl), 1, 0)
        both = jnp.concatenate([top] + [u[f : f + 1] for u in ups] + [jnp.zeros((4, 128), F32)], axis=0).astype(BF)
        for xr in range(2):
            out_ref[xr, lax.bitwise_xor(me[1], f % 2), lax.bitwise_xor(me[0], f // 2), 0:16, :] = both


def attn_bwd_kernel(me_ref, s1_ref, s2_ref, ub_ref, *refs):
    first_in, rest_in, dc_in = refs[:5], refs[5:10], refs[10]
    hbm, refs = refs[11:14], refs[14:]
    dm_hbm, keep_ref, send_ref, db_ref, e_ref = refs[:5]
    bufs, refs = refs[5:11], refs[11:]
    qm_ref, km_ref, xt_ref, dm_ref, kx, vx, qx, cx, pt, dst, dw, psem, sem, dsem, wsem = refs
    seq = xt_ref.shape[1]
    gw = dw.shape[2] // 3
    per = gw // 128
    npair = GROUPS * per
    lane = lane_iota((seq, 128))
    low = lane < HD
    columns_of = lambda i: pl.ds(mult(i * 128, 128), 128)

    def pair_copies(i, go):
        slot, g, at = lax.rem(i, 2), lax.div(i, per), columns_of(lax.rem(i, per))

        def move(src, j):
            copy = pltpu.make_async_copy(src, bufs[j].at[slot], psem.at[slot, j])
            copy.start() if go else copy.wait()

        move(dc_in.at[:, columns_of(i)], 5)
        if not go:
            for j in range(5):
                move(first_in[j].at[0, :, at], j)
            return

        @pl.when(g == 0)
        def _():
            for j in range(5):
                move(first_in[j].at[0, :, at], j)

        @pl.when(g > 0)
        def _():
            for j in range(5):
                move(rest_in[j].at[lax.max(g - 1, 0), :, at], j)

    pair_copies(0, True)
    whole = tuple(zip(hbm, (qm_ref, km_ref, xt_ref)))
    for j, (src, dst_) in enumerate(whole):
        pltpu.make_async_copy(src, dst_, sem.at[j]).start()
    for j, (src, dst_) in enumerate(whole):
        pltpu.make_async_copy(src, dst_, sem.at[j]).wait()
    me = read_me(me_ref)

    def pair_body(pair, carry):
        slot = lax.rem(pair, 2)
        pair_copies(pair, False)

        @pl.when(pair + 1 < npair)
        def _():
            pair_copies(pair + 1, True)

        qp, kp, vp, cp, lsep, dcp = (b[slot] for b in bufs)
        prod = dcp.astype(F32) * cp.astype(F32)
        zero = jnp.zeros_like(kp)
        one = jnp.ones_like(kp)
        qm = qm_ref[...].astype(F32)
        qx[:, :128] = qp
        cx[:, :128] = dcp
        for h in range(2):
            sel = low if h == 0 else jnp.logical_not(low)
            lse = jnp.max(jnp.where(sel, lsep, -3e38), axis=1, keepdims=True)
            delta = jnp.sum(jnp.where(sel, prod, 0.0), axis=1, keepdims=True)
            a, b, c = split3(-lse)
            qext = jnp.where(lane == 16, a, jnp.where(lane == 17, b, jnp.where(lane == 18, c, qm)))
            a, b, c = split3(-delta)
            cext = jnp.where(lane == 0, a, jnp.where(lane == 1, b, jnp.where(lane == 2, c, 0.0)))
            kx[h, :, :128] = jnp.where(sel, kp, zero)
            kx[h, :, 128:] = jnp.where((lane >= 16) & (lane < 19), one, km_ref[...])
            vx[h, :, :128] = jnp.where(sel, vp, zero)
            vx[h, :, 128:] = jnp.where(lane < 3, one, zero)
            qx[:, 128:] = qext.astype(BF)
            cx[:, 128:] = cext.astype(BF)
            p = jnp.exp(dotf(kx[h], qx[...], 1, 1))
            dp = dotf(vx[h], cx[...], 1, 1)
            pt[:, h * seq : (h + 1) * seq] = p.astype(BF)
            dst[:, h * seq : (h + 1) * seq] = (p * dp).astype(BF)
        qz = jnp.concatenate([jnp.where(low, qp, zero), jnp.where(low, zero, qp)], axis=0)
        cz = jnp.concatenate([jnp.where(low, dcp, zero), jnp.where(low, zero, dcp)], axis=0)
        dv = dotf(pt[...], cz, 1, 0)
        dk = dotf(dst[...], qz, 1, 0)
        dq = dotf(kx[0, :, :128], dst[:, :seq], 0, 0) + dotf(kx[1, :, :128], dst[:, seq:], 0, 0)
        dq = dq.T * (HD**-0.5)
        db_ref[0:1, columns_of(pair)] = jnp.sum(dq, axis=0, keepdims=True)
        db_ref[1:2, columns_of(pair)] = jnp.sum(dv, axis=0, keepdims=True)
        g, i = lax.div(pair, per), lax.rem(pair, per)
        for j, part in enumerate((dq, dk, dv)):
            at = columns_of(j * per + i)
            dm_ref[g, :, at] = part.astype(BF)
            pltpu.make_async_copy(dm_ref.at[g, :, at], dm_hbm.at[g, :, at], dsem).start()

        @pl.when(i == per - 1)
        def _():
            dw[g] = dotf(xt_ref[...], dm_ref[g], 1, 0).astype(BF)
            store_pieces(me, dw.at[g], keep_ref.at[g], send_ref.at[g], wsem)

        return carry

    lax.fori_loop(0, npair, pair_body, 0)
    small_rows(me, db_ref[...], s1_ref[...], s2_ref[...], ub_ref[...], e_ref)
    wait_all(dm_ref, dsem)
    wait_all(dw, wsem)


def attn_bwd(me, xt, first, rest, dc, qm, km, s1, s2, ub):
    n, seq, gw = rest[0].shape
    d = xt.shape[0]
    ps = pltpu.HBM((GROUPS,) + piece_shape(d, 3 * gw).shape, BF)
    shapes = [((GROUPS, seq, 3 * gw), BF)]
    one = pltpu.VMEM((2, seq, 128), BF)
    return pl.pallas_call(
        attn_bwd_kernel,
        in_specs=[SM] + [VM] * 3 + [ANY] * 14,
        out_specs=[ANY, ANY, ANY] + [VM] * 2,
        out_shape=[
            pltpu.HBM((GROUPS, seq, 3 * gw), BF),
            ps,
            ps,
            jax.ShapeDtypeStruct((2, d), F32),
            jax.ShapeDtypeStruct((2, 2, 4, d // 16, 128), BF),
        ],
        scratch_shapes=[
            one,
            one,
            one,
            one,
            pltpu.VMEM((2, seq, 128), F32),
            one,
            pltpu.VMEM((seq, 128), BF),
            pltpu.VMEM((seq, 128), BF),
            pltpu.VMEM((d, seq), BF),
            pltpu.VMEM((GROUPS, seq, 3 * gw), BF),
            pltpu.VMEM((2, seq, 256), BF),
            pltpu.VMEM((2, seq, 256), BF),
            pltpu.VMEM((seq, 256), BF),
            pltpu.VMEM((seq, 256), BF),
            pltpu.VMEM((seq, 2 * seq), BF),
            pltpu.VMEM((seq, 2 * seq), BF),
            pltpu.VMEM((GROUPS, d, 3 * gw), BF),
            pltpu.SemaphoreType.DMA((2, 6)),
            pltpu.SemaphoreType.DMA((3,)),
            pltpu.SemaphoreType.DMA,
            pltpu.SemaphoreType.DMA,
        ],
        compiler_params=pltpu.CompilerParams(vmem_limit_bytes=52 << 20),
        cost_estimate=pl.CostEstimate(flops=51_000_000_000, bytes_accessed=10 << 20, transcendentals=seq * seq * 12),
        name="attn_bwd",
    )(me, s1, s2, ub, *in_hbm(*first, *rest, dc, qm, km, xt))


def copies(pairs, sem):
    for src, dst in pairs:
        pltpu.make_async_copy(src, dst, sem).start()


def gelu_parts(u):
    u2 = u * u
    k1 = 0.7978845608028654
    k2 = k1 * 0.044715
    h = 0.5 + 0.5 * jnp.tanh(u * (k1 + k2 * u2))
    g = u * h
    return g, h + g * (1.0 - h) * (2 * k1 + (6 * k2) * u2)


def mid_a_kernel(rt, ft, me_ref, par_ref, ub_ref, x_hbm, c0_hbm, c12_hbm, *refs):
    pieces, refs = refs[:2], refs[2:]
    g, gp, y, yb, n1, r1, wo, wu, us, x_ref, c_ref, sem = refs
    me = read_me(me_ref)
    loads = ((c0_hbm, c_ref.at[pl.ds(0, 1)], 2), (c12_hbm, c_ref.at[pl.ds(1, 2)], 3), (x_hbm, x_ref, 4))
    for src, dst, k in loads:
        pltpu.make_async_copy(src, dst, sem.at[k]).start()
    nu, no = wu.shape[1] // 2, wo.shape[1] // 2
    for cr, ref in enumerate(pieces):
        pltpu.make_async_copy(ref.at[:, pl.ds(nu, no)], wo.at[:, columns(me, cr, no)], sem.at[0]).start()
    for cr, ref in enumerate(pieces):
        pltpu.make_async_copy(ref.at[:, pl.ds(0, nu)], wu.at[:, columns(me, cr, nu)], sem.at[1]).start()
    seq, d = x_ref.shape
    ff = wu.shape[1]
    gw = c_ref.shape[2]
    for src, dst, k in loads:
        pltpu.make_async_copy(src, dst, sem.at[k]).wait()
    wait_all(wo, sem.at[0])

    def rows_body(i, carry):
        rows = pl.ds(mult(i * rt, rt), rt)
        a = dotf(c_ref[0, rows, :], wo[:gw], 1, 0)
        a += dotf(c_ref[1, rows, :], wo[gw : 2 * gw], 1, 0)
        a += dotf(c_ref[2, rows, :], wo[2 * gw :], 1, 0)
        h = x_ref[rows, :].astype(F32) + (a + par_ref[2:3, :])
        cen = h - jnp.mean(h, axis=1, keepdims=True)
        r = lax.rsqrt(jnp.mean(cen * cen, axis=1, keepdims=True) + EPS)
        n = cen * r
        yt = n * par_ref[4:5, :] + par_ref[6:7, :]
        n1[rows, :] = n
        r1[rows, :] = jnp.broadcast_to(r, (rt, 128))
        y[rows, :] = yt
        yb[rows, :] = yt.astype(BF)
        return carry

    lax.fori_loop(0, seq // rt, rows_body, 0)
    wait_all(wu, sem.at[1])

    def product(i, slot):
        cs = pl.ds(mult(i * ft, ft), ft)
        us[slot] = dotf(yb[...], wu[:, cs], 1, 0)

    def finish(i, slot):
        cs = pl.ds(mult(i * ft, ft), ft)
        gt, gpt = gelu_parts(us[slot] + ub_ref[:, cs])
        g[:, cs] = gt.astype(BF)
        gp[:, cs] = gpt.astype(BF)

    last = ff // ft - 1
    product(0, 0)

    def cols_body(i, carry):
        product(2 * i + 1, 1)
        finish(2 * i, 0)
        product(lax.min(2 * i + 2, last), 0)
        finish(2 * i + 1, 1)
        return carry

    lax.fori_loop(0, ff // ft // 2, cols_body, 0)


def in_vmem(*arrays):
    return [pltpu.with_memory_space_constraint(a, pltpu.VMEM) for a in arrays]


def in_hbm(*arrays):
    return [pltpu.with_memory_space_constraint(a, pltpu.HBM) for a in arrays]


def mid_a(me, x, cs, par, ub, pieces):
    seq, d = x.shape
    ff = ub.shape[1]
    ft = 512
    shapes = [((seq, ff), BF), ((seq, ff), BF), ((seq, d), F32), ((seq, d), BF), ((seq, d), F32), ((seq, 128), F32)]
    shapes += [((d, d), BF), ((d, ff), BF)]
    return pl.pallas_call(
        functools.partial(mid_a_kernel, 256, ft),
        in_specs=[SM] + [VM] * 2 + [ANY] * 5,
        out_specs=[VM] * 8,
        out_shape=[pltpu.VMEM(*sh) for sh in shapes],
        scratch_shapes=[pltpu.VMEM((2, seq, ft), F32), pltpu.VMEM((seq, d), BF)]
        + [pltpu.VMEM((GROUPS, seq, d // GROUPS), BF), pltpu.SemaphoreType.DMA((5,))],
        compiler_params=pltpu.CompilerParams(vmem_limit_bytes=15 << 20),
        cost_estimate=pl.CostEstimate(
            flops=2 * seq * d * (d + ff), bytes_accessed=20 << 20, transcendentals=seq * ff
        ),
        name="mid_a",
    )(me, par, ub, *in_hbm(x, *cs, *pieces))


def mid_b_kernel(rt, ft, me_ref, len_ref, par_ref, y, g, gp, cot_hbm, *refs):
    wd_p, refs = refs[:8], refs[8:]
    out_hbm, dh2, du, keep_ref, send_ref, sm_ref, ubg_ref, cot, wd, dz, dw, sem, tsem = refs
    me = read_me(me_ref)
    load_pieces(me, wd_p, wd, sem.at[0])
    pltpu.make_async_copy(cot_hbm, cot, sem.at[1]).start()
    seq, d = y.shape
    ff = g.shape[1]
    tiles = seq // rt
    length = len_ref[0]
    sm_ref[...] = jnp.zeros_like(sm_ref)
    wait_all(wd, sem.at[0])
    pltpu.make_async_copy(cot_hbm, cot, sem.at[1]).wait()

    def rows_body(i, carry):
        rows = pl.ds(mult(i * rt, rt), rt)
        z = dotf(g[rows, :], wd[...], 1, 0) + par_ref[3:4, :]
        h = y[rows, :] + z
        cen = h - jnp.mean(h, axis=1, keepdims=True)
        r = lax.rsqrt(jnp.mean(cen * cen, axis=1, keepdims=True) + EPS)
        n = cen * r
        pos = lax.broadcasted_iota(jnp.int32, (rt, 1), 0) + i * rt
        valid = pos < length
        do = jnp.where(valid, cot[rows, :].astype(F32), 0.0)
        res = n * par_ref[5:6, :] + par_ref[7:8, :]
        cot[rows, :] = jnp.where(valid, res, 0.0).astype(BF)
        e = do * par_ref[5:6, :]
        me_ = jnp.mean(e, axis=1, keepdims=True)
        men = jnp.mean(e * n, axis=1, keepdims=True)
        dh = r * (e - me_ - n * men)
        dh2[rows, :] = dh
        dz[rows, :] = dh.astype(BF)
        sm_ref[0:1, :] += jnp.sum(do * n, axis=0, keepdims=True)
        sm_ref[1:2, :] += jnp.sum(do, axis=0, keepdims=True)
        sm_ref[2:3, :] += jnp.sum(dh, axis=0, keepdims=True)
        return carry

    lax.fori_loop(0, tiles, rows_body, 0)
    pltpu.make_async_copy(cot, out_hbm, sem.at[2]).start()
    n = d // 2
    part = ff // 32

    def dw_body(f, carry):
        rows = pl.ds(mult(f * 4 * part, part), 4 * part)
        dw[rows, :] = dotf(g[:, rows], dz[...], 0, 0).astype(BF)
        for cr, ref in ((1, send_ref), (0, keep_ref)):
            for j in range(4):
                at = dw.at[pl.ds(mult((f * 4 + j) * part, part), part), columns(me, cr, n)]
                to = ref.at[pl.ds(mult(f * part, part), part), pl.ds(j * n, n)]
                pltpu.make_async_copy(at, to, sem.at[3]).start()
        return carry

    lax.fori_loop(0, 8, dw_body, 0)

    def du_body(i, carry):
        cs = pl.ds(mult(i * 4 * part, 4 * part), 4 * part)
        dg = dotf(dz[...], wd[cs, :], 1, 1)
        dut = dg * gp[:, cs].astype(F32)
        ubg_ref[pl.ds(i, 1), :] = jnp.sum(dut, axis=0, keepdims=True)
        du[:, cs] = dut.astype(BF)
        return carry

    lax.fori_loop(0, 8, du_body, 0)
    pltpu.make_async_copy(cot, out_hbm, sem.at[2]).wait()
    wait_all(dw, sem.at[3])


def mid_b(me, length, y, cot, par, g, gp, wd_p):
    seq, d = y.shape
    ff = g.shape[1]
    rt = 256
    S = jax.ShapeDtypeStruct
    ps = pltpu.HBM((ff // 4, 2 * d), BF)
    return pl.pallas_call(
        functools.partial(mid_b_kernel, rt, 512),
        in_specs=[SM] * 2 + [VM] * 4 + [ANY] * 9,
        out_specs=[ANY] + [VM] * 2 + [ANY] * 2 + [VM] * 2,
        out_shape=[
            pltpu.HBM((seq, d), BF),
            pltpu.VMEM((seq, d), F32),
            pltpu.VMEM((seq, ff), BF),
            ps,
            ps,
            S((8, d), F32),
            S((8, ff // 8), F32),
        ],
        input_output_aliases={3: 1, 5: 2},
        scratch_shapes=[
            pltpu.VMEM((seq, d), BF),
            pltpu.VMEM((ff, d), BF),
            pltpu.VMEM((seq, d), BF),
            pltpu.VMEM((ff, d), BF),
            pltpu.SemaphoreType.DMA((4,)),
            pltpu.SemaphoreType.DMA((3, seq // rt)),
        ],
        compiler_params=pltpu.CompilerParams(vmem_limit_bytes=17 << 20),
        cost_estimate=pl.CostEstimate(flops=6 * seq * d * ff, bytes_accessed=20 << 20, transcendentals=seq),
        name="mid_b",
    )(me, length, par, *in_vmem(y, g, gp), *in_hbm(cot, *wd_p))


def mid_c_kernel(rt, ft, me_ref, par_ref, n1, r1, dh2, yb, wo, du, wu, *refs):
    c0_h, c12_h = refs[:2]
    dh1_h, dc_h, keep, send, sm_ref = refs[2:7]
    cs_, dwu, dwo, da, dc, dh1, sem = refs[7:]
    me = read_me(me_ref)
    seq, d = n1.shape
    ff = du.shape[1]
    gw = d // 3
    nu, no = ff // 2, d // 2
    steps = nu // ft
    for i in range(GROUPS):
        ref = c0_h.at[0] if i == 0 else c12_h.at[i - 1]
        pltpu.make_async_copy(ref, cs_.at[:, i * gw : (i + 1) * gw], sem.at[0]).start()
    sm_ref[...] = jnp.zeros_like(sm_ref)
    for cr, ref in ((1, send), (0, keep)):

        def dwu_body(j, carry):
            at = pl.ds(mult(lax.bitwise_xor(me[3], cr) * nu + j * ft, ft), ft)
            dwu[:, at] = dotf(yb[...], du[:, at], 0, 0).astype(BF)
            pltpu.make_async_copy(dwu.at[:, at], ref.at[:, pl.ds(mult(j * ft, ft), ft)], sem.at[1]).start()
            return carry

        lax.fori_loop(0, steps, dwu_body, 0)

    def rows_body(i, carry):
        rows = pl.ds(mult(i * rt, rt), rt)
        dy = dh2[rows, :] + dotf(du[rows, :], wu[...], 1, 1)
        n = n1[rows, :]
        e = dy * par_ref[4:5, :]
        me_ = jnp.mean(e, axis=1, keepdims=True)
        men = jnp.mean(e * n, axis=1, keepdims=True)
        dh = r1[rows, 0:1] * (e - me_ - n * men)
        dh1[rows, :] = dh
        dat = dh.astype(BF)
        da[rows, :] = dat
        sm_ref[0:1, :] += jnp.sum(dy * n, axis=0, keepdims=True)
        sm_ref[1:2, :] += jnp.sum(dy, axis=0, keepdims=True)
        sm_ref[2:3, :] += jnp.sum(dh, axis=0, keepdims=True)
        dc[rows, :] = dotf(dat, wo[...], 1, 1).astype(BF)
        return carry

    lax.fori_loop(0, seq // rt, rows_body, 0)
    pltpu.make_async_copy(dh1, dh1_h, sem.at[2]).start()
    pltpu.make_async_copy(dc, dc_h, sem.at[3]).start()
    wait_all(cs_, sem.at[0])
    for cr, ref in ((1, send), (0, keep)):
        at = columns(me, cr, no)
        dwo[:, at] = dotf(cs_[...], da[:, at], 0, 0).astype(BF)
        pltpu.make_async_copy(dwo.at[:, at], ref.at[:, pl.ds(nu, no)], sem.at[4]).start()
    pltpu.make_async_copy(dh1, dh1_h, sem.at[2]).wait()
    wait_all(dc, sem.at[3])
    wait_all(dwu, sem.at[1])
    wait_all(dwo, sem.at[4])


def mid_c(me, n1, r1, dh2, yb, cs, par, wo, du, wu):
    seq, d = n1.shape
    ff = du.shape[1]
    S = jax.ShapeDtypeStruct
    ps = pltpu.HBM((d, (ff + d) // 2), BF)
    dc = pltpu.HBM((seq, d), BF)
    ft = 512
    return pl.pallas_call(
        functools.partial(mid_c_kernel, 256, ft),
        in_specs=[SM] + [VM] * 8 + [ANY] * 2,
        out_specs=[ANY] * 4 + [VM],
        out_shape=[pltpu.HBM((seq, d), F32), dc, ps, ps, S((8, d), F32)],
        scratch_shapes=[
            pltpu.VMEM((seq, d), BF),
            pltpu.VMEM((d, ff), BF),
            pltpu.VMEM((d, d), BF),
            pltpu.VMEM((seq, d), BF),
            pltpu.VMEM((seq, d), BF),
            pltpu.VMEM((seq, d), F32),
            pltpu.SemaphoreType.DMA((5,)),
        ],
        compiler_params=pltpu.CompilerParams(vmem_limit_bytes=18 << 20),
        cost_estimate=pl.CostEstimate(flops=4 * seq * d * (ff + d), bytes_accessed=20 << 20, transcendentals=seq),
        name="mid_c",
    )(me, par, *in_vmem(n1, r1, dh2, yb, wo, du, wu), *in_hbm(*cs))


def input_grad_kernel(dh1_ref, m_ref, w0, w12, out_ref):
    acc = dh1_ref[...]
    for g in range(GROUPS):
        acc += dotf(m_ref[g], w0[0] if g == 0 else w12[g - 1], 1, 1)
    out_ref[...] = acc


def input_grad(dh1, dm, w0, w12):
    seq, d = dh1.shape
    n = dm.shape[2]
    rt = 256
    row = pl.BlockSpec((rt, d), lambda i: (i, 0))
    full = lambda k: pl.BlockSpec((k, d, n), lambda i: (0, 0, 0))
    return pl.pallas_call(
        input_grad_kernel,
        grid=(seq // rt,),
        in_specs=[row, pl.BlockSpec((GROUPS, rt, n), lambda i: (0, i, 0)), full(1), full(GROUPS - 1)],
        out_specs=row,
        out_shape=jax.ShapeDtypeStruct((seq, d), F32),
        compiler_params=pltpu.CompilerParams(vmem_limit_bytes=60 << 20),
        cost_estimate=pl.CostEstimate(flops=6 * seq * d * n, bytes_accessed=15 << 20, transcendentals=0),
        name="input_grad",
    )(dh1, dm, w0, w12)


def sum_kernel(*refs):
    out = refs[-1]
    first = 0
    for a, b in zip(refs[0:-1:2], refs[1:-1:2]):
        w = a.shape[1]
        out[:, first : first + w] = (a[...].astype(F32) + b[...].astype(F32)).astype(BF)
        first += w


def summed(*pairs):
    rows = pairs[0][0].shape[0]
    rt = rows // 8
    width = sum(a.shape[1] for a, _ in pairs)
    one = lambda w: pl.BlockSpec((rt, w), lambda i: (i, 0))
    arrays = [a for pair in pairs for a in pair]
    return pl.pallas_call(
        sum_kernel,
        grid=(8,),
        in_specs=[one(a.shape[1]) for a in arrays],
        out_specs=one(width),
        out_shape=jax.ShapeDtypeStruct((rows, width), BF),
        compiler_params=pltpu.CompilerParams(vmem_limit_bytes=16 << 20),
        cost_estimate=pl.CostEstimate(flops=rows * width, bytes_accessed=6 * rows * width, transcendentals=0),
        name="summed",
    )(*arrays)


def parts_of(groups, e, lower):
    n = groups.shape[-1] // 3
    if lower:
        return [(groups.at[1], 2 * n, n), (groups.at[2], 0, 3 * n), (e, 0, 128)]
    return [(groups.at[0], 0, 3 * n), (groups.at[1], 0, 2 * n)]


def fill(out, index, keeps, recvs, lower, at, more=()):
    first = 0
    for (k, c, w), (r, _, _) in zip(parts_of(*keeps, lower), parts_of(*recvs, lower)):
        total = k[at + (slice(c, c + w),)].astype(F32) + r[at + (slice(c, c + w),)].astype(F32)
        for m, m_at in more:
            total += m[m_at + (slice(first, first + w),)].astype(F32)
        out[index + (slice(first, first + w),)] = total.astype(out.dtype)
        first += w


def stage1_kernel(*refs):
    keeps, recvs, (ta, tb) = refs[:2], refs[2:4], refs[4:]
    for i in range(2):
        fill(ta, (i, slice(None), slice(None)), keeps, recvs, False, (1, i, slice(None), slice(None)))
        fill(tb, (i, slice(None), slice(None)), keeps, recvs, True, (i, 1, slice(None), slice(None)))


def stage2_kernel(*refs):
    keeps, recvs, (ra, rb), (ta, tb) = refs[:2], refs[2:4], refs[4:6], refs[6:]
    every = (slice(None), slice(None))
    fill(ta, every, keeps, recvs, False, (0, 1) + every, [(ra, (1,) + every)])
    fill(tb, every, keeps, recvs, True, (1, 0) + every, [(rb, (1,) + every)])


def stage3_kernel(*refs):
    keeps, recvs, (ra, rb, sa, sb), outs = refs[:2], refs[2:4], refs[4:8], refs[8:]
    half = sa.shape[-1]
    for zr, out in enumerate(outs):
        at = (0, 0, zr, slice(None))
        for lower, r, t in ((False, ra, sa), (True, rb, sb)):
            view = out.at[:, pl.ds(half * lower, half)]
            fill(view, (slice(None),), keeps, recvs, lower, at, [(r, (0, zr, slice(None))), (t, (zr, slice(None)))])


def stage(kernel, arrays, shapes):
    nbytes = sum(a.size * 2 for a in arrays)
    return pl.pallas_call(
        kernel,
        in_specs=[VM] * len(arrays),
        out_specs=[VM] * len(shapes),
        out_shape=[jax.ShapeDtypeStruct(sh, dt) for sh, dt in shapes],
        compiler_params=pltpu.CompilerParams(vmem_limit_bytes=12 << 20),
        cost_estimate=pl.CostEstimate(flops=nbytes, bytes_accessed=nbytes, transcendentals=0),
        name=kernel.__name__[:6],
    )(*arrays)


def after(value, *others):
    return lax.optimization_barrier((value, *others))[0]


def added(*parts):
    return sum(p.astype(F32) for p in parts)


def flipped(array, bits, axes):
    for bit, axis in zip(bits, axes):
        array = jnp.where(bit == 1, jnp.flip(array, axis), array)
    return array


class Links:
    def __init__(self, mesh):
        r, f = mesh.shape["replica"], mesh.shape["fsdp"]
        self.direct = (r, f) == (4, 8)
        if self.direct:
            fi, ri = lax.axis_index("fsdp"), lax.axis_index("replica")
            self.me = jnp.stack([fi // 2, fi % 2, ri // 2, ri % 2]).astype(jnp.int32)
        else:
            self.me = jnp.zeros((4,), jnp.int32)

    def core(self, a):
        return lax.ppermute(a, "replica", [(i, i ^ 1) for i in range(4)])

    def x(self, a):
        return lax.ppermute(a, "replica", [(i, i ^ 2) for i in range(4)])

    def y(self, a):
        return lax.ppermute(a, "fsdp", [(i, i ^ 1) for i in range(8)])

    def z(self, a, d):
        return lax.ppermute(a, "fsdp", [(i, i ^ (2 * d)) for i in range(8)])

    def xy(self, a):
        both = ("replica", "fsdp")
        return lax.ppermute(a, both, [(i, i ^ 17) for i in range(32)])

    def to_plane(self, a):
        return [self.y(a), self.x(a), self.xy(a)]

    def to_z(self, own):
        return [self.z(own, d) for d in (1, 2, 3)]

    def half(self, shard):
        n = shard.shape[-1] // 2
        return lax.dynamic_slice_in_dim(shard, self.me[3] * n, n, shard.ndim - 1)

    def quarter(self, shard):
        r = shard.shape[0] // 2
        return lax.dynamic_slice_in_dim(self.half(shard), self.me[2] * r, r, 0)

    def bits(self):
        z, y, x, c = (self.me[i] for i in range(4))
        return z // 2, z % 2, y, x, c

    def wide(self, own, other):
        c0 = self.me[3] == 0
        return jnp.concatenate([jnp.where(c0, own, other), jnp.where(c0, other, own)], axis=1)


def masks(length, chosen, seq):
    nb = chosen.shape[0]
    used = (length + BLK - 1) // BLK
    lane = jnp.arange(128, dtype=jnp.int32)[None, :]
    pos = jnp.arange(seq, dtype=jnp.int32)[:, None]
    kb = pos // BLK
    onehot = (kb == lane).astype(BF)
    picks = jnp.pad(chosen, ((0, 128 - nb), (0, 0)), constant_values=-1)
    allowed = (jnp.abs(lane - kb) <= 1) | (kb == 0) | (kb == used - 1) | (lane == 0) | (lane == used - 1)
    for i in range(chosen.shape[1]):
        allowed |= picks[:, i][None, :] == kb
    bias = jnp.where(allowed & (pos < length), 0.0, -1e9)
    return onehot, jnp.where(lane < nb, bias, 0.0).astype(BF)


def shards(mesh, tokens, lengths, random_blocks, qkv_weight, out_weight, up_weight, down_weight, proj_bias,
           up_bias, norm_gain, norm_bias, cotangent):
    links = Links(mesh)
    me = links.me
    direct = links.direct
    seq, d = tokens.shape
    gw = d // GROUPS
    hw = 3 * gw // 2
    f_size = mesh.shape["fsdp"]
    dl = proj_bias.shape[1]
    ul = up_bias.shape[0]
    n_up = ul // dl
    ff = ul * f_size
    nu, no = ff // 2, d // 2
    small = jnp.concatenate([proj_bias, norm_gain, norm_bias, up_bias.reshape(n_up, dl)], axis=0)

    groups = []
    for g in range(GROUPS):
        cut = [qkv_weight[:, j * d + g * gw : j * d + (g + 1) * gw] for j in range(3)]
        groups.append(jnp.concatenate(cut, axis=1))
    if direct:
        own0 = jnp.concatenate([links.half(groups[0]), jnp.pad(small.reshape(-1, hw), ((0, 8 - small.size // hw), (0, 0)))])
        own_m = jnp.concatenate([links.half(up_weight), links.half(out_weight)], axis=1)
        m_own = lax.all_gather(own_m, "fsdp", axis=0, tiled=True)
        own0 = after(own0, own_m)
        rows = groups[0].shape[0] // 2
        own12 = lax.dynamic_slice_in_dim(links.half(jnp.stack(groups[1:])), me[2] * rows, rows, 1)
        own12 = after(own12, own0)
        own_d = links.quarter(down_weight)
        z0 = links.to_z(own0)
        z12 = links.to_z(own12)
        b0 = jnp.stack([own0] + z0)
        by0 = links.y(b0)
        q0 = [b0, by0, links.core(b0), links.core(by0)]
        small = jnp.stack([b0[:, -8:], by0[:, -8:]], axis=1)
        small = small.reshape(2, 2, 2, -1)[..., : (8 + n_up) * dl]
        small = flipped(small, links.bits()[:3], (0, 1, 2)).reshape(f_size, 8 + n_up, dl)
    else:
        small = lax.all_gather(small, "fsdp", axis=0)
        every = [lax.all_gather(w, "fsdp", axis=0, tiled=True) for w in groups]
        q0 = every[0].reshape(4, 2, d // 8, 2, hw)
        q0 = [q0[:, y, :, c] for c in range(2) for y in range(2)]
        q12 = jnp.stack([w.reshape(4, 2, 2, d // 16, 2, hw) for w in every[1:]], axis=1)
        q12 = [q12[:, :, y, x, :, c] for c in range(2) for x in range(2) for y in range(2)]
        up_all = lax.all_gather(up_weight, "fsdp", axis=0, tiled=True)
        out_all = lax.all_gather(out_weight, "fsdp", axis=0, tiled=True)
        m_parts = [
            jnp.concatenate([up_all[:, c * nu : (c + 1) * nu], out_all[:, c * no : (c + 1) * no]], axis=1)
            for c in range(2)
        ]
        every = lax.all_gather(down_weight, "fsdp", axis=0, tiled=True).reshape(4, 2, 2, ff // 16, 2, d // 2)
        d_parts = [every[:, y, x, :, c] for c in range(2) for x in range(2) for y in range(2)]

    ub = small[:, 8:].reshape(1, ff).astype(F32)
    par = small[:, :8].transpose(1, 0, 2).reshape(8, d).astype(F32)
    onehot, bias = masks(lengths[0], random_blocks[0], seq)
    xt = tokens.T

    par3 = jnp.stack([par[:2, g * gw : (g + 1) * gw] for g in range(GROUPS)])
    one_rows = lambda m, refs, dst, sem: load_rows(m, [(ref, d // 8) for ref in refs], dst, sem)

    if direct:
        b12 = jnp.stack([own12] + z12)
        plane = links.to_plane(b12)
        f0 = attn_fwd(me, after(tokens, xt, b12), par3, onehot, bias, q0, 0, 1, one_rows)
        own_d, *plane = after((own_d, *plane), f0[3])
        z_d = links.to_z(own_d)
        near = [b12] + plane
        q12 = near + [links.core(a) for a in near]
        f12 = attn_fwd(me, tokens, par3, onehot, bias, q12, 1, 2, load_pieces)
        m_own, *z_d = after((m_own, *z_d), f12[3])
        b_d = jnp.stack([own_d] + z_d)
        plane = links.to_plane(b_d)
        core_b = links.core(b_d)
        m_parts = [m_own, after(links.core(m_own), b_d)]
    else:
        f0 = attn_fwd(me, tokens, par3, onehot, bias, q0, 0, 1, one_rows)
        f12 = attn_fwd(me, tokens, par3, onehot, bias, q12, 1, 2, load_pieces)
    cs = [f0[3], f12[3]]
    gact, gp, y, yb, n1, r1, wo, wu = mid_a(me, tokens, cs, par, ub, m_parts)
    if direct:
        *plane, core_b = after((*plane, core_b), y)
        d_parts = [b_d] + plane + [core_b] + [links.core(a) for a in plane]
    result, dh2, du, dkeep, dsend, sm2, ubg = mid_b(me, lengths, y, cotangent, par, gact, gp, d_parts)
    dh1, dc, mkeep, msend, sm1 = mid_c(me, n1, r1, dh2, yb, cs, par, wo, du, wu)

    def backward(dc):
        return attn_bwd(me, xt, f0[:5], f12[:5], dc, onehot, bias, sm1, sm2, ubg)

    if direct:
        dwid, mwid = dkeep.shape[1], mkeep.shape[1]
        drecv = after(links.core(dsend), dc)
        mrecv = links.core(after(msend, drecv))
        total = summed((dkeep, drecv), (mkeep, mrecv))
        part = lax.psum_scatter(total, "fsdp", scatter_dimension=0, tiled=True)
        dm, keep, send, db, e = backward(after(dc, total))
        rows = keep.shape[4]
        arrays = [keep, e, links.core(send), links.core(e)]
        hq = (3 * hw + 128) // 2
        ta, tb = stage(stage1_kernel, arrays, [((2, 4, rows, hq), BF)] * 2)
        ra, rb = links.x(ta), links.y(tb)
        grad_in = input_grad(after(dh1, ta, tb), dm, f0[5], f12[5])
        ra, rb = after((ra, rb), grad_in)
        ta, tb = stage(stage2_kernel, arrays + [ra, rb], [((4, rows, hq), BF)] * 2)
        sa, sb = links.y(ta), links.x(tb)
        base, *sends = stage(
            stage3_kernel, arrays + [ra, rb, sa, sb], [((rows, 2 * hq), F32)] + [((rows, 2 * hq), BF)] * 3
        )
        last = [links.z(t, i + 1) for i, t in enumerate(sends)]
        fin = added(base, *last).astype(BF)
        fx = links.x(fin)
        fc, fxc = links.core(fin), links.core(fx)
        part = after(part, fxc)
        part = added(part, links.x(part)).astype(BF)
        part_c = links.core(part)
        fourth = part.shape[1] * 4 // 9
        down = [p[:, :fourth].reshape(-1, 4, no).transpose(1, 0, 2).reshape(-1, no) for p in (part, part_c)]
        down_grad = links.wide(*down).astype(F32)
        up_grad = links.wide(*(p[:, dwid : dwid + nu] for p in (part, part_c))).astype(F32)
        out_grad = links.wide(*(p[:, dwid + nu :] for p in (part, part_c))).astype(F32)
        x0, c0 = me[2] == 0, me[3] == 0
        qkv_cols = []
        for g in range(GROUPS):
            cut = [q[:, g * hw : (g + 1) * hw] for q in (fin, fc, fx, fxc)]
            m, t = links.wide(*cut[:2]), links.wide(*cut[2:])
            qkv_cols.append(
                jnp.concatenate([jnp.where(x0, m, t), jnp.where(x0, t, m)], axis=0).astype(F32)
            )
        cut = [q[: 8 + n_up, GROUPS * hw : GROUPS * hw + dl] for q in (fin, fc, fx, fxc)]
        own = jnp.where(x0, jnp.where(c0, cut[0], cut[1]), jnp.where(c0, cut[2], cut[3])).astype(F32)
    else:

        def total(full):
            part = lax.psum_scatter(full.astype(F32), "fsdp", scatter_dimension=0, tiled=True)
            return lax.psum(part.astype(BF), "replica").astype(F32)

        def pieces_total(keep, send):
            full = jnp.stack([keep, send])
            c, x, y_, z, r, n = full.shape
            return total(full.transpose(3, 2, 1, 4, 0, 5).reshape(z * y_ * x * r, c * n))

        dm, keep, send, db, _ = backward(dc)
        grad_in = input_grad(dh1, dm, f0[5], f12[5])
        downs = jnp.stack([p.reshape(8, -1, 4, no).transpose(0, 2, 1, 3).reshape(ff, no) for p in (dkeep, dsend)], axis=1)
        down_grad = total(downs.reshape(ff, d))
        up_grad = total(jnp.concatenate([mkeep[:, :nu], msend[:, :nu]], axis=1))
        out_grad = total(jnp.concatenate([mkeep[:, nu:], msend[:, nu:]], axis=1))
        qkv_cols = [pieces_total(keep[g], send[g]) for g in range(GROUPS)]
        rows = jnp.stack([db[0], db[1], sm1[2], sm2[2], sm1[0], sm2[0], sm1[1], sm2[1]])
        rows = rows.reshape(8, f_size, dl).transpose(1, 0, 2)
        every = jnp.concatenate([rows, ubg.reshape(f_size, n_up, dl)], axis=1)
        every = lax.psum(every, ("replica", "fsdp"))
        own = lax.dynamic_index_in_dim(every, lax.axis_index("fsdp"), 0, keepdims=False)
    qkv_grad = jnp.concatenate(
        [qkv_cols[g][:, j * gw : (j + 1) * gw] for j in range(3) for g in range(GROUPS)], axis=1
    )
    return (
        result,
        grad_in,
        qkv_grad,
        out_grad,
        up_grad,
        down_grad,
        own[:4],
        own[8:].reshape(ul),
        own[4:6],
        own[6:8],
    )


def solution(mesh):
    both = ("replica", "fsdp")
    return jax.shard_map(
        functools.partial(shards, mesh),
        mesh=mesh,
        in_specs=(
            P(both, None),
            P(both),
            P(both, None, None),
            P("fsdp", None),
            P("fsdp", None),
            P("fsdp", None),
            P("fsdp", None),
            P(None, "fsdp"),
            P("fsdp"),
            P(None, "fsdp"),
            P(None, "fsdp"),
            P(both, None),
        ),
        out_specs=(
            P(both, None),
            P(both, None),
            P("fsdp", None),
            P("fsdp", None),
            P("fsdp", None),
            P("fsdp", None),
            P(None, "fsdp"),
            P("fsdp"),
            P(None, "fsdp"),
            P(None, "fsdp"),
        ),
        check_vma=False,
    )
```

```python
import functools

import jax
import jax.numpy as jnp
from jax import lax
from jax.experimental import pallas as pl
from jax.experimental.pallas import tpu as pltpu
from jax.sharding import PartitionSpec as P

D = 768
HD = 64
BLK = 64
GROUPS = 3
EPS = 1e-06
BF = jnp.bfloat16
F32 = jnp.float32
ANY = pl.BlockSpec(memory_space=pl.ANY)
VM = pl.BlockSpec(memory_space=pltpu.VMEM)
SM = pl.BlockSpec(memory_space=pltpu.SMEM)


def dotf(a, b, ca, cb):
    return lax.dot_general(a, b, (((ca,), (cb,)), ((), ())), preferred_element_type=F32)


def lane_iota(shape):
    return lax.broadcasted_iota(jnp.int32, shape, 1)


def mult(v, m):
    return pl.multiple_of(v, m)


def columns(me, cr, cols):
    return pl.ds(mult(lax.bitwise_xor(me[3], cr) * cols, cols), cols)


def load_rows(me, refs, dst, sem):
    for k, (ref, rows) in enumerate(refs):
        cols = ref.shape[-1]
        for zr in range(4):
            f = lax.bitwise_xor(me[0], zr) * 2 + lax.bitwise_xor(me[1], k % 2)
            at = dst.at[pl.ds(mult(f * rows, rows), rows), columns(me, k // 2, cols)]
            pltpu.make_async_copy(ref.at[zr, pl.ds(0, rows)], at, sem).start()


def piece_rows(me, xr, yr, zr, rows):
    z = lax.bitwise_xor(me[0], zr)
    y = lax.bitwise_xor(me[1], yr)
    x = lax.bitwise_xor(me[2], xr)
    return pl.ds(mult(((z * 2 + y) * 2 + x) * rows, rows), rows)


def load_pieces(me, refs, dst, sem):
    for k, ref in enumerate(refs):
        cr, xr, yr = k // 4, (k // 2) % 2, k % 2
        rows, cols = ref.shape[1:]
        for zr in range(4):
            at = dst.at[piece_rows(me, xr, yr, zr, rows), columns(me, cr, cols)]
            pltpu.make_async_copy(ref.at[zr], at, sem).start()


def cut_pieces(me, src, at, ref, to, sem):
    rows = ref.shape[3]
    for xr in range(2):
        for yr in range(2):
            for zr in range(4):
                part = src.at[piece_rows(me, xr, yr, zr, rows), at]
                pltpu.make_async_copy(part, ref.at[xr, yr, zr, :, to], sem).start()


def store_pieces(me, src, keep, send, sem):
    for cr, ref in ((1, send), (0, keep)):
        cols = ref.shape[4]
        cut_pieces(me, src, columns(me, cr, cols), ref, pl.ds(0, cols), sem)


def wait_all(ref, sem):
    pltpu.make_async_copy(ref, ref, sem).wait()


def read_me(me_ref):
    return [me_ref[i] for i in range(4)]


def piece_shape(rows, cols):
    return jax.ShapeDtypeStruct((2, 2, 4, rows // 16, cols // 2), BF)


def attn_fwd_kernel(first, n, load, me_ref, par_ref, x_hbm, qm_hbm, km_hbm, *refs):
    pieces, refs = refs[: len(refs) - 19], refs[len(refs) - 19 :]
    outs, refs = refs[:6], refs[6:]
    x_ref, qm_ref, km_ref, q_ref, k_ref, v_ref, c_ref, lse_ref, w_ref, kx_ref, vx_ref, sem, gsem = refs
    seq, gw = q_ref.shape[1:]
    me = read_me(me_ref)

    def fetch(g):
        load(me, [ref if n == 1 else ref.at[:, g] for ref in pieces], w_ref.at[g], gsem.at[g, 0])

    fetch(0)
    loads = ((x_hbm, x_ref, 0), (qm_hbm, qm_ref, 1), (km_hbm, km_ref, 2))
    for src, dst, i in loads:
        pltpu.make_async_copy(src, dst, sem.at[i]).start()
    for g in range(1, n):
        fetch(g)
    low = lane_iota((seq, 128)) < HD
    for src, dst, i in loads:
        pltpu.make_async_copy(src, dst, sem.at[i]).wait()

    def out_copies(g):
        whole = ((q_ref, 0), (k_ref, 1), (v_ref, 2), (w_ref, 5), (c_ref, 3), (lse_ref, 4))
        return [pltpu.make_async_copy(src.at[g], outs[i].at[g], gsem.at[g, i + 1]) for src, i in whole]

    def group_body(g, carry):
        wait_all(w_ref.at[g], gsem.at[g, 0])
        x = x_ref[...]
        w = w_ref.at[g]
        par = par_ref.at[first + g]
        q = dotf(x, w[:, :gw], 1, 0) + par[0:1, :]
        q_ref[g] = (q * (HD**-0.5)).astype(BF)
        k_ref[g] = dotf(x, w[:, gw : 2 * gw], 1, 0).astype(BF)
        v_ref[g] = (dotf(x, w[:, 2 * gw :], 1, 0) + par[1:2, :]).astype(BF)
        started = out_copies(g)
        for copy in started[:4]:
            copy.start()

        def pair_body(pair, carry):
            sl = pl.ds(mult(pair * 128, 128), 128)
            kp = k_ref[g, :, sl]
            vp = v_ref[g, :, sl]
            qx = jnp.concatenate([q_ref[g, :, sl], qm_ref[...]], axis=1)
            sums, lses = [], []
            for h in range(2):
                sel = low if h == 0 else jnp.logical_not(low)
                kx_ref[h, :, :128] = jnp.where(sel, kp, jnp.zeros_like(kp))
                kx_ref[h, :, 128:] = km_ref[...]
                vx_ref[h] = jnp.where(sel, vp, jnp.ones_like(vp))
            for h in range(2):
                s = dotf(qx, kx_ref[h], 1, 1)
                m = jnp.max(s, axis=1, keepdims=True)
                p = jnp.exp(s - m).astype(BF)
                c = dotf(p, vx_ref[h], 1, 0)
                t = pltpu.roll(c, HD, 1)
                sums.append(c / t)
                lses.append(m + jnp.log(t))
            c_ref[g, :, sl] = jnp.where(low, sums[0], sums[1]).astype(BF)
            lse_ref[g, :, sl] = jnp.where(low, lses[0], lses[1])
            return carry

        lax.fori_loop(0, gw // 128, pair_body, 0)
        for copy in started[4:]:
            copy.start()
        return carry

    lax.fori_loop(0, n, group_body, 0)
    for g in range(n):
        for copy in out_copies(g):
            copy.wait()


def attn_fwd(me, x, par, qm, km, pieces, first, n, load):
    seq, d = x.shape
    gw = d // GROUPS
    b = ((n, seq, gw), BF)
    shapes = [b, b, b, b, ((n, seq, gw), F32), ((n, d, 3 * gw), BF)]
    loaded = [((seq, d), BF), ((seq, 128), BF), ((seq, 128), BF)]
    return pl.pallas_call(
        functools.partial(attn_fwd_kernel, first, n, load),
        in_specs=[SM, VM] + [ANY] * (3 + len(pieces)),
        out_specs=[ANY] * 6,
        out_shape=[pltpu.HBM(*sh) for sh in shapes],
        scratch_shapes=[pltpu.VMEM(*sh) for sh in loaded + shapes]
        + [
            pltpu.VMEM((2, seq, 256), BF),
            pltpu.VMEM((2, seq, 128), BF),
            pltpu.SemaphoreType.DMA((3,)),
            pltpu.SemaphoreType.DMA((n, 7)),
        ],
        compiler_params=pltpu.CompilerParams(vmem_limit_bytes=38 << 20),
        cost_estimate=pl.CostEstimate(flops=n * 10_000_000_000, bytes_accessed=8 << 20, transcendentals=seq * seq * 4),
        name="attn_fwd",
    )(me, par, *in_hbm(x, qm, km), *pieces)


def split3(t):
    hi = t.astype(BF).astype(F32)
    r = t - hi
    mid = r.astype(BF).astype(F32)
    return hi, mid, r - mid


def small_rows(me, db, s1, s2, ub, out_ref):
    d = s1.shape[1]
    dl = d // 8
    rows = [db[0:1], db[1:2], s1[2:3], s2[2:3], s1[0:1], s2[0:1], s1[1:2], s2[1:2]]
    table = jnp.concatenate(rows, axis=0).astype(BF)
    out_ref[...] = jnp.zeros_like(out_ref)

    def pick(n, first):
        j = lax.broadcasted_iota(jnp.int32, (n, 128), 0)
        lane = lane_iota((n, 128))
        return ((j == lane + first) & (lane < dl)).astype(BF)

    ups = [dotf(ub.astype(BF), pick(ub.shape[1], k * dl), 1, 0) for k in range(4)]
    for f in range(8):
        top = dotf(table, pick(d, f * dl), 1, 0)
        both = jnp.concatenate([top] + [u[f : f + 1] for u in ups] + [jnp.zeros((4, 128), F32)], axis=0).astype(BF)
        for xr in range(2):
            out_ref[xr, lax.bitwise_xor(me[1], f % 2), lax.bitwise_xor(me[0], f // 2), 0:16, :] = both


def attn_bwd_kernel(me_ref, s1_ref, s2_ref, ub_ref, *refs):
    first_in, rest_in, dc_in = refs[:5], refs[5:10], refs[10]
    hbm, refs = refs[11:14], refs[14:]
    dm_hbm, keep_ref, send_ref, db_ref, e_ref = refs[:5]
    bufs, refs = refs[5:11], refs[11:]
    qm_ref, km_ref, xt_ref, dm_ref, kx, vx, qx, cx, pt, dst, dw, psem, sem, dsem, wsem = refs
    seq = xt_ref.shape[1]
    gw = dw.shape[2] // 3
    per = gw // 128
    npair = GROUPS * per
    lane = lane_iota((seq, 128))
    low = lane < HD
    columns_of = lambda i: pl.ds(mult(i * 128, 128), 128)

    def pair_copies(i, go):
        slot, g, at = lax.rem(i, 2), lax.div(i, per), columns_of(lax.rem(i, per))

        def move(src, j):
            copy = pltpu.make_async_copy(src, bufs[j].at[slot], psem.at[slot, j])
            copy.start() if go else copy.wait()

        move(dc_in.at[:, columns_of(i)], 5)
        if not go:
            for j in range(5):
                move(first_in[j].at[0, :, at], j)
            return

        @pl.when(g == 0)
        def _():
            for j in range(5):
                move(first_in[j].at[0, :, at], j)

        @pl.when(g > 0)
        def _():
            for j in range(5):
                move(rest_in[j].at[lax.max(g - 1, 0), :, at], j)

    pair_copies(0, True)
    whole = tuple(zip(hbm, (qm_ref, km_ref, xt_ref)))
    for j, (src, dst_) in enumerate(whole):
        pltpu.make_async_copy(src, dst_, sem.at[j]).start()
    for j, (src, dst_) in enumerate(whole):
        pltpu.make_async_copy(src, dst_, sem.at[j]).wait()
    me = read_me(me_ref)

    def pair_body(pair, carry):
        slot = lax.rem(pair, 2)
        pair_copies(pair, False)

        @pl.when(pair + 1 < npair)
        def _():
            pair_copies(pair + 1, True)

        qp, kp, vp, cp, lsep, dcp = (b[slot] for b in bufs)
        prod = dcp.astype(F32) * cp.astype(F32)
        zero = jnp.zeros_like(kp)
        one = jnp.ones_like(kp)
        qm = qm_ref[...].astype(F32)
        qx[:, :128] = qp
        cx[:, :128] = dcp
        for h in range(2):
            sel = low if h == 0 else jnp.logical_not(low)
            lse = jnp.max(jnp.where(sel, lsep, -3e38), axis=1, keepdims=True)
            delta = jnp.sum(jnp.where(sel, prod, 0.0), axis=1, keepdims=True)
            a, b, c = split3(-lse)
            qext = jnp.where(lane == 16, a, jnp.where(lane == 17, b, jnp.where(lane == 18, c, qm)))
            a, b, c = split3(-delta)
            cext = jnp.where(lane == 0, a, jnp.where(lane == 1, b, jnp.where(lane == 2, c, 0.0)))
            kx[h, :, :128] = jnp.where(sel, kp, zero)
            kx[h, :, 128:] = jnp.where((lane >= 16) & (lane < 19), one, km_ref[...])
            vx[h, :, :128] = jnp.where(sel, vp, zero)
            vx[h, :, 128:] = jnp.where(lane < 3, one, zero)
            qx[:, 128:] = qext.astype(BF)
            cx[:, 128:] = cext.astype(BF)
            p = jnp.exp(dotf(kx[h], qx[...], 1, 1))
            dp = dotf(vx[h], cx[...], 1, 1)
            pt[:, h * seq : (h + 1) * seq] = p.astype(BF)
            dst[:, h * seq : (h + 1) * seq] = (p * dp).astype(BF)
        qz = jnp.concatenate([jnp.where(low, qp, zero), jnp.where(low, zero, qp)], axis=0)
        cz = jnp.concatenate([jnp.where(low, dcp, zero), jnp.where(low, zero, dcp)], axis=0)
        dv = dotf(pt[...], cz, 1, 0)
        dk = dotf(dst[...], qz, 1, 0)
        dq = dotf(kx[0, :, :128], dst[:, :seq], 0, 0) + dotf(kx[1, :, :128], dst[:, seq:], 0, 0)
        dq = dq.T * (HD**-0.5)
        db_ref[0:1, columns_of(pair)] = jnp.sum(dq, axis=0, keepdims=True)
        db_ref[1:2, columns_of(pair)] = jnp.sum(dv, axis=0, keepdims=True)
        g, i = lax.div(pair, per), lax.rem(pair, per)
        for j, part in enumerate((dq, dk, dv)):
            at = columns_of(j * per + i)
            dm_ref[g, :, at] = part.astype(BF)
            pltpu.make_async_copy(dm_ref.at[g, :, at], dm_hbm.at[g, :, at], dsem).start()

        @pl.when(i == per - 1)
        def _():
            dw[g] = dotf(xt_ref[...], dm_ref[g], 1, 0).astype(BF)
            store_pieces(me, dw.at[g], keep_ref.at[g], send_ref.at[g], wsem)

        return carry

    lax.fori_loop(0, npair, pair_body, 0)
    small_rows(me, db_ref[...], s1_ref[...], s2_ref[...], ub_ref[...], e_ref)
    wait_all(dm_ref, dsem)
    wait_all(dw, wsem)


def attn_bwd(me, xt, first, rest, dc, qm, km, s1, s2, ub):
    n, seq, gw = rest[0].shape
    d = xt.shape[0]
    ps = pltpu.HBM((GROUPS,) + piece_shape(d, 3 * gw).shape, BF)
    shapes = [((GROUPS, seq, 3 * gw), BF)]
    one = pltpu.VMEM((2, seq, 128), BF)
    return pl.pallas_call(
        attn_bwd_kernel,
        in_specs=[SM] + [VM] * 3 + [ANY] * 14,
        out_specs=[ANY, ANY, ANY] + [VM] * 2,
        out_shape=[
            pltpu.HBM((GROUPS, seq, 3 * gw), BF),
            ps,
            ps,
            jax.ShapeDtypeStruct((2, d), F32),
            jax.ShapeDtypeStruct((2, 2, 4, d // 16, 128), BF),
        ],
        scratch_shapes=[
            one,
            one,
            one,
            one,
            pltpu.VMEM((2, seq, 128), F32),
            one,
            pltpu.VMEM((seq, 128), BF),
            pltpu.VMEM((seq, 128), BF),
            pltpu.VMEM((d, seq), BF),
            pltpu.VMEM((GROUPS, seq, 3 * gw), BF),
            pltpu.VMEM((2, seq, 256), BF),
            pltpu.VMEM((2, seq, 256), BF),
            pltpu.VMEM((seq, 256), BF),
            pltpu.VMEM((seq, 256), BF),
            pltpu.VMEM((seq, 2 * seq), BF),
            pltpu.VMEM((seq, 2 * seq), BF),
            pltpu.VMEM((GROUPS, d, 3 * gw), BF),
            pltpu.SemaphoreType.DMA((2, 6)),
            pltpu.SemaphoreType.DMA((3,)),
            pltpu.SemaphoreType.DMA,
            pltpu.SemaphoreType.DMA,
        ],
        compiler_params=pltpu.CompilerParams(vmem_limit_bytes=52 << 20),
        cost_estimate=pl.CostEstimate(flops=12_000_000_000, bytes_accessed=10 << 20, transcendentals=seq * seq * 12),
        name="attn_bwd",
    )(me, s1, s2, ub, *in_hbm(*first, *rest, dc, qm, km, xt))


def copies(pairs, sem):
    for src, dst in pairs:
        pltpu.make_async_copy(src, dst, sem).start()


def gelu_parts(u):
    u2 = u * u
    k1 = 0.7978845608028654
    k2 = k1 * 0.044715
    h = 0.5 + 0.5 * jnp.tanh(u * (k1 + k2 * u2))
    g = u * h
    return g, h + g * (1.0 - h) * (2 * k1 + (6 * k2) * u2)


def mid_a_kernel(rt, ft, me_ref, par_ref, ub_ref, x_hbm, c0_hbm, c12_hbm, *refs):
    pieces, refs = refs[:2], refs[2:]
    g, gp, y, yb, n1, r1, wo, wu, us, x_ref, c_ref, sem = refs
    me = read_me(me_ref)
    loads = ((c0_hbm, c_ref.at[pl.ds(0, 1)], 2), (c12_hbm, c_ref.at[pl.ds(1, 2)], 3), (x_hbm, x_ref, 4))
    for src, dst, k in loads:
        pltpu.make_async_copy(src, dst, sem.at[k]).start()
    nu, no = wu.shape[1] // 2, wo.shape[1] // 2
    for cr, ref in enumerate(pieces):
        pltpu.make_async_copy(ref.at[:, pl.ds(nu, no)], wo.at[:, columns(me, cr, no)], sem.at[0]).start()
    for cr, ref in enumerate(pieces):
        pltpu.make_async_copy(ref.at[:, pl.ds(0, nu)], wu.at[:, columns(me, cr, nu)], sem.at[1]).start()
    seq, d = x_ref.shape
    ff = wu.shape[1]
    gw = c_ref.shape[2]
    for src, dst, k in loads:
        pltpu.make_async_copy(src, dst, sem.at[k]).wait()
    wait_all(wo, sem.at[0])

    def rows_body(i, carry):
        rows = pl.ds(mult(i * rt, rt), rt)
        a = dotf(c_ref[0, rows, :], wo[:gw], 1, 0)
        a += dotf(c_ref[1, rows, :], wo[gw : 2 * gw], 1, 0)
        a += dotf(c_ref[2, rows, :], wo[2 * gw :], 1, 0)
        h = x_ref[rows, :].astype(F32) + (a + par_ref[2:3, :])
        cen = h - jnp.mean(h, axis=1, keepdims=True)
        r = lax.rsqrt(jnp.mean(cen * cen, axis=1, keepdims=True) + EPS)
        n = cen * r
        yt = n * par_ref[4:5, :] + par_ref[6:7, :]
        n1[rows, :] = n
        r1[rows, :] = jnp.broadcast_to(r, (rt, 128))
        y[rows, :] = yt
        yb[rows, :] = yt.astype(BF)
        return carry

    lax.fori_loop(0, seq // rt, rows_body, 0)
    wait_all(wu, sem.at[1])

    def product(i, slot):
        cs = pl.ds(mult(i * ft, ft), ft)
        us[slot] = dotf(yb[...], wu[:, cs], 1, 0)

    def finish(i, slot):
        cs = pl.ds(mult(i * ft, ft), ft)
        gt, gpt = gelu_parts(us[slot] + ub_ref[:, cs])
        g[:, cs] = gt.astype(BF)
        gp[:, cs] = gpt.astype(BF)

    last = ff // ft - 1
    product(0, 0)

    def cols_body(i, carry):
        product(2 * i + 1, 1)
        finish(2 * i, 0)
        product(lax.min(2 * i + 2, last), 0)
        finish(2 * i + 1, 1)
        return carry

    lax.fori_loop(0, ff // ft // 2, cols_body, 0)


def in_vmem(*arrays):
    return [pltpu.with_memory_space_constraint(a, pltpu.VMEM) for a in arrays]


def in_hbm(*arrays):
    return [pltpu.with_memory_space_constraint(a, pltpu.HBM) for a in arrays]


def mid_a(me, x, cs, par, ub, pieces):
    seq, d = x.shape
    ff = ub.shape[1]
    ft = 512
    shapes = [((seq, ff), BF), ((seq, ff), BF), ((seq, d), F32), ((seq, d), BF), ((seq, d), F32), ((seq, 128), F32)]
    shapes += [((d, d), BF), ((d, ff), BF)]
    return pl.pallas_call(
        functools.partial(mid_a_kernel, 256, ft),
        in_specs=[SM] + [VM] * 2 + [ANY] * 5,
        out_specs=[VM] * 8,
        out_shape=[pltpu.VMEM(*sh) for sh in shapes],
        scratch_shapes=[pltpu.VMEM((2, seq, ft), F32), pltpu.VMEM((seq, d), BF)]
        + [pltpu.VMEM((GROUPS, seq, d // GROUPS), BF), pltpu.SemaphoreType.DMA((5,))],
        compiler_params=pltpu.CompilerParams(vmem_limit_bytes=15 << 20),
        cost_estimate=pl.CostEstimate(
            flops=2 * seq * d * (d + ff), bytes_accessed=20 << 20, transcendentals=seq * ff
        ),
        name="mid_a",
    )(me, par, ub, *in_hbm(x, *cs, *pieces))


def mid_b_kernel(rt, ft, me_ref, len_ref, par_ref, y, g, gp, cot_hbm, *refs):
    wd_p, refs = refs[:8], refs[8:]
    out_hbm, dh2, du, keep_ref, send_ref, sm_ref, ubg_ref, cot, wd, dz, dw, sem, tsem = refs
    me = read_me(me_ref)
    load_pieces(me, wd_p, wd, sem.at[0])
    pltpu.make_async_copy(cot_hbm, cot, sem.at[1]).start()
    seq, d = y.shape
    ff = g.shape[1]
    tiles = seq // rt
    length = len_ref[0]
    sm_ref[...] = jnp.zeros_like(sm_ref)
    wait_all(wd, sem.at[0])
    pltpu.make_async_copy(cot_hbm, cot, sem.at[1]).wait()

    def rows_body(i, carry):
        rows = pl.ds(mult(i * rt, rt), rt)
        z = dotf(g[rows, :], wd[...], 1, 0) + par_ref[3:4, :]
        h = y[rows, :] + z
        cen = h - jnp.mean(h, axis=1, keepdims=True)
        r = lax.rsqrt(jnp.mean(cen * cen, axis=1, keepdims=True) + EPS)
        n = cen * r
        pos = lax.broadcasted_iota(jnp.int32, (rt, 1), 0) + i * rt
        valid = pos < length
        do = jnp.where(valid, cot[rows, :].astype(F32), 0.0)
        res = n * par_ref[5:6, :] + par_ref[7:8, :]
        cot[rows, :] = jnp.where(valid, res, 0.0).astype(BF)
        e = do * par_ref[5:6, :]
        me_ = jnp.mean(e, axis=1, keepdims=True)
        men = jnp.mean(e * n, axis=1, keepdims=True)
        dh = r * (e - me_ - n * men)
        dh2[rows, :] = dh
        dz[rows, :] = dh.astype(BF)
        sm_ref[0:1, :] += jnp.sum(do * n, axis=0, keepdims=True)
        sm_ref[1:2, :] += jnp.sum(do, axis=0, keepdims=True)
        sm_ref[2:3, :] += jnp.sum(dh, axis=0, keepdims=True)
        return carry

    lax.fori_loop(0, tiles, rows_body, 0)
    pltpu.make_async_copy(cot, out_hbm, sem.at[2]).start()
    n = d // 2
    part = ff // 32

    def dw_body(f, carry):
        rows = pl.ds(mult(f * 4 * part, part), 4 * part)
        dw[rows, :] = dotf(g[:, rows], dz[...], 0, 0).astype(BF)
        for cr, ref in ((1, send_ref), (0, keep_ref)):
            for j in range(4):
                at = dw.at[pl.ds(mult((f * 4 + j) * part, part), part), columns(me, cr, n)]
                to = ref.at[pl.ds(mult(f * part, part), part), pl.ds(j * n, n)]
                pltpu.make_async_copy(at, to, sem.at[3]).start()
        return carry

    lax.fori_loop(0, 8, dw_body, 0)

    def du_body(i, carry):
        cs = pl.ds(mult(i * 4 * part, 4 * part), 4 * part)
        dg = dotf(dz[...], wd[cs, :], 1, 1)
        dut = dg * gp[:, cs].astype(F32)
        ubg_ref[pl.ds(i, 1), :] = jnp.sum(dut, axis=0, keepdims=True)
        du[:, cs] = dut.astype(BF)
        return carry

    lax.fori_loop(0, 8, du_body, 0)
    pltpu.make_async_copy(cot, out_hbm, sem.at[2]).wait()
    wait_all(dw, sem.at[3])


def mid_b(me, length, y, cot, par, g, gp, wd_p):
    seq, d = y.shape
    ff = g.shape[1]
    rt = 256
    S = jax.ShapeDtypeStruct
    ps = pltpu.HBM((ff // 4, 2 * d), BF)
    return pl.pallas_call(
        functools.partial(mid_b_kernel, rt, 512),
        in_specs=[SM] * 2 + [VM] * 4 + [ANY] * 9,
        out_specs=[ANY] + [VM] * 2 + [ANY] * 2 + [VM] * 2,
        out_shape=[
            pltpu.HBM((seq, d), BF),
            pltpu.VMEM((seq, d), F32),
            pltpu.VMEM((seq, ff), BF),
            ps,
            ps,
            S((8, d), F32),
            S((8, ff // 8), F32),
        ],
        input_output_aliases={3: 1, 5: 2},
        scratch_shapes=[
            pltpu.VMEM((seq, d), BF),
            pltpu.VMEM((ff, d), BF),
            pltpu.VMEM((seq, d), BF),
            pltpu.VMEM((ff, d), BF),
            pltpu.SemaphoreType.DMA((4,)),
            pltpu.SemaphoreType.DMA((3, seq // rt)),
        ],
        compiler_params=pltpu.CompilerParams(vmem_limit_bytes=17 << 20),
        cost_estimate=pl.CostEstimate(flops=6 * seq * d * ff, bytes_accessed=20 << 20, transcendentals=seq),
        name="mid_b",
    )(me, length, par, *in_vmem(y, g, gp), *in_hbm(cot, *wd_p))


def mid_c_kernel(rt, ft, me_ref, par_ref, n1, r1, dh2, yb, wo, du, wu, *refs):
    c0_h, c12_h = refs[:2]
    dh1_h, dc_h, keep, send, sm_ref = refs[2:7]
    cs_, dwu, dwo, da, dc, dh1, sem = refs[7:]
    me = read_me(me_ref)
    seq, d = n1.shape
    ff = du.shape[1]
    gw = d // 3
    nu, no = ff // 2, d // 2
    steps = nu // ft
    for i in range(GROUPS):
        ref = c0_h.at[0] if i == 0 else c12_h.at[i - 1]
        pltpu.make_async_copy(ref, cs_.at[:, i * gw : (i + 1) * gw], sem.at[0]).start()
    sm_ref[...] = jnp.zeros_like(sm_ref)
    for cr, ref in ((1, send), (0, keep)):

        def dwu_body(j, carry):
            at = pl.ds(mult(lax.bitwise_xor(me[3], cr) * nu + j * ft, ft), ft)
            dwu[:, at] = dotf(yb[...], du[:, at], 0, 0).astype(BF)
            cut_pieces(me, dwu, at, ref, pl.ds(mult(j * ft, ft), ft), sem.at[1])
            return carry

        lax.fori_loop(0, steps, dwu_body, 0)

    def rows_body(i, carry):
        rows = pl.ds(mult(i * rt, rt), rt)
        dy = dh2[rows, :] + dotf(du[rows, :], wu[...], 1, 1)
        n = n1[rows, :]
        e = dy * par_ref[4:5, :]
        me_ = jnp.mean(e, axis=1, keepdims=True)
        men = jnp.mean(e * n, axis=1, keepdims=True)
        dh = r1[rows, 0:1] * (e - me_ - n * men)
        dh1[rows, :] = dh
        dat = dh.astype(BF)
        da[rows, :] = dat
        sm_ref[0:1, :] += jnp.sum(dy * n, axis=0, keepdims=True)
        sm_ref[1:2, :] += jnp.sum(dy, axis=0, keepdims=True)
        sm_ref[2:3, :] += jnp.sum(dh, axis=0, keepdims=True)
        dc[rows, :] = dotf(dat, wo[...], 1, 1).astype(BF)
        return carry

    lax.fori_loop(0, seq // rt, rows_body, 0)
    pltpu.make_async_copy(dh1, dh1_h, sem.at[2]).start()
    pltpu.make_async_copy(dc, dc_h, sem.at[3]).start()
    wait_all(cs_, sem.at[0])
    for cr, ref in ((1, send), (0, keep)):
        at = columns(me, cr, no)
        dwo[:, at] = dotf(cs_[...], da[:, at], 0, 0).astype(BF)
        cut_pieces(me, dwo, at, ref, pl.ds(nu, no), sem.at[4])
    pltpu.make_async_copy(dh1, dh1_h, sem.at[2]).wait()
    wait_all(dc, sem.at[3])
    wait_all(dwu, sem.at[1])
    wait_all(dwo, sem.at[4])


def mid_c(me, n1, r1, dh2, yb, cs, par, wo, du, wu):
    seq, d = n1.shape
    ff = du.shape[1]
    S = jax.ShapeDtypeStruct
    ps = pltpu.HBM(piece_shape(d, ff + d).shape, BF)
    dc = pltpu.HBM((seq, d), BF)
    ft = 512
    return pl.pallas_call(
        functools.partial(mid_c_kernel, 256, ft),
        in_specs=[SM] + [VM] * 8 + [ANY] * 2,
        out_specs=[ANY] * 4 + [VM],
        out_shape=[pltpu.HBM((seq, d), F32), dc, ps, ps, S((8, d), F32)],
        scratch_shapes=[
            pltpu.VMEM((seq, d), BF),
            pltpu.VMEM((d, ff), BF),
            pltpu.VMEM((d, d), BF),
            pltpu.VMEM((seq, d), BF),
            pltpu.VMEM((seq, d), BF),
            pltpu.VMEM((seq, d), F32),
            pltpu.SemaphoreType.DMA((5,)),
        ],
        compiler_params=pltpu.CompilerParams(vmem_limit_bytes=18 << 20),
        cost_estimate=pl.CostEstimate(flops=4 * seq * d * (ff + d), bytes_accessed=20 << 20, transcendentals=seq),
        name="mid_c",
    )(me, par, *in_vmem(n1, r1, dh2, yb, wo, du, wu), *in_hbm(*cs))


def input_grad_kernel(dh1_ref, m_ref, w0, w12, out_ref):
    acc = dh1_ref[...]
    for g in range(GROUPS):
        acc += dotf(m_ref[g], w0[0] if g == 0 else w12[g - 1], 1, 1)
    out_ref[...] = acc


def input_grad(dh1, dm, w0, w12):
    seq, d = dh1.shape
    n = dm.shape[2]
    rt = 256
    row = pl.BlockSpec((rt, d), lambda i: (i, 0))
    full = lambda k: pl.BlockSpec((k, d, n), lambda i: (0, 0, 0))
    return pl.pallas_call(
        input_grad_kernel,
        grid=(seq // rt,),
        in_specs=[row, pl.BlockSpec((GROUPS, rt, n), lambda i: (0, i, 0)), full(1), full(GROUPS - 1)],
        out_specs=row,
        out_shape=jax.ShapeDtypeStruct((seq, d), F32),
        compiler_params=pltpu.CompilerParams(vmem_limit_bytes=60 << 20),
        cost_estimate=pl.CostEstimate(flops=6 * seq * d * n, bytes_accessed=15 << 20, transcendentals=0),
        name="input_grad",
    )(dh1, dm, w0, w12)


def sum_kernel(*refs):
    out = refs[-1]
    first = 0
    for a, b in zip(refs[0:-1:2], refs[1:-1:2]):
        w = a.shape[1]
        out[:, first : first + w] = (a[...].astype(F32) + b[...].astype(F32)).astype(BF)
        first += w


def summed(*pairs):
    rows = pairs[0][0].shape[0]
    rt = rows // 8
    width = sum(a.shape[1] for a, _ in pairs)
    one = lambda w: pl.BlockSpec((rt, w), lambda i: (i, 0))
    arrays = [a for pair in pairs for a in pair]
    return pl.pallas_call(
        sum_kernel,
        grid=(8,),
        in_specs=[one(a.shape[1]) for a in arrays],
        out_specs=one(width),
        out_shape=pltpu.HBM((rows, width), BF),
        compiler_params=pltpu.CompilerParams(vmem_limit_bytes=6 << 20),
        cost_estimate=pl.CostEstimate(flops=rows * width, bytes_accessed=6 * rows * width, transcendentals=0),
        name="summed",
    )(*in_hbm(*arrays))


def load_parts(parts, arrays, at, buf, sem):
    first = 0
    for array, group, w in parts:
        ref = arrays[array] if group is None else arrays[array].at[group]
        pltpu.make_async_copy(ref.at[at], buf.at[..., pl.ds(first, w)], sem).start()
        first += w


PLANE = ((0, 0), (0, 1), (1, 0), (1, 1))


def plane_kernel(parts, n, *refs):
    both, outs, (buf, sem) = (refs[:n], refs[n : 2 * n]), refs[2 * n : 2 * n + 4], refs[2 * n + 4 :]
    for j, at in enumerate(PLANE):
        for i, arrays in enumerate(both):
            load_parts(parts, arrays, at, buf.at[j, i], sem.at[j, i])
    for j in (1, 2, 3, 0):
        for i in range(2):
            wait_all(buf.at[j, i], sem.at[j, i])
        outs[j][...] = (buf[j, 0].astype(F32) + buf[j, 1].astype(F32)).astype(outs[j].dtype)


def line_kernel(stay, y, x, xy, *outs):
    for z, out in enumerate(outs):
        total = stay[z] + y[z].astype(F32) + x[z].astype(F32) + xy[z].astype(F32)
        out[...] = total.astype(out.dtype)


def plane_sums(parts, keeps, recvs):
    rows = keeps[0].shape[-2]
    width = sum(w for _, _, w in parts)
    shape = (4, rows, width)
    n = len(keeps)
    nbytes = 16 * rows * width * 10
    return pl.pallas_call(
        functools.partial(plane_kernel, parts, n),
        in_specs=[ANY] * (2 * n),
        out_specs=[VM] * 4,
        out_shape=[jax.ShapeDtypeStruct(shape, F32)] + [jax.ShapeDtypeStruct(shape, BF)] * 3,
        scratch_shapes=[pltpu.VMEM((4, 2) + shape, BF), pltpu.SemaphoreType.DMA((4, 2))],
        compiler_params=pltpu.CompilerParams(vmem_limit_bytes=12 << 20),
        cost_estimate=pl.CostEstimate(flops=nbytes, bytes_accessed=nbytes, transcendentals=0),
        name="plane_sums",
    )(*keeps, *recvs)


def line_sums(stay, y, x, xy):
    shape = stay.shape[1:]
    nbytes = 4 * stay.size * 4
    return pl.pallas_call(
        line_kernel,
        in_specs=[VM] * 4,
        out_specs=[VM] * 4,
        out_shape=[jax.ShapeDtypeStruct(shape, F32)] + [jax.ShapeDtypeStruct(shape, BF)] * 3,
        compiler_params=pltpu.CompilerParams(vmem_limit_bytes=8 << 20),
        cost_estimate=pl.CostEstimate(flops=nbytes, bytes_accessed=nbytes, transcendentals=0),
        name="line_sums",
    )(stay, y, x, xy)


def after(value, *others):
    return lax.optimization_barrier((value, *others))[0]


def added(*parts):
    return sum(p.astype(F32) for p in parts)


def flipped(array, bits, axes):
    for bit, axis in zip(bits, axes):
        array = jnp.where(bit == 1, jnp.flip(array, axis), array)
    return array


class Links:
    def __init__(self, mesh):
        r, f = mesh.shape["replica"], mesh.shape["fsdp"]
        self.direct = (r, f) == (4, 8)
        if self.direct:
            fi, ri = lax.axis_index("fsdp"), lax.axis_index("replica")
            self.me = jnp.stack([fi // 2, fi % 2, ri // 2, ri % 2]).astype(jnp.int32)
        else:
            self.me = jnp.zeros((4,), jnp.int32)

    def core(self, a):
        return lax.ppermute(a, "replica", [(i, i ^ 1) for i in range(4)])

    def x(self, a):
        return lax.ppermute(a, "replica", [(i, i ^ 2) for i in range(4)])

    def y(self, a):
        return lax.ppermute(a, "fsdp", [(i, i ^ 1) for i in range(8)])

    def z(self, a, d):
        return lax.ppermute(a, "fsdp", [(i, i ^ (2 * d)) for i in range(8)])

    def xy(self, a):
        both = ("replica", "fsdp")
        return lax.ppermute(a, both, [(i, i ^ 17) for i in range(32)])

    def to_plane(self, a):
        return [self.y(a), self.x(a), self.xy(a)]

    def to_z(self, own):
        return [self.z(own, d) for d in (1, 2, 3)]

    def across(self, sends):
        y, x, xy = sends
        return [self.y(y), self.x(x), self.xy(xy)]

    def down_z(self, sends):
        return [self.z(t, i + 1) for i, t in enumerate(sends)]

    def half(self, shard):
        n = shard.shape[-1] // 2
        return lax.dynamic_slice_in_dim(shard, self.me[3] * n, n, shard.ndim - 1)

    def quarter(self, shard):
        r = shard.shape[0] // 2
        return lax.dynamic_slice_in_dim(self.half(shard), self.me[2] * r, r, 0)

    def bits(self):
        z, y, x, c = (self.me[i] for i in range(4))
        return z // 2, z % 2, y, x, c

    def wide(self, own, other):
        c0 = self.me[3] == 0
        return jnp.concatenate([jnp.where(c0, own, other), jnp.where(c0, other, own)], axis=1)


def masks(length, chosen, seq):
    nb = chosen.shape[0]
    used = (length + BLK - 1) // BLK
    lane = jnp.arange(128, dtype=jnp.int32)[None, :]
    pos = jnp.arange(seq, dtype=jnp.int32)[:, None]
    kb = pos // BLK
    onehot = (kb == lane).astype(BF)
    picks = jnp.pad(chosen, ((0, 128 - nb), (0, 0)), constant_values=-1)
    allowed = (jnp.abs(lane - kb) <= 1) | (kb == 0) | (kb == used - 1) | (lane == 0) | (lane == used - 1)
    for i in range(chosen.shape[1]):
        allowed |= picks[:, i][None, :] == kb
    bias = jnp.where(allowed & (pos < length), 0.0, -1e9)
    return onehot, jnp.where(lane < nb, bias, 0.0).astype(BF)


def shards(mesh, tokens, lengths, random_blocks, qkv_weight, out_weight, up_weight, down_weight, proj_bias,
           up_bias, norm_gain, norm_bias, cotangent):
    links = Links(mesh)
    me = links.me
    direct = links.direct
    seq, d = tokens.shape
    gw = d // GROUPS
    hw = 3 * gw // 2
    f_size = mesh.shape["fsdp"]
    dl = proj_bias.shape[1]
    ul = up_bias.shape[0]
    n_up = ul // dl
    ff = ul * f_size
    nu, no = ff // 2, d // 2
    small = jnp.concatenate([proj_bias, norm_gain, norm_bias, up_bias.reshape(n_up, dl)], axis=0)

    groups = []
    for g in range(GROUPS):
        cut = [qkv_weight[:, j * d + g * gw : j * d + (g + 1) * gw] for j in range(3)]
        groups.append(jnp.concatenate(cut, axis=1))
    if direct:
        own0 = jnp.concatenate([links.half(groups[0]), jnp.pad(small.reshape(-1, hw), ((0, 8 - small.size // hw), (0, 0)))])
        own_m = jnp.concatenate([links.half(up_weight), links.half(out_weight)], axis=1)
        m_own = lax.all_gather(own_m, "fsdp", axis=0, tiled=True)
        own0 = after(own0, own_m)
        rows = groups[0].shape[0] // 2
        own12 = lax.dynamic_slice_in_dim(links.half(jnp.stack(groups[1:])), me[2] * rows, rows, 1)
        own12 = after(own12, own0)
        own_d = links.quarter(down_weight)
        z0 = links.to_z(own0)
        z12 = links.to_z(own12)
        b0 = jnp.stack([own0] + z0)
        by0 = links.y(b0)
        q0 = [b0, by0, links.core(b0), links.core(by0)]
        small = jnp.stack([b0[:, -8:], by0[:, -8:]], axis=1)
        small = small.reshape(2, 2, 2, -1)[..., : (8 + n_up) * dl]
        small = flipped(small, links.bits()[:3], (0, 1, 2)).reshape(f_size, 8 + n_up, dl)
    else:
        small = lax.all_gather(small, "fsdp", axis=0)
        every = [lax.all_gather(w, "fsdp", axis=0, tiled=True) for w in groups]
        q0 = every[0].reshape(4, 2, d // 8, 2, hw)
        q0 = [q0[:, y, :, c] for c in range(2) for y in range(2)]
        q12 = jnp.stack([w.reshape(4, 2, 2, d // 16, 2, hw) for w in every[1:]], axis=1)
        q12 = [q12[:, :, y, x, :, c] for c in range(2) for x in range(2) for y in range(2)]
        up_all = lax.all_gather(up_weight, "fsdp", axis=0, tiled=True)
        out_all = lax.all_gather(out_weight, "fsdp", axis=0, tiled=True)
        m_parts = [
            jnp.concatenate([up_all[:, c * nu : (c + 1) * nu], out_all[:, c * no : (c + 1) * no]], axis=1)
            for c in range(2)
        ]
        every = lax.all_gather(down_weight, "fsdp", axis=0, tiled=True).reshape(4, 2, 2, ff // 16, 2, d // 2)
        d_parts = [every[:, y, x, :, c] for c in range(2) for x in range(2) for y in range(2)]

    ub = small[:, 8:].reshape(1, ff).astype(F32)
    par = small[:, :8].transpose(1, 0, 2).reshape(8, d).astype(F32)
    onehot, bias = masks(lengths[0], random_blocks[0], seq)
    xt = tokens.T

    par3 = jnp.stack([par[:2, g * gw : (g + 1) * gw] for g in range(GROUPS)])
    one_rows = lambda m, refs, dst, sem: load_rows(m, [(ref, d // 8) for ref in refs], dst, sem)

    if direct:
        b12 = jnp.stack([own12] + z12)
        plane = links.to_plane(b12)
        f0 = attn_fwd(me, after(tokens, xt, b12), par3, onehot, bias, q0, 0, 1, one_rows)
        own_d, *plane = after((own_d, *plane), f0[3])
        z_d = links.to_z(own_d)
        near = [b12] + plane
        q12 = near + [links.core(a) for a in near]
        f12 = attn_fwd(me, tokens, par3, onehot, bias, q12, 1, 2, load_pieces)
        m_own, *z_d = after((m_own, *z_d), f12[3])
        b_d = jnp.stack([own_d] + z_d)
        plane = links.to_plane(b_d)
        core_b = links.core(b_d)
        m_parts = [m_own, after(links.core(m_own), b_d)]
    else:
        f0 = attn_fwd(me, tokens, par3, onehot, bias, q0, 0, 1, one_rows)
        f12 = attn_fwd(me, tokens, par3, onehot, bias, q12, 1, 2, load_pieces)
    cs = [f0[3], f12[3]]
    gact, gp, y, yb, n1, r1, wo, wu = mid_a(me, tokens, cs, par, ub, m_parts)
    if direct:
        *plane, core_b = after((*plane, core_b), y)
        d_parts = [b_d] + plane + [core_b] + [links.core(a) for a in plane]
    result, dh2, du, dkeep, dsend, sm2, ubg = mid_b(me, lengths, y, cotangent, par, gact, gp, d_parts)
    dh1, dc, mkeep, msend, sm1 = mid_c(me, n1, r1, dh2, yb, cs, par, wo, du, wu)

    def backward(dc):
        return attn_bwd(me, xt, f0[:5], f12[:5], dc, onehot, bias, sm1, sm2, ubg)

    if direct:
        drecv = after(links.core(dsend), dc)
        mrecv = links.core(msend)
        total = summed((dkeep, drecv))
        part = lax.psum_scatter(total, "fsdp", scatter_dimension=0, tiled=True)
        mrecv = after(mrecv, total)
        m_stay, *m_sends = plane_sums(((0, None, mkeep.shape[-1]),), [mkeep], [mrecv])
        m_plane = links.across(m_sends)
        dm, keep, send, db, e = backward(after(dc, *m_sends))
        keep, send, e, m_plane = after((keep, send, e, m_plane), db)
        q_parts = tuple((0, g, hw) for g in range(GROUPS)) + ((1, None, 128),)
        q_stay, *q_sends = plane_sums(q_parts, [keep, e], [links.core(send), links.core(e)])
        q_plane = links.across(q_sends)
        m_base, *m_line = line_sums(m_stay, *m_plane)
        m_last = links.down_z(m_line)
        grad_in = input_grad(after(dh1, *q_sends, *m_line), dm, f0[5], f12[5])
        part, *q_plane = after((part, *q_plane), grad_in)
        part_x = links.x(part)
        q_base, *q_line = line_sums(q_stay, *q_plane)
        q_last = links.down_z(q_line)
        m_last = after(tuple(m_last), q_base)
        part, part_x = after((part, part_x), q_base)
        part = added(part, part_x).astype(BF)
        part_c = links.core(part)
        down = [p.reshape(-1, 4, no).transpose(1, 0, 2).reshape(-1, no) for p in (part, part_c)]
        down_grad = links.wide(*down).astype(F32)
        fin = jnp.concatenate([added(q_base, *q_last), added(m_base, *m_last)], axis=1).astype(BF)
        fx = links.x(fin)
        fc, fxc = links.core(fin), links.core(fx)
        quarters = (fin, fc, fx, fxc)
        x0, c0 = me[2] == 0, me[3] == 0

        def whole(first, w):
            cut = [q[:, first : first + w] for q in quarters]
            m, t = links.wide(*cut[:2]), links.wide(*cut[2:])
            return jnp.concatenate([jnp.where(x0, m, t), jnp.where(x0, t, m)], axis=0).astype(F32)

        qkv_cols = [whole(g * hw, hw) for g in range(GROUPS)]
        first = GROUPS * hw + 128
        up_grad, out_grad = whole(first, nu), whole(first + nu, no)
        cut = [q[: 8 + n_up, GROUPS * hw : GROUPS * hw + dl] for q in quarters]
        own = jnp.where(x0, jnp.where(c0, cut[0], cut[1]), jnp.where(c0, cut[2], cut[3])).astype(F32)
    else:

        def total(full):
            part = lax.psum_scatter(full.astype(F32), "fsdp", scatter_dimension=0, tiled=True)
            return lax.psum(part.astype(BF), "replica").astype(F32)

        def pieces_total(keep, send):
            full = jnp.stack([keep, send])
            c, x, y_, z, r, n = full.shape
            return total(full.transpose(3, 2, 1, 4, 0, 5).reshape(z * y_ * x * r, c * n))

        dm, keep, send, db, _ = backward(dc)
        grad_in = input_grad(dh1, dm, f0[5], f12[5])
        downs = jnp.stack([p.reshape(8, -1, 4, no).transpose(0, 2, 1, 3).reshape(ff, no) for p in (dkeep, dsend)], axis=1)
        down_grad = total(downs.reshape(ff, d))
        both_g = pieces_total(mkeep, msend)
        both_g = both_g.reshape(both_g.shape[0], 2, nu + no)
        up_grad = both_g[:, :, :nu].reshape(-1, ff)
        out_grad = both_g[:, :, nu:].reshape(-1, d)
        qkv_cols = [pieces_total(keep[g], send[g]) for g in range(GROUPS)]
        rows = jnp.stack([db[0], db[1], sm1[2], sm2[2], sm1[0], sm2[0], sm1[1], sm2[1]])
        rows = rows.reshape(8, f_size, dl).transpose(1, 0, 2)
        every = jnp.concatenate([rows, ubg.reshape(f_size, n_up, dl)], axis=1)
        every = lax.psum(every, ("replica", "fsdp"))
        own = lax.dynamic_index_in_dim(every, lax.axis_index("fsdp"), 0, keepdims=False)
    qkv_grad = jnp.concatenate(
        [qkv_cols[g][:, j * gw : (j + 1) * gw] for j in range(3) for g in range(GROUPS)], axis=1
    )
    return (
        result,
        grad_in,
        qkv_grad,
        out_grad,
        up_grad,
        down_grad,
        own[:4],
        own[8:].reshape(ul),
        own[4:6],
        own[6:8],
    )


def solution(mesh):
    both = ("replica", "fsdp")
    return jax.shard_map(
        functools.partial(shards, mesh),
        mesh=mesh,
        in_specs=(
            P(both, None),
            P(both),
            P(both, None, None),
            P("fsdp", None),
            P("fsdp", None),
            P("fsdp", None),
            P("fsdp", None),
            P(None, "fsdp"),
            P("fsdp"),
            P(None, "fsdp"),
            P(None, "fsdp"),
            P(both, None),
        ),
        out_specs=(
            P(both, None),
            P(both, None),
            P("fsdp", None),
            P("fsdp", None),
            P("fsdp", None),
            P("fsdp", None),
            P(None, "fsdp"),
            P("fsdp"),
            P(None, "fsdp"),
            P(None, "fsdp"),
        ),
        check_vma=False,
    )
```

```python
import functools

import jax
import jax.numpy as jnp
from jax import lax
from jax.experimental import pallas as pl
from jax.experimental.pallas import tpu as pltpu
from jax.sharding import PartitionSpec as P

D = 768
HD = 64
BLK = 64
GROUPS = 3
EPS = 1e-06
BF = jnp.bfloat16
F32 = jnp.float32
ANY = pl.BlockSpec(memory_space=pl.ANY)
VM = pl.BlockSpec(memory_space=pltpu.VMEM)
SM = pl.BlockSpec(memory_space=pltpu.SMEM)


def dotf(a, b, ca, cb):
    return lax.dot_general(a, b, (((ca,), (cb,)), ((), ())), preferred_element_type=F32)


def lane_iota(shape):
    return lax.broadcasted_iota(jnp.int32, shape, 1)


def mult(v, m):
    return pl.multiple_of(v, m)


def columns(me, cr, cols):
    return pl.ds(mult(lax.bitwise_xor(me[3], cr) * cols, cols), cols)


def load_rows(me, refs, dst, sem):
    for k, (ref, rows) in enumerate(refs):
        cols = ref.shape[-1]
        for zr in range(4):
            f = lax.bitwise_xor(me[0], zr) * 2 + lax.bitwise_xor(me[1], k % 2)
            at = dst.at[pl.ds(mult(f * rows, rows), rows), columns(me, k // 2, cols)]
            pltpu.make_async_copy(ref.at[zr, pl.ds(0, rows)], at, sem).start()


def piece_rows(me, xr, yr, zr, rows):
    z = lax.bitwise_xor(me[0], zr)
    y = lax.bitwise_xor(me[1], yr)
    x = lax.bitwise_xor(me[2], xr)
    return pl.ds(mult(((z * 2 + y) * 2 + x) * rows, rows), rows)


def load_pieces(me, refs, dst, sem):
    for k, ref in enumerate(refs):
        cr, xr, yr = k // 4, (k // 2) % 2, k % 2
        rows, cols = ref.shape[1:]
        for zr in range(4):
            at = dst.at[piece_rows(me, xr, yr, zr, rows), columns(me, cr, cols)]
            pltpu.make_async_copy(ref.at[zr], at, sem).start()


def cut_pieces(me, src, at, ref, to, sem):
    rows = ref.shape[3]
    for xr in range(2):
        for yr in range(2):
            for zr in range(4):
                part = src.at[piece_rows(me, xr, yr, zr, rows), at]
                pltpu.make_async_copy(part, ref.at[xr, yr, zr, :, to], sem).start()


def store_pieces(me, src, keep, send, sem):
    for cr, ref in ((1, send), (0, keep)):
        cols = ref.shape[4]
        cut_pieces(me, src, columns(me, cr, cols), ref, pl.ds(0, cols), sem)


def wait_all(ref, sem):
    pltpu.make_async_copy(ref, ref, sem).wait()


def read_me(me_ref):
    return [me_ref[i] for i in range(4)]


def piece_shape(rows, cols):
    return jax.ShapeDtypeStruct((2, 2, 4, rows // 16, cols // 2), BF)


def attn_fwd_kernel(first, n, load, me_ref, par_ref, x_hbm, qm_hbm, km_hbm, *refs):
    pieces, refs = refs[: len(refs) - 19], refs[len(refs) - 19 :]
    outs, refs = refs[:6], refs[6:]
    x_ref, qm_ref, km_ref, q_ref, k_ref, v_ref, c_ref, lse_ref, w_ref, kx_ref, vx_ref, sem, gsem = refs
    seq, gw = q_ref.shape[1:]
    me = read_me(me_ref)

    def fetch(g):
        load(me, [ref if n == 1 else ref.at[:, g] for ref in pieces], w_ref.at[g], gsem.at[g, 0])

    fetch(0)
    loads = ((x_hbm, x_ref, 0), (qm_hbm, qm_ref, 1), (km_hbm, km_ref, 2))
    for src, dst, i in loads:
        pltpu.make_async_copy(src, dst, sem.at[i]).start()
    for g in range(1, n):
        fetch(g)
    low = lane_iota((seq, 128)) < HD
    for src, dst, i in loads:
        pltpu.make_async_copy(src, dst, sem.at[i]).wait()

    def out_copies(g):
        whole = ((q_ref, 0), (k_ref, 1), (v_ref, 2), (w_ref, 5), (c_ref, 3), (lse_ref, 4))
        return [pltpu.make_async_copy(src.at[g], outs[i].at[g], gsem.at[g, i + 1]) for src, i in whole]

    def group_body(g, carry):
        wait_all(w_ref.at[g], gsem.at[g, 0])
        x = x_ref[...]
        w = w_ref.at[g]
        par = par_ref.at[first + g]
        q = dotf(x, w[:, :gw], 1, 0) + par[0:1, :]
        q_ref[g] = (q * (HD**-0.5)).astype(BF)
        k_ref[g] = dotf(x, w[:, gw : 2 * gw], 1, 0).astype(BF)
        v_ref[g] = (dotf(x, w[:, 2 * gw :], 1, 0) + par[1:2, :]).astype(BF)
        started = out_copies(g)
        for copy in started[:4]:
            copy.start()

        def pair_body(pair, carry):
            sl = pl.ds(mult(pair * 128, 128), 128)
            kp = k_ref[g, :, sl]
            vp = v_ref[g, :, sl]
            qx = jnp.concatenate([q_ref[g, :, sl], qm_ref[...]], axis=1)
            sums, lses = [], []
            for h in range(2):
                sel = low if h == 0 else jnp.logical_not(low)
                kx_ref[h, :, :128] = jnp.where(sel, kp, jnp.zeros_like(kp))
                kx_ref[h, :, 128:] = km_ref[...]
                vx_ref[h] = jnp.where(sel, vp, jnp.ones_like(vp))
            for h in range(2):
                s = dotf(qx, kx_ref[h], 1, 1)
                m = jnp.max(s, axis=1, keepdims=True)
                p = jnp.exp(s - m).astype(BF)
                c = dotf(p, vx_ref[h], 1, 0)
                t = pltpu.roll(c, HD, 1)
                sums.append(c / t)
                lses.append(m + jnp.log(t))
            c_ref[g, :, sl] = jnp.where(low, sums[0], sums[1]).astype(BF)
            lse_ref[g, :, sl] = jnp.where(low, lses[0], lses[1])
            return carry

        lax.fori_loop(0, gw // 128, pair_body, 0)
        for copy in started[4:]:
            copy.start()
        return carry

    lax.fori_loop(0, n, group_body, 0)
    for g in range(n):
        for copy in out_copies(g):
            copy.wait()


def attn_fwd(me, x, par, qm, km, pieces, first, n, load):
    seq, d = x.shape
    gw = d // GROUPS
    b = ((n, seq, gw), BF)
    shapes = [b, b, b, b, ((n, seq, gw), F32), ((n, d, 3 * gw), BF)]
    loaded = [((seq, d), BF), ((seq, 128), BF), ((seq, 128), BF)]
    return pl.pallas_call(
        functools.partial(attn_fwd_kernel, first, n, load),
        in_specs=[SM, VM] + [ANY] * (3 + len(pieces)),
        out_specs=[ANY] * 6,
        out_shape=[pltpu.HBM(*sh) for sh in shapes],
        scratch_shapes=[pltpu.VMEM(*sh) for sh in loaded + shapes]
        + [
            pltpu.VMEM((2, seq, 256), BF),
            pltpu.VMEM((2, seq, 128), BF),
            pltpu.SemaphoreType.DMA((3,)),
            pltpu.SemaphoreType.DMA((n, 7)),
        ],
        compiler_params=pltpu.CompilerParams(vmem_limit_bytes=38 << 20),
        cost_estimate=pl.CostEstimate(flops=n * 10_000_000_000, bytes_accessed=8 << 20, transcendentals=seq * seq * 4),
        name="attn_fwd",
    )(me, par, *in_hbm(x, qm, km), *pieces)


def split3(t):
    hi = t.astype(BF).astype(F32)
    r = t - hi
    mid = r.astype(BF).astype(F32)
    return hi, mid, r - mid


def small_rows(me, db, s1, s2, ub, out_ref):
    d = s1.shape[1]
    dl = d // 8
    rows = [db[0:1], db[1:2], s1[2:3], s2[2:3], s1[0:1], s2[0:1], s1[1:2], s2[1:2]]
    table = jnp.concatenate(rows, axis=0).astype(BF)
    out_ref[...] = jnp.zeros_like(out_ref)

    def pick(n, first):
        j = lax.broadcasted_iota(jnp.int32, (n, 128), 0)
        lane = lane_iota((n, 128))
        return ((j == lane + first) & (lane < dl)).astype(BF)

    ups = [dotf(ub.astype(BF), pick(ub.shape[1], k * dl), 1, 0) for k in range(4)]
    for f in range(8):
        top = dotf(table, pick(d, f * dl), 1, 0)
        both = jnp.concatenate([top] + [u[f : f + 1] for u in ups] + [jnp.zeros((4, 128), F32)], axis=0).astype(BF)
        for xr in range(2):
            out_ref[xr, lax.bitwise_xor(me[1], f % 2), lax.bitwise_xor(me[0], f // 2), 0:16, :] = both


def attn_bwd_kernel(me_ref, s1_ref, s2_ref, ub_ref, *refs):
    first_in, rest_in, dc_in = refs[:5], refs[5:10], refs[10]
    hbm, refs = refs[11:14], refs[14:]
    dm_hbm, keep_ref, send_ref, db_ref, e_ref = refs[:5]
    bufs, refs = refs[5:11], refs[11:]
    qm_ref, km_ref, xt_ref, dm_ref, kx, vx, qx, cx, pt, dst, dw, psem, sem, dsem, wsem = refs
    seq = xt_ref.shape[1]
    gw = dw.shape[2] // 3
    per = gw // 128
    npair = GROUPS * per
    lane = lane_iota((seq, 128))
    low = lane < HD
    columns_of = lambda i: pl.ds(mult(i * 128, 128), 128)

    def pair_copies(i, go):
        slot, g, at = lax.rem(i, 2), lax.div(i, per), columns_of(lax.rem(i, per))

        def move(src, j):
            copy = pltpu.make_async_copy(src, bufs[j].at[slot], psem.at[slot, j])
            copy.start() if go else copy.wait()

        move(dc_in.at[:, columns_of(i)], 5)
        if not go:
            for j in range(5):
                move(first_in[j].at[0, :, at], j)
            return

        @pl.when(g == 0)
        def _():
            for j in range(5):
                move(first_in[j].at[0, :, at], j)

        @pl.when(g > 0)
        def _():
            for j in range(5):
                move(rest_in[j].at[lax.max(g - 1, 0), :, at], j)

    pair_copies(0, True)
    whole = tuple(zip(hbm, (qm_ref, km_ref, xt_ref)))
    for j, (src, dst_) in enumerate(whole):
        pltpu.make_async_copy(src, dst_, sem.at[j]).start()
    for j, (src, dst_) in enumerate(whole):
        pltpu.make_async_copy(src, dst_, sem.at[j]).wait()
    me = read_me(me_ref)

    def pair_body(pair, carry):
        slot = lax.rem(pair, 2)
        pair_copies(pair, False)

        @pl.when(pair + 1 < npair)
        def _():
            pair_copies(pair + 1, True)

        qp, kp, vp, cp, lsep, dcp = (b[slot] for b in bufs)
        prod = dcp.astype(F32) * cp.astype(F32)
        zero = jnp.zeros_like(kp)
        one = jnp.ones_like(kp)
        qm = qm_ref[...].astype(F32)
        qx[:, :128] = qp
        cx[:, :128] = dcp
        for h in range(2):
            sel = low if h == 0 else jnp.logical_not(low)
            lse = jnp.max(jnp.where(sel, lsep, -3e38), axis=1, keepdims=True)
            delta = jnp.sum(jnp.where(sel, prod, 0.0), axis=1, keepdims=True)
            a, b, c = split3(-lse)
            qext = jnp.where(lane == 16, a, jnp.where(lane == 17, b, jnp.where(lane == 18, c, qm)))
            a, b, c = split3(-delta)
            cext = jnp.where(lane == 0, a, jnp.where(lane == 1, b, jnp.where(lane == 2, c, 0.0)))
            kx[h, :, :128] = jnp.where(sel, kp, zero)
            kx[h, :, 128:] = jnp.where((lane >= 16) & (lane < 19), one, km_ref[...])
            vx[h, :, :128] = jnp.where(sel, vp, zero)
            vx[h, :, 128:] = jnp.where(lane < 3, one, zero)
            qx[:, 128:] = qext.astype(BF)
            cx[:, 128:] = cext.astype(BF)
            p = jnp.exp(dotf(kx[h], qx[...], 1, 1))
            dp = dotf(vx[h], cx[...], 1, 1)
            pt[:, h * seq : (h + 1) * seq] = p.astype(BF)
            dst[:, h * seq : (h + 1) * seq] = (p * dp).astype(BF)
        qz = jnp.concatenate([jnp.where(low, qp, zero), jnp.where(low, zero, qp)], axis=0)
        cz = jnp.concatenate([jnp.where(low, dcp, zero), jnp.where(low, zero, dcp)], axis=0)
        dv = dotf(pt[...], cz, 1, 0)
        dk = dotf(dst[...], qz, 1, 0)
        dq = dotf(kx[0, :, :128], dst[:, :seq], 0, 0) + dotf(kx[1, :, :128], dst[:, seq:], 0, 0)
        dq = dq.T * (HD**-0.5)
        db_ref[0:1, columns_of(pair)] = jnp.sum(dq, axis=0, keepdims=True)
        db_ref[1:2, columns_of(pair)] = jnp.sum(dv, axis=0, keepdims=True)
        g, i = lax.div(pair, per), lax.rem(pair, per)
        for j, part in enumerate((dq, dk, dv)):
            at = columns_of(j * per + i)
            dm_ref[g, :, at] = part.astype(BF)
            pltpu.make_async_copy(dm_ref.at[g, :, at], dm_hbm.at[g, :, at], dsem).start()

        @pl.when(i == per - 1)
        def _():
            dw[g] = dotf(xt_ref[...], dm_ref[g], 1, 0).astype(BF)
            store_pieces(me, dw.at[g], keep_ref.at[g], send_ref.at[g], wsem)

        return carry

    lax.fori_loop(0, npair, pair_body, 0)
    small_rows(me, db_ref[...], s1_ref[...], s2_ref[...], ub_ref[...], e_ref)
    wait_all(dm_ref, dsem)
    wait_all(dw, wsem)


def attn_bwd(me, xt, first, rest, dc, qm, km, s1, s2, ub):
    n, seq, gw = rest[0].shape
    d = xt.shape[0]
    ps = pltpu.HBM((GROUPS,) + piece_shape(d, 3 * gw).shape, BF)
    shapes = [((GROUPS, seq, 3 * gw), BF)]
    one = pltpu.VMEM((2, seq, 128), BF)
    return pl.pallas_call(
        attn_bwd_kernel,
        in_specs=[SM] + [VM] * 3 + [ANY] * 14,
        out_specs=[ANY, ANY, ANY] + [VM] * 2,
        out_shape=[
            pltpu.HBM((GROUPS, seq, 3 * gw), BF),
            ps,
            ps,
            jax.ShapeDtypeStruct((2, d), F32),
            jax.ShapeDtypeStruct((2, 2, 4, d // 16, 128), BF),
        ],
        scratch_shapes=[
            one,
            one,
            one,
            one,
            pltpu.VMEM((2, seq, 128), F32),
            one,
            pltpu.VMEM((seq, 128), BF),
            pltpu.VMEM((seq, 128), BF),
            pltpu.VMEM((d, seq), BF),
            pltpu.VMEM((GROUPS, seq, 3 * gw), BF),
            pltpu.VMEM((2, seq, 256), BF),
            pltpu.VMEM((2, seq, 256), BF),
            pltpu.VMEM((seq, 256), BF),
            pltpu.VMEM((seq, 256), BF),
            pltpu.VMEM((seq, 2 * seq), BF),
            pltpu.VMEM((seq, 2 * seq), BF),
            pltpu.VMEM((GROUPS, d, 3 * gw), BF),
            pltpu.SemaphoreType.DMA((2, 6)),
            pltpu.SemaphoreType.DMA((3,)),
            pltpu.SemaphoreType.DMA,
            pltpu.SemaphoreType.DMA,
        ],
        compiler_params=pltpu.CompilerParams(vmem_limit_bytes=52 << 20),
        cost_estimate=pl.CostEstimate(flops=12_000_000_000, bytes_accessed=10 << 20, transcendentals=seq * seq * 12),
        name="attn_bwd",
    )(me, s1, s2, ub, *in_hbm(*first, *rest, dc, qm, km, xt))


def copies(pairs, sem):
    for src, dst in pairs:
        pltpu.make_async_copy(src, dst, sem).start()


def gelu_parts(u):
    u2 = u * u
    k1 = 0.7978845608028654
    k2 = k1 * 0.044715
    h = 0.5 + 0.5 * jnp.tanh(u * (k1 + k2 * u2))
    g = u * h
    return g, h + g * (1.0 - h) * (2 * k1 + (6 * k2) * u2)


def mid_a_kernel(rt, ft, me_ref, par_ref, ub_ref, x_hbm, c0_hbm, c12_hbm, *refs):
    pieces, refs = refs[:2], refs[2:]
    g, gp, y, yb, n1, r1, wo, wu, us, x_ref, c_ref, sem = refs
    me = read_me(me_ref)
    loads = ((c0_hbm, c_ref.at[pl.ds(0, 1)], 2), (c12_hbm, c_ref.at[pl.ds(1, 2)], 3), (x_hbm, x_ref, 4))
    for src, dst, k in loads:
        pltpu.make_async_copy(src, dst, sem.at[k]).start()
    nu, no = wu.shape[1] // 2, wo.shape[1] // 2
    for cr, ref in enumerate(pieces):
        pltpu.make_async_copy(ref.at[:, pl.ds(nu, no)], wo.at[:, columns(me, cr, no)], sem.at[0]).start()
    for cr, ref in enumerate(pieces):
        pltpu.make_async_copy(ref.at[:, pl.ds(0, nu)], wu.at[:, columns(me, cr, nu)], sem.at[1]).start()
    seq, d = x_ref.shape
    ff = wu.shape[1]
    gw = c_ref.shape[2]
    for src, dst, k in loads:
        pltpu.make_async_copy(src, dst, sem.at[k]).wait()
    wait_all(wo, sem.at[0])

    def rows_body(i, carry):
        rows = pl.ds(mult(i * rt, rt), rt)
        a = dotf(c_ref[0, rows, :], wo[:gw], 1, 0)
        a += dotf(c_ref[1, rows, :], wo[gw : 2 * gw], 1, 0)
        a += dotf(c_ref[2, rows, :], wo[2 * gw :], 1, 0)
        h = x_ref[rows, :].astype(F32) + (a + par_ref[2:3, :])
        cen = h - jnp.mean(h, axis=1, keepdims=True)
        r = lax.rsqrt(jnp.mean(cen * cen, axis=1, keepdims=True) + EPS)
        n = cen * r
        yt = n * par_ref[4:5, :] + par_ref[6:7, :]
        n1[rows, :] = n
        r1[rows, :] = jnp.broadcast_to(r, (rt, 128))
        y[rows, :] = yt
        yb[rows, :] = yt.astype(BF)
        return carry

    lax.fori_loop(0, seq // rt, rows_body, 0)
    wait_all(wu, sem.at[1])

    def product(i, slot):
        cs = pl.ds(mult(i * ft, ft), ft)
        us[slot] = dotf(yb[...], wu[:, cs], 1, 0)

    def finish(i, slot):
        cs = pl.ds(mult(i * ft, ft), ft)
        gt, gpt = gelu_parts(us[slot] + ub_ref[:, cs])
        g[:, cs] = gt.astype(BF)
        gp[:, cs] = gpt.astype(BF)

    last = ff // ft - 1
    product(0, 0)

    def cols_body(i, carry):
        product(2 * i + 1, 1)
        finish(2 * i, 0)
        product(lax.min(2 * i + 2, last), 0)
        finish(2 * i + 1, 1)
        return carry

    lax.fori_loop(0, ff // ft // 2, cols_body, 0)


def in_vmem(*arrays):
    return [pltpu.with_memory_space_constraint(a, pltpu.VMEM) for a in arrays]


def in_hbm(*arrays):
    return [pltpu.with_memory_space_constraint(a, pltpu.HBM) for a in arrays]


def mid_a(me, x, cs, par, ub, pieces):
    seq, d = x.shape
    ff = ub.shape[1]
    ft = 512
    shapes = [((seq, ff), BF), ((seq, ff), BF), ((seq, d), F32), ((seq, d), BF), ((seq, d), F32), ((seq, 128), F32)]
    shapes += [((d, d), BF), ((d, ff), BF)]
    return pl.pallas_call(
        functools.partial(mid_a_kernel, 256, ft),
        in_specs=[SM] + [VM] * 2 + [ANY] * 5,
        out_specs=[VM] * 8,
        out_shape=[pltpu.VMEM(*sh) for sh in shapes],
        scratch_shapes=[pltpu.VMEM((2, seq, ft), F32), pltpu.VMEM((seq, d), BF)]
        + [pltpu.VMEM((GROUPS, seq, d // GROUPS), BF), pltpu.SemaphoreType.DMA((5,))],
        compiler_params=pltpu.CompilerParams(vmem_limit_bytes=15 << 20),
        cost_estimate=pl.CostEstimate(
            flops=2 * seq * d * (d + ff), bytes_accessed=20 << 20, transcendentals=seq * ff
        ),
        name="mid_a",
    )(me, par, ub, *in_hbm(x, *cs, *pieces))


def mid_b_kernel(rt, ft, me_ref, len_ref, par_ref, y, g, gp, cot_hbm, *refs):
    wd_p, refs = refs[:8], refs[8:]
    out_hbm, dh2, du, keep_ref, send_ref, sm_ref, ubg_ref, cot, wd, dz, dw, sem, tsem = refs
    me = read_me(me_ref)
    load_pieces(me, wd_p, wd, sem.at[0])
    pltpu.make_async_copy(cot_hbm, cot, sem.at[1]).start()
    seq, d = y.shape
    ff = g.shape[1]
    tiles = seq // rt
    length = len_ref[0]
    sm_ref[...] = jnp.zeros_like(sm_ref)
    wait_all(wd, sem.at[0])
    pltpu.make_async_copy(cot_hbm, cot, sem.at[1]).wait()

    def rows_body(i, carry):
        rows = pl.ds(mult(i * rt, rt), rt)
        z = dotf(g[rows, :], wd[...], 1, 0) + par_ref[3:4, :]
        h = y[rows, :] + z
        cen = h - jnp.mean(h, axis=1, keepdims=True)
        r = lax.rsqrt(jnp.mean(cen * cen, axis=1, keepdims=True) + EPS)
        n = cen * r
        pos = lax.broadcasted_iota(jnp.int32, (rt, 1), 0) + i * rt
        valid = pos < length
        do = jnp.where(valid, cot[rows, :].astype(F32), 0.0)
        res = n * par_ref[5:6, :] + par_ref[7:8, :]
        cot[rows, :] = jnp.where(valid, res, 0.0).astype(BF)
        e = do * par_ref[5:6, :]
        me_ = jnp.mean(e, axis=1, keepdims=True)
        men = jnp.mean(e * n, axis=1, keepdims=True)
        dh = r * (e - me_ - n * men)
        dh2[rows, :] = dh
        dz[rows, :] = dh.astype(BF)
        sm_ref[0:1, :] += jnp.sum(do * n, axis=0, keepdims=True)
        sm_ref[1:2, :] += jnp.sum(do, axis=0, keepdims=True)
        sm_ref[2:3, :] += jnp.sum(dh, axis=0, keepdims=True)
        return carry

    lax.fori_loop(0, tiles, rows_body, 0)
    pltpu.make_async_copy(cot, out_hbm, sem.at[2]).start()
    n = d // 2
    part = ff // 32

    def dw_body(f, carry):
        rows = pl.ds(mult(f * 4 * part, part), 4 * part)
        dw[rows, :] = dotf(g[:, rows], dz[...], 0, 0).astype(BF)
        for cr, ref in ((1, send_ref), (0, keep_ref)):
            for j in range(4):
                at = dw.at[pl.ds(mult((f * 4 + j) * part, part), part), columns(me, cr, n)]
                to = ref.at[pl.ds(mult(f * part, part), part), pl.ds(j * n, n)]
                pltpu.make_async_copy(at, to, sem.at[3]).start()
        return carry

    lax.fori_loop(0, 8, dw_body, 0)

    def du_body(i, carry):
        cs = pl.ds(mult(i * 4 * part, 4 * part), 4 * part)
        dg = dotf(dz[...], wd[cs, :], 1, 1)
        dut = dg * gp[:, cs].astype(F32)
        ubg_ref[pl.ds(i, 1), :] = jnp.sum(dut, axis=0, keepdims=True)
        du[:, cs] = dut.astype(BF)
        return carry

    lax.fori_loop(0, 8, du_body, 0)
    pltpu.make_async_copy(cot, out_hbm, sem.at[2]).wait()
    wait_all(dw, sem.at[3])


def mid_b(me, length, y, cot, par, g, gp, wd_p):
    seq, d = y.shape
    ff = g.shape[1]
    rt = 256
    S = jax.ShapeDtypeStruct
    ps = pltpu.HBM((ff // 4, 2 * d), BF)
    return pl.pallas_call(
        functools.partial(mid_b_kernel, rt, 512),
        in_specs=[SM] * 2 + [VM] * 4 + [ANY] * 9,
        out_specs=[ANY] + [VM] * 2 + [ANY] * 2 + [VM] * 2,
        out_shape=[
            pltpu.HBM((seq, d), BF),
            pltpu.VMEM((seq, d), F32),
            pltpu.VMEM((seq, ff), BF),
            ps,
            ps,
            S((8, d), F32),
            S((8, ff // 8), F32),
        ],
        input_output_aliases={3: 1, 5: 2},
        scratch_shapes=[
            pltpu.VMEM((seq, d), BF),
            pltpu.VMEM((ff, d), BF),
            pltpu.VMEM((seq, d), BF),
            pltpu.VMEM((ff, d), BF),
            pltpu.SemaphoreType.DMA((4,)),
            pltpu.SemaphoreType.DMA((3, seq // rt)),
        ],
        compiler_params=pltpu.CompilerParams(vmem_limit_bytes=17 << 20),
        cost_estimate=pl.CostEstimate(flops=6 * seq * d * ff, bytes_accessed=20 << 20, transcendentals=seq),
        name="mid_b",
    )(me, length, par, *in_vmem(y, g, gp), *in_hbm(cot, *wd_p))


def mid_c_kernel(rt, ft, me_ref, par_ref, n1, r1, dh2, yb, wo, du, wu, *refs):
    c0_h, c12_h = refs[:2]
    dh1_h, dc_h, keep, send, sm_ref = refs[2:7]
    cs_, dwu, dwo, da, dc, dh1, sem = refs[7:]
    me = read_me(me_ref)
    seq, d = n1.shape
    ff = du.shape[1]
    gw = d // 3
    nu, no = ff // 2, d // 2
    steps = nu // ft
    for i in range(GROUPS):
        ref = c0_h.at[0] if i == 0 else c12_h.at[i - 1]
        pltpu.make_async_copy(ref, cs_.at[:, i * gw : (i + 1) * gw], sem.at[0]).start()
    sm_ref[...] = jnp.zeros_like(sm_ref)
    for cr, ref in ((1, send), (0, keep)):

        def dwu_body(j, carry):
            at = pl.ds(mult(lax.bitwise_xor(me[3], cr) * nu + j * ft, ft), ft)
            dwu[:, at] = dotf(yb[...], du[:, at], 0, 0).astype(BF)
            cut_pieces(me, dwu, at, ref, pl.ds(mult(j * ft, ft), ft), sem.at[1])
            return carry

        lax.fori_loop(0, steps, dwu_body, 0)

    def rows_body(i, carry):
        rows = pl.ds(mult(i * rt, rt), rt)
        dy = dh2[rows, :] + dotf(du[rows, :], wu[...], 1, 1)
        n = n1[rows, :]
        e = dy * par_ref[4:5, :]
        me_ = jnp.mean(e, axis=1, keepdims=True)
        men = jnp.mean(e * n, axis=1, keepdims=True)
        dh = r1[rows, 0:1] * (e - me_ - n * men)
        dh1[rows, :] = dh
        dat = dh.astype(BF)
        da[rows, :] = dat
        sm_ref[0:1, :] += jnp.sum(dy * n, axis=0, keepdims=True)
        sm_ref[1:2, :] += jnp.sum(dy, axis=0, keepdims=True)
        sm_ref[2:3, :] += jnp.sum(dh, axis=0, keepdims=True)
        dc[rows, :] = dotf(dat, wo[...], 1, 1).astype(BF)
        return carry

    lax.fori_loop(0, seq // rt, rows_body, 0)
    pltpu.make_async_copy(dh1, dh1_h, sem.at[2]).start()
    pltpu.make_async_copy(dc, dc_h, sem.at[3]).start()
    wait_all(cs_, sem.at[0])
    for cr, ref in ((1, send), (0, keep)):
        at = columns(me, cr, no)
        dwo[:, at] = dotf(cs_[...], da[:, at], 0, 0).astype(BF)
        cut_pieces(me, dwo, at, ref, pl.ds(nu, no), sem.at[4])
    pltpu.make_async_copy(dh1, dh1_h, sem.at[2]).wait()
    wait_all(dc, sem.at[3])
    wait_all(dwu, sem.at[1])
    wait_all(dwo, sem.at[4])


def mid_c(me, n1, r1, dh2, yb, cs, par, wo, du, wu):
    seq, d = n1.shape
    ff = du.shape[1]
    S = jax.ShapeDtypeStruct
    ps = pltpu.HBM(piece_shape(d, ff + d).shape, BF)
    dc = pltpu.HBM((seq, d), BF)
    ft = 512
    return pl.pallas_call(
        functools.partial(mid_c_kernel, 256, ft),
        in_specs=[SM] + [VM] * 8 + [ANY] * 2,
        out_specs=[ANY] * 4 + [VM],
        out_shape=[pltpu.HBM((seq, d), F32), dc, ps, ps, S((8, d), F32)],
        scratch_shapes=[
            pltpu.VMEM((seq, d), BF),
            pltpu.VMEM((d, ff), BF),
            pltpu.VMEM((d, d), BF),
            pltpu.VMEM((seq, d), BF),
            pltpu.VMEM((seq, d), BF),
            pltpu.VMEM((seq, d), F32),
            pltpu.SemaphoreType.DMA((5,)),
        ],
        compiler_params=pltpu.CompilerParams(vmem_limit_bytes=18 << 20),
        cost_estimate=pl.CostEstimate(flops=4 * seq * d * (ff + d), bytes_accessed=20 << 20, transcendentals=seq),
        name="mid_c",
    )(me, par, *in_vmem(n1, r1, dh2, yb, wo, du, wu), *in_hbm(*cs))


def input_grad_kernel(dh1_ref, m_ref, w0, w12, out_ref):
    acc = dh1_ref[...]
    for g in range(GROUPS):
        acc += dotf(m_ref[g], w0[0] if g == 0 else w12[g - 1], 1, 1)
    out_ref[...] = acc


def input_grad(dh1, dm, w0, w12):
    seq, d = dh1.shape
    n = dm.shape[2]
    rt = 256
    row = pl.BlockSpec((rt, d), lambda i: (i, 0))
    full = lambda k: pl.BlockSpec((k, d, n), lambda i: (0, 0, 0))
    return pl.pallas_call(
        input_grad_kernel,
        grid=(seq // rt,),
        in_specs=[row, pl.BlockSpec((GROUPS, rt, n), lambda i: (0, i, 0)), full(1), full(GROUPS - 1)],
        out_specs=row,
        out_shape=jax.ShapeDtypeStruct((seq, d), F32),
        compiler_params=pltpu.CompilerParams(vmem_limit_bytes=60 << 20),
        cost_estimate=pl.CostEstimate(flops=6 * seq * d * n, bytes_accessed=15 << 20, transcendentals=0),
        name="input_grad",
    )(dh1, dm, w0, w12)


def sum_kernel(*refs):
    out = refs[-1]
    first = 0
    for a, b in zip(refs[0:-1:2], refs[1:-1:2]):
        w = a.shape[1]
        out[:, first : first + w] = (a[...].astype(F32) + b[...].astype(F32)).astype(BF)
        first += w


def summed(*pairs):
    rows = pairs[0][0].shape[0]
    rt = rows // 8
    width = sum(a.shape[1] for a, _ in pairs)
    one = lambda w: pl.BlockSpec((rt, w), lambda i: (i, 0))
    arrays = [a for pair in pairs for a in pair]
    return pl.pallas_call(
        sum_kernel,
        grid=(8,),
        in_specs=[one(a.shape[1]) for a in arrays],
        out_specs=one(width),
        out_shape=jax.ShapeDtypeStruct((rows, width), BF),
        compiler_params=pltpu.CompilerParams(vmem_limit_bytes=16 << 20),
        cost_estimate=pl.CostEstimate(flops=rows * width, bytes_accessed=6 * rows * width, transcendentals=0),
        name="summed",
    )(*arrays)


def load_parts(parts, arrays, at, buf, sem):
    first = 0
    for array, group, w in parts:
        ref = arrays[array] if group is None else arrays[array].at[group]
        pltpu.make_async_copy(ref.at[at], buf.at[..., pl.ds(first, w)], sem).start()
        first += w


PLANE = ((0, 0), (0, 1), (1, 0), (1, 1))


def plane_kernel(parts, n, *refs):
    both, outs, (buf, sem) = (refs[:n], refs[n : 2 * n]), refs[2 * n : 2 * n + 4], refs[2 * n + 4 :]
    for j, at in enumerate(PLANE):
        for i, arrays in enumerate(both):
            load_parts(parts, arrays, at, buf.at[j, i], sem.at[j, i])
    for j in (1, 2, 3, 0):
        for i in range(2):
            wait_all(buf.at[j, i], sem.at[j, i])
        outs[j][...] = (buf[j, 0].astype(F32) + buf[j, 1].astype(F32)).astype(outs[j].dtype)


def line_kernel(stay, y, x, xy, *outs):
    for z, out in enumerate(outs):
        total = stay[z] + y[z].astype(F32) + x[z].astype(F32) + xy[z].astype(F32)
        out[...] = total.astype(out.dtype)


def plane_sums(parts, keeps, recvs):
    rows = keeps[0].shape[-2]
    width = sum(w for _, _, w in parts)
    shape = (4, rows, width)
    n = len(keeps)
    nbytes = 16 * rows * width * 10
    return pl.pallas_call(
        functools.partial(plane_kernel, parts, n),
        in_specs=[ANY] * (2 * n),
        out_specs=[VM] * 4,
        out_shape=[jax.ShapeDtypeStruct(shape, F32)] + [jax.ShapeDtypeStruct(shape, BF)] * 3,
        scratch_shapes=[pltpu.VMEM((4, 2) + shape, BF), pltpu.SemaphoreType.DMA((4, 2))],
        compiler_params=pltpu.CompilerParams(vmem_limit_bytes=12 << 20),
        cost_estimate=pl.CostEstimate(flops=nbytes, bytes_accessed=nbytes, transcendentals=0),
        name="plane_sums",
    )(*keeps, *recvs)


def line_sums(stay, y, x, xy):
    shape = stay.shape[1:]
    nbytes = 4 * stay.size * 4
    return pl.pallas_call(
        line_kernel,
        in_specs=[VM] * 4,
        out_specs=[VM] * 4,
        out_shape=[jax.ShapeDtypeStruct(shape, F32)] + [jax.ShapeDtypeStruct(shape, BF)] * 3,
        compiler_params=pltpu.CompilerParams(vmem_limit_bytes=8 << 20),
        cost_estimate=pl.CostEstimate(flops=nbytes, bytes_accessed=nbytes, transcendentals=0),
        name="line_sums",
    )(stay, y, x, xy)


def after(value, *others):
    return lax.optimization_barrier((value, *others))[0]


def added(*parts):
    return sum(p.astype(F32) for p in parts)


def flipped(array, bits, axes):
    for bit, axis in zip(bits, axes):
        array = jnp.where(bit == 1, jnp.flip(array, axis), array)
    return array


class Links:
    def __init__(self, mesh):
        r, f = mesh.shape["replica"], mesh.shape["fsdp"]
        self.direct = (r, f) == (4, 8)
        if self.direct:
            fi, ri = lax.axis_index("fsdp"), lax.axis_index("replica")
            self.me = jnp.stack([fi // 2, fi % 2, ri // 2, ri % 2]).astype(jnp.int32)
        else:
            self.me = jnp.zeros((4,), jnp.int32)

    def core(self, a):
        return lax.ppermute(a, "replica", [(i, i ^ 1) for i in range(4)])

    def x(self, a):
        return lax.ppermute(a, "replica", [(i, i ^ 2) for i in range(4)])

    def y(self, a):
        return lax.ppermute(a, "fsdp", [(i, i ^ 1) for i in range(8)])

    def z(self, a, d):
        return lax.ppermute(a, "fsdp", [(i, i ^ (2 * d)) for i in range(8)])

    def xy(self, a):
        both = ("replica", "fsdp")
        return lax.ppermute(a, both, [(i, i ^ 17) for i in range(32)])

    def to_plane(self, a):
        return [self.y(a), self.x(a), self.xy(a)]

    def to_z(self, own):
        return [self.z(own, d) for d in (1, 2, 3)]

    def across(self, sends):
        y, x, xy = sends
        return [self.y(y), self.x(x), self.xy(xy)]

    def down_z(self, sends):
        return [self.z(t, i + 1) for i, t in enumerate(sends)]

    def half(self, shard):
        n = shard.shape[-1] // 2
        return lax.dynamic_slice_in_dim(shard, self.me[3] * n, n, shard.ndim - 1)

    def quarter(self, shard):
        r = shard.shape[0] // 2
        return lax.dynamic_slice_in_dim(self.half(shard), self.me[2] * r, r, 0)

    def bits(self):
        z, y, x, c = (self.me[i] for i in range(4))
        return z // 2, z % 2, y, x, c

    def wide(self, own, other):
        c0 = self.me[3] == 0
        return jnp.concatenate([jnp.where(c0, own, other), jnp.where(c0, other, own)], axis=1)


def masks(length, chosen, seq):
    nb = chosen.shape[0]
    used = (length + BLK - 1) // BLK
    lane = jnp.arange(128, dtype=jnp.int32)[None, :]
    pos = jnp.arange(seq, dtype=jnp.int32)[:, None]
    kb = pos // BLK
    onehot = (kb == lane).astype(BF)
    picks = jnp.pad(chosen, ((0, 128 - nb), (0, 0)), constant_values=-1)
    allowed = (jnp.abs(lane - kb) <= 1) | (kb == 0) | (kb == used - 1) | (lane == 0) | (lane == used - 1)
    for i in range(chosen.shape[1]):
        allowed |= picks[:, i][None, :] == kb
    bias = jnp.where(allowed & (pos < length), 0.0, -1e9)
    return onehot, jnp.where(lane < nb, bias, 0.0).astype(BF)


def shards(mesh, tokens, lengths, random_blocks, qkv_weight, out_weight, up_weight, down_weight, proj_bias,
           up_bias, norm_gain, norm_bias, cotangent):
    links = Links(mesh)
    me = links.me
    direct = links.direct
    seq, d = tokens.shape
    gw = d // GROUPS
    hw = 3 * gw // 2
    f_size = mesh.shape["fsdp"]
    dl = proj_bias.shape[1]
    ul = up_bias.shape[0]
    n_up = ul // dl
    ff = ul * f_size
    nu, no = ff // 2, d // 2
    small = jnp.concatenate([proj_bias, norm_gain, norm_bias, up_bias.reshape(n_up, dl)], axis=0)

    groups = []
    for g in range(GROUPS):
        cut = [qkv_weight[:, j * d + g * gw : j * d + (g + 1) * gw] for j in range(3)]
        groups.append(jnp.concatenate(cut, axis=1))
    if direct:
        own0 = jnp.concatenate([links.half(groups[0]), jnp.pad(small.reshape(-1, hw), ((0, 8 - small.size // hw), (0, 0)))])
        own_m = jnp.concatenate([links.half(up_weight), links.half(out_weight)], axis=1)
        m_own = lax.all_gather(own_m, "fsdp", axis=0, tiled=True)
        own0 = after(own0, own_m)
        rows = groups[0].shape[0] // 2
        own12 = lax.dynamic_slice_in_dim(links.half(jnp.stack(groups[1:])), me[2] * rows, rows, 1)
        own12 = after(own12, own0)
        own_d = links.quarter(down_weight)
        z0 = links.to_z(own0)
        z12 = links.to_z(own12)
        b0 = jnp.stack([own0] + z0)
        by0 = links.y(b0)
        q0 = [b0, by0, links.core(b0), links.core(by0)]
        small = jnp.stack([b0[:, -8:], by0[:, -8:]], axis=1)
        small = small.reshape(2, 2, 2, -1)[..., : (8 + n_up) * dl]
        small = flipped(small, links.bits()[:3], (0, 1, 2)).reshape(f_size, 8 + n_up, dl)
    else:
        small = lax.all_gather(small, "fsdp", axis=0)
        every = [lax.all_gather(w, "fsdp", axis=0, tiled=True) for w in groups]
        q0 = every[0].reshape(4, 2, d // 8, 2, hw)
        q0 = [q0[:, y, :, c] for c in range(2) for y in range(2)]
        q12 = jnp.stack([w.reshape(4, 2, 2, d // 16, 2, hw) for w in every[1:]], axis=1)
        q12 = [q12[:, :, y, x, :, c] for c in range(2) for x in range(2) for y in range(2)]
        up_all = lax.all_gather(up_weight, "fsdp", axis=0, tiled=True)
        out_all = lax.all_gather(out_weight, "fsdp", axis=0, tiled=True)
        m_parts = [
            jnp.concatenate([up_all[:, c * nu : (c + 1) * nu], out_all[:, c * no : (c + 1) * no]], axis=1)
            for c in range(2)
        ]
        every = lax.all_gather(down_weight, "fsdp", axis=0, tiled=True).reshape(4, 2, 2, ff // 16, 2, d // 2)
        d_parts = [every[:, y, x, :, c] for c in range(2) for x in range(2) for y in range(2)]

    ub = small[:, 8:].reshape(1, ff).astype(F32)
    par = small[:, :8].transpose(1, 0, 2).reshape(8, d).astype(F32)
    onehot, bias = masks(lengths[0], random_blocks[0], seq)
    xt = tokens.T

    par3 = jnp.stack([par[:2, g * gw : (g + 1) * gw] for g in range(GROUPS)])
    one_rows = lambda m, refs, dst, sem: load_rows(m, [(ref, d // 8) for ref in refs], dst, sem)

    if direct:
        b12 = jnp.stack([own12] + z12)
        plane = links.to_plane(b12)
        z_d = links.to_z(after(own_d, b12))
        f0 = attn_fwd(me, after(tokens, xt, b12), par3, onehot, bias, q0, 0, 1, one_rows)
        plane, z_d = after((plane, z_d), f0[3])
        near = [b12] + plane
        q12 = near + [links.core(a) for a in near]
        b_d = jnp.stack([own_d] + z_d)
        plane = links.to_plane(b_d)
        core_b = links.core(b_d)
        f12 = attn_fwd(me, after(tokens, b_d), par3, onehot, bias, q12, 1, 2, load_pieces)
        m_own, core_b, *plane = after((m_own, core_b, *plane), f12[3])
        m_parts = [m_own, links.core(m_own)]
    else:
        f0 = attn_fwd(me, tokens, par3, onehot, bias, q0, 0, 1, one_rows)
        f12 = attn_fwd(me, tokens, par3, onehot, bias, q12, 1, 2, load_pieces)
    cs = [f0[3], f12[3]]
    gact, gp, y, yb, n1, r1, wo, wu = mid_a(me, tokens, cs, par, ub, m_parts)
    if direct:
        far = [links.core(a) for a in plane]
        d_parts = [b_d] + plane + [core_b] + list(after(tuple(far), y))
    result, dh2, du, dkeep, dsend, sm2, ubg = mid_b(me, lengths, y, cotangent, par, gact, gp, d_parts)
    dh1, dc, mkeep, msend, sm1 = mid_c(me, n1, r1, dh2, yb, cs, par, wo, du, wu)

    def backward(dc):
        return attn_bwd(me, xt, f0[:5], f12[:5], dc, onehot, bias, sm1, sm2, ubg)

    if direct:
        drecv = after(links.core(dsend), dc)
        mrecv = links.core(msend)
        total = summed((dkeep, drecv))
        part = lax.psum_scatter(total, "fsdp", scatter_dimension=0, tiled=True)
        mrecv = after(mrecv, total)
        m_stay, *m_sends = plane_sums(((0, None, mkeep.shape[-1]),), [mkeep], [mrecv])
        m_plane = links.across(m_sends)
        dm, keep, send, db, e = backward(after(dc, *m_sends))
        keep, send, e, m_plane = after((keep, send, e, m_plane), db)
        q_parts = tuple((0, g, hw) for g in range(GROUPS)) + ((1, None, 128),)
        q_stay, *q_sends = plane_sums(q_parts, [keep, e], [links.core(send), links.core(e)])
        q_plane = links.across(q_sends)
        m_base, *m_line = line_sums(m_stay, *m_plane)
        m_last = links.down_z(m_line)
        grad_in = input_grad(after(dh1, *q_sends, *m_line), dm, f0[5], f12[5])
        part, *q_plane = after((part, *q_plane), grad_in)
        part_x = links.x(part)
        q_base, *q_line = line_sums(q_stay, *q_plane)
        q_last = links.down_z(q_line)
        m_last = after(tuple(m_last), q_base)
        part, part_x = after((part, part_x), q_base)
        part = added(part, part_x).astype(BF)
        part_c = links.core(part)
        down = [p.reshape(-1, 4, no).transpose(1, 0, 2).reshape(-1, no) for p in (part, part_c)]
        down_grad = links.wide(*down).astype(F32)
        fin = jnp.concatenate([added(q_base, *q_last), added(m_base, *m_last)], axis=1).astype(BF)
        fx = links.x(fin)
        fc, fxc = links.core(fin), links.core(fx)
        quarters = (fin, fc, fx, fxc)
        x0, c0 = me[2] == 0, me[3] == 0

        def whole(first, w):
            cut = [q[:, first : first + w] for q in quarters]
            m, t = links.wide(*cut[:2]), links.wide(*cut[2:])
            return jnp.concatenate([jnp.where(x0, m, t), jnp.where(x0, t, m)], axis=0).astype(F32)

        qkv_cols = [whole(g * hw, hw) for g in range(GROUPS)]
        first = GROUPS * hw + 128
        up_grad, out_grad = whole(first, nu), whole(first + nu, no)
        cut = [q[: 8 + n_up, GROUPS * hw : GROUPS * hw + dl] for q in quarters]
        own = jnp.where(x0, jnp.where(c0, cut[0], cut[1]), jnp.where(c0, cut[2], cut[3])).astype(F32)
    else:

        def total(full):
            part = lax.psum_scatter(full.astype(F32), "fsdp", scatter_dimension=0, tiled=True)
            return lax.psum(part.astype(BF), "replica").astype(F32)

        def pieces_total(keep, send):
            full = jnp.stack([keep, send])
            c, x, y_, z, r, n = full.shape
            return total(full.transpose(3, 2, 1, 4, 0, 5).reshape(z * y_ * x * r, c * n))

        dm, keep, send, db, _ = backward(dc)
        grad_in = input_grad(dh1, dm, f0[5], f12[5])
        downs = jnp.stack([p.reshape(8, -1, 4, no).transpose(0, 2, 1, 3).reshape(ff, no) for p in (dkeep, dsend)], axis=1)
        down_grad = total(downs.reshape(ff, d))
        both_g = pieces_total(mkeep, msend)
        both_g = both_g.reshape(both_g.shape[0], 2, nu + no)
        up_grad = both_g[:, :, :nu].reshape(-1, ff)
        out_grad = both_g[:, :, nu:].reshape(-1, d)
        qkv_cols = [pieces_total(keep[g], send[g]) for g in range(GROUPS)]
        rows = jnp.stack([db[0], db[1], sm1[2], sm2[2], sm1[0], sm2[0], sm1[1], sm2[1]])
        rows = rows.reshape(8, f_size, dl).transpose(1, 0, 2)
        every = jnp.concatenate([rows, ubg.reshape(f_size, n_up, dl)], axis=1)
        every = lax.psum(every, ("replica", "fsdp"))
        own = lax.dynamic_index_in_dim(every, lax.axis_index("fsdp"), 0, keepdims=False)
    qkv_grad = jnp.concatenate(
        [qkv_cols[g][:, j * gw : (j + 1) * gw] for j in range(3) for g in range(GROUPS)], axis=1
    )
    return (
        result,
        grad_in,
        qkv_grad,
        out_grad,
        up_grad,
        down_grad,
        own[:4],
        own[8:].reshape(ul),
        own[4:6],
        own[6:8],
    )


def solution(mesh):
    both = ("replica", "fsdp")
    return jax.shard_map(
        functools.partial(shards, mesh),
        mesh=mesh,
        in_specs=(
            P(both, None),
            P(both),
            P(both, None, None),
            P("fsdp", None),
            P("fsdp", None),
            P("fsdp", None),
            P("fsdp", None),
            P(None, "fsdp"),
            P("fsdp"),
            P(None, "fsdp"),
            P(None, "fsdp"),
            P(both, None),
        ),
        out_specs=(
            P(both, None),
            P(both, None),
            P("fsdp", None),
            P("fsdp", None),
            P("fsdp", None),
            P("fsdp", None),
            P(None, "fsdp"),
            P("fsdp"),
            P(None, "fsdp"),
            P(None, "fsdp"),
        ),
        check_vma=False,
    )
```

```python
import functools

import jax
import jax.numpy as jnp
from jax import lax
from jax.experimental import pallas as pl
from jax.experimental.pallas import tpu as pltpu
from jax.sharding import PartitionSpec as P

D = 768
HD = 64
BLK = 64
GROUPS = 3
EPS = 1e-06
BF = jnp.bfloat16
F32 = jnp.float32
ANY = pl.BlockSpec(memory_space=pl.ANY)
VM = pl.BlockSpec(memory_space=pltpu.VMEM)
SM = pl.BlockSpec(memory_space=pltpu.SMEM)


def dotf(a, b, ca, cb):
    return lax.dot_general(a, b, (((ca,), (cb,)), ((), ())), preferred_element_type=F32)


def lane_iota(shape):
    return lax.broadcasted_iota(jnp.int32, shape, 1)


def mult(v, m):
    return pl.multiple_of(v, m)


def columns(me, cr, cols):
    return pl.ds(mult(lax.bitwise_xor(me[3], cr) * cols, cols), cols)


def load_rows(me, refs, dst, sem):
    for k, (ref, rows) in enumerate(refs):
        cols = ref.shape[-1]
        for zr in range(4):
            f = lax.bitwise_xor(me[0], zr) * 2 + lax.bitwise_xor(me[1], k % 2)
            at = dst.at[pl.ds(mult(f * rows, rows), rows), columns(me, k // 2, cols)]
            pltpu.make_async_copy(ref.at[zr, pl.ds(0, rows)], at, sem).start()


def piece_rows(me, xr, yr, zr, rows):
    z = lax.bitwise_xor(me[0], zr)
    y = lax.bitwise_xor(me[1], yr)
    x = lax.bitwise_xor(me[2], xr)
    return pl.ds(mult(((z * 2 + y) * 2 + x) * rows, rows), rows)


def load_pieces(me, refs, dst, sem):
    for k, ref in enumerate(refs):
        cr, xr, yr = k // 4, (k // 2) % 2, k % 2
        rows, cols = ref.shape[1:]
        for zr in range(4):
            at = dst.at[piece_rows(me, xr, yr, zr, rows), columns(me, cr, cols)]
            pltpu.make_async_copy(ref.at[zr], at, sem).start()


def cut_pieces(me, src, at, ref, to, sem):
    rows = ref.shape[3]
    for xr in range(2):
        for yr in range(2):
            for zr in range(4):
                part = src.at[piece_rows(me, xr, yr, zr, rows), at]
                pltpu.make_async_copy(part, ref.at[xr, yr, zr, :, to], sem).start()


def store_pieces(me, src, keep, send, sem):
    for cr, ref in ((1, send), (0, keep)):
        cols = ref.shape[4]
        cut_pieces(me, src, columns(me, cr, cols), ref, pl.ds(0, cols), sem)


def wait_all(ref, sem):
    pltpu.make_async_copy(ref, ref, sem).wait()


def read_me(me_ref):
    return [me_ref[i] for i in range(4)]


def piece_shape(rows, cols):
    return jax.ShapeDtypeStruct((2, 2, 4, rows // 16, cols // 2), BF)


def attn_fwd_kernel(first, n, load, me_ref, par_ref, x_hbm, qm_hbm, km_hbm, *refs):
    pieces, refs = refs[: len(refs) - 19], refs[len(refs) - 19 :]
    outs, refs = refs[:6], refs[6:]
    x_ref, qm_ref, km_ref, q_ref, k_ref, v_ref, c_ref, lse_ref, w_ref, kx_ref, vx_ref, sem, gsem = refs
    seq, gw = q_ref.shape[1:]
    me = read_me(me_ref)

    def fetch(g):
        load(me, [ref if n == 1 else ref.at[:, g] for ref in pieces], w_ref.at[g], gsem.at[g, 0])

    fetch(0)
    loads = ((x_hbm, x_ref, 0), (qm_hbm, qm_ref, 1), (km_hbm, km_ref, 2))
    for src, dst, i in loads:
        pltpu.make_async_copy(src, dst, sem.at[i]).start()
    for g in range(1, n):
        fetch(g)
    low = lane_iota((seq, 128)) < HD
    for src, dst, i in loads:
        pltpu.make_async_copy(src, dst, sem.at[i]).wait()

    def out_copies(g):
        whole = ((q_ref, 0), (k_ref, 1), (v_ref, 2), (w_ref, 5), (c_ref, 3), (lse_ref, 4))
        return [pltpu.make_async_copy(src.at[g], outs[i].at[g], gsem.at[g, i + 1]) for src, i in whole]

    def group_body(g, carry):
        wait_all(w_ref.at[g], gsem.at[g, 0])
        x = x_ref[...]
        w = w_ref.at[g]
        par = par_ref.at[first + g]
        q = dotf(x, w[:, :gw], 1, 0) + par[0:1, :]
        q_ref[g] = (q * (HD**-0.5)).astype(BF)
        k_ref[g] = dotf(x, w[:, gw : 2 * gw], 1, 0).astype(BF)
        v_ref[g] = (dotf(x, w[:, 2 * gw :], 1, 0) + par[1:2, :]).astype(BF)
        started = out_copies(g)
        for copy in started[:4]:
            copy.start()

        def pair_body(pair, carry):
            sl = pl.ds(mult(pair * 128, 128), 128)
            kp = k_ref[g, :, sl]
            vp = v_ref[g, :, sl]
            qx = jnp.concatenate([q_ref[g, :, sl], qm_ref[...]], axis=1)
            sums, lses = [], []
            for h in range(2):
                sel = low if h == 0 else jnp.logical_not(low)
                kx_ref[h, :, :128] = jnp.where(sel, kp, jnp.zeros_like(kp))
                kx_ref[h, :, 128:] = km_ref[...]
                vx_ref[h] = jnp.where(sel, vp, jnp.ones_like(vp))
            for h in range(2):
                s = dotf(qx, kx_ref[h], 1, 1)
                m = jnp.max(s, axis=1, keepdims=True)
                p = jnp.exp(s - m).astype(BF)
                c = dotf(p, vx_ref[h], 1, 0)
                t = pltpu.roll(c, HD, 1)
                sums.append(c / t)
                lses.append(m + jnp.log(t))
            c_ref[g, :, sl] = jnp.where(low, sums[0], sums[1]).astype(BF)
            lse_ref[g, :, sl] = jnp.where(low, lses[0], lses[1])
            return carry

        lax.fori_loop(0, gw // 128, pair_body, 0)
        for copy in started[4:]:
            copy.start()
        return carry

    lax.fori_loop(0, n, group_body, 0)
    for g in range(n):
        for copy in out_copies(g):
            copy.wait()


def attn_fwd(me, x, par, qm, km, pieces, first, n, load):
    seq, d = x.shape
    gw = d // GROUPS
    b = ((n, seq, gw), BF)
    shapes = [b, b, b, b, ((n, seq, gw), F32), ((n, d, 3 * gw), BF)]
    loaded = [((seq, d), BF), ((seq, 128), BF), ((seq, 128), BF)]
    return pl.pallas_call(
        functools.partial(attn_fwd_kernel, first, n, load),
        in_specs=[SM, VM] + [ANY] * (3 + len(pieces)),
        out_specs=[ANY] * 6,
        out_shape=[pltpu.HBM(*sh) for sh in shapes],
        scratch_shapes=[pltpu.VMEM(*sh) for sh in loaded + shapes]
        + [
            pltpu.VMEM((2, seq, 256), BF),
            pltpu.VMEM((2, seq, 128), BF),
            pltpu.SemaphoreType.DMA((3,)),
            pltpu.SemaphoreType.DMA((n, 7)),
        ],
        compiler_params=pltpu.CompilerParams(vmem_limit_bytes=38 << 20),
        cost_estimate=pl.CostEstimate(flops=n * 10_000_000_000, bytes_accessed=8 << 20, transcendentals=seq * seq * 4),
        name="attn_fwd",
    )(me, par, *in_hbm(x, qm, km), *pieces)


def split3(t):
    hi = t.astype(BF).astype(F32)
    r = t - hi
    mid = r.astype(BF).astype(F32)
    return hi, mid, r - mid


def small_rows(me, db, s1, s2, ub, out_ref):
    d = s1.shape[1]
    dl = d // 8
    rows = [db[0:1], db[1:2], s1[2:3], s2[2:3], s1[0:1], s2[0:1], s1[1:2], s2[1:2]]
    table = jnp.concatenate(rows, axis=0).astype(BF)
    out_ref[...] = jnp.zeros_like(out_ref)

    def pick(n, first):
        j = lax.broadcasted_iota(jnp.int32, (n, 128), 0)
        lane = lane_iota((n, 128))
        return ((j == lane + first) & (lane < dl)).astype(BF)

    ups = [dotf(ub.astype(BF), pick(ub.shape[1], k * dl), 1, 0) for k in range(4)]
    for f in range(8):
        top = dotf(table, pick(d, f * dl), 1, 0)
        both = jnp.concatenate([top] + [u[f : f + 1] for u in ups] + [jnp.zeros((4, 128), F32)], axis=0).astype(BF)
        for xr in range(2):
            out_ref[xr, lax.bitwise_xor(me[1], f % 2), lax.bitwise_xor(me[0], f // 2), 0:16, :] = both


def attn_bwd_kernel(me_ref, s1_ref, s2_ref, ub_ref, *refs):
    first_in, rest_in, dc_in = refs[:5], refs[5:10], refs[10]
    hbm, refs = refs[11:14], refs[14:]
    dm_hbm, keep_ref, send_ref, db_ref, e_ref = refs[:5]
    bufs, refs = refs[5:11], refs[11:]
    qm_ref, km_ref, xt_ref, dm_ref, kx, vx, qx, cx, pt, dst, dw, psem, sem, dsem, wsem = refs
    seq = xt_ref.shape[1]
    gw = dw.shape[2] // 3
    per = gw // 128
    npair = GROUPS * per
    lane = lane_iota((seq, 128))
    low = lane < HD
    columns_of = lambda i: pl.ds(mult(i * 128, 128), 128)

    def pair_copies(i, go):
        slot, g, at = lax.rem(i, 2), lax.div(i, per), columns_of(lax.rem(i, per))

        def move(src, j):
            copy = pltpu.make_async_copy(src, bufs[j].at[slot], psem.at[slot, j])
            copy.start() if go else copy.wait()

        move(dc_in.at[:, columns_of(i)], 5)
        if not go:
            for j in range(5):
                move(first_in[j].at[0, :, at], j)
            return

        @pl.when(g == 0)
        def _():
            for j in range(5):
                move(first_in[j].at[0, :, at], j)

        @pl.when(g > 0)
        def _():
            for j in range(5):
                move(rest_in[j].at[lax.max(g - 1, 0), :, at], j)

    pair_copies(0, True)
    whole = tuple(zip(hbm, (qm_ref, km_ref, xt_ref)))
    for j, (src, dst_) in enumerate(whole):
        pltpu.make_async_copy(src, dst_, sem.at[j]).start()
    for j, (src, dst_) in enumerate(whole):
        pltpu.make_async_copy(src, dst_, sem.at[j]).wait()
    me = read_me(me_ref)

    def pair_body(pair, carry):
        slot = lax.rem(pair, 2)
        pair_copies(pair, False)

        @pl.when(pair + 1 < npair)
        def _():
            pair_copies(pair + 1, True)

        qp, kp, vp, cp, lsep, dcp = (b[slot] for b in bufs)
        prod = dcp.astype(F32) * cp.astype(F32)
        zero = jnp.zeros_like(kp)
        one = jnp.ones_like(kp)
        qm = qm_ref[...].astype(F32)
        qx[:, :128] = qp
        cx[:, :128] = dcp
        for h in range(2):
            sel = low if h == 0 else jnp.logical_not(low)
            lse = jnp.max(jnp.where(sel, lsep, -3e38), axis=1, keepdims=True)
            delta = jnp.sum(jnp.where(sel, prod, 0.0), axis=1, keepdims=True)
            a, b, c = split3(-lse)
            qext = jnp.where(lane == 16, a, jnp.where(lane == 17, b, jnp.where(lane == 18, c, qm)))
            a, b, c = split3(-delta)
            cext = jnp.where(lane == 0, a, jnp.where(lane == 1, b, jnp.where(lane == 2, c, 0.0)))
            kx[h, :, :128] = jnp.where(sel, kp, zero)
            kx[h, :, 128:] = jnp.where((lane >= 16) & (lane < 19), one, km_ref[...])
            vx[h, :, :128] = jnp.where(sel, vp, zero)
            vx[h, :, 128:] = jnp.where(lane < 3, one, zero)
            qx[:, 128:] = qext.astype(BF)
            cx[:, 128:] = cext.astype(BF)
            p = jnp.exp(dotf(kx[h], qx[...], 1, 1))
            dp = dotf(vx[h], cx[...], 1, 1)
            pt[:, h * seq : (h + 1) * seq] = p.astype(BF)
            dst[:, h * seq : (h + 1) * seq] = (p * dp).astype(BF)
        qz = jnp.concatenate([jnp.where(low, qp, zero), jnp.where(low, zero, qp)], axis=0)
        cz = jnp.concatenate([jnp.where(low, dcp, zero), jnp.where(low, zero, dcp)], axis=0)
        dv = dotf(pt[...], cz, 1, 0)
        dk = dotf(dst[...], qz, 1, 0)
        dq = dotf(kx[0, :, :128], dst[:, :seq], 0, 0) + dotf(kx[1, :, :128], dst[:, seq:], 0, 0)
        dq = dq.T * (HD**-0.5)
        db_ref[0:1, columns_of(pair)] = jnp.sum(dq, axis=0, keepdims=True)
        db_ref[1:2, columns_of(pair)] = jnp.sum(dv, axis=0, keepdims=True)
        g, i = lax.div(pair, per), lax.rem(pair, per)
        for j, part in enumerate((dq, dk, dv)):
            at = columns_of(j * per + i)
            dm_ref[g, :, at] = part.astype(BF)
            pltpu.make_async_copy(dm_ref.at[g, :, at], dm_hbm.at[g, :, at], dsem).start()

        @pl.when(i == per - 1)
        def _():
            dw[g] = dotf(xt_ref[...], dm_ref[g], 1, 0).astype(BF)
            store_pieces(me, dw.at[g], keep_ref.at[g], send_ref.at[g], wsem)

        return carry

    lax.fori_loop(0, npair, pair_body, 0)
    small_rows(me, db_ref[...], s1_ref[...], s2_ref[...], ub_ref[...], e_ref)
    wait_all(dm_ref, dsem)
    wait_all(dw, wsem)


def attn_bwd(me, xt, first, rest, dc, qm, km, s1, s2, ub):
    n, seq, gw = rest[0].shape
    d = xt.shape[0]
    ps = pltpu.HBM((GROUPS,) + piece_shape(d, 3 * gw).shape, BF)
    shapes = [((GROUPS, seq, 3 * gw), BF)]
    one = pltpu.VMEM((2, seq, 128), BF)
    return pl.pallas_call(
        attn_bwd_kernel,
        in_specs=[SM] + [VM] * 3 + [ANY] * 14,
        out_specs=[ANY, ANY, ANY] + [VM] * 2,
        out_shape=[
            pltpu.HBM((GROUPS, seq, 3 * gw), BF),
            ps,
            ps,
            jax.ShapeDtypeStruct((2, d), F32),
            jax.ShapeDtypeStruct((2, 2, 4, d // 16, 128), BF),
        ],
        scratch_shapes=[
            one,
            one,
            one,
            one,
            pltpu.VMEM((2, seq, 128), F32),
            one,
            pltpu.VMEM((seq, 128), BF),
            pltpu.VMEM((seq, 128), BF),
            pltpu.VMEM((d, seq), BF),
            pltpu.VMEM((GROUPS, seq, 3 * gw), BF),
            pltpu.VMEM((2, seq, 256), BF),
            pltpu.VMEM((2, seq, 256), BF),
            pltpu.VMEM((seq, 256), BF),
            pltpu.VMEM((seq, 256), BF),
            pltpu.VMEM((seq, 2 * seq), BF),
            pltpu.VMEM((seq, 2 * seq), BF),
            pltpu.VMEM((GROUPS, d, 3 * gw), BF),
            pltpu.SemaphoreType.DMA((2, 6)),
            pltpu.SemaphoreType.DMA((3,)),
            pltpu.SemaphoreType.DMA,
            pltpu.SemaphoreType.DMA,
        ],
        compiler_params=pltpu.CompilerParams(vmem_limit_bytes=52 << 20),
        cost_estimate=pl.CostEstimate(flops=12_000_000_000, bytes_accessed=10 << 20, transcendentals=seq * seq * 12),
        name="attn_bwd",
    )(me, s1, s2, ub, *in_hbm(*first, *rest, dc, qm, km, xt))


def copies(pairs, sem):
    for src, dst in pairs:
        pltpu.make_async_copy(src, dst, sem).start()


def gelu_parts(u):
    u2 = u * u
    k1 = 0.7978845608028654
    k2 = k1 * 0.044715
    h = 0.5 + 0.5 * jnp.tanh(u * (k1 + k2 * u2))
    g = u * h
    return g, h + g * (1.0 - h) * (2 * k1 + (6 * k2) * u2)


def mid_a_kernel(rt, ft, me_ref, par_ref, ub_ref, x_hbm, c0_hbm, c12_hbm, *refs):
    pieces, refs = refs[:2], refs[2:]
    g, gp, y, yb, n1, r1, wo, wu, us, x_ref, c_ref, sem = refs
    me = read_me(me_ref)
    loads = ((c0_hbm, c_ref.at[pl.ds(0, 1)], 2), (c12_hbm, c_ref.at[pl.ds(1, 2)], 3), (x_hbm, x_ref, 4))
    for src, dst, k in loads:
        pltpu.make_async_copy(src, dst, sem.at[k]).start()
    nu, no = wu.shape[1] // 2, wo.shape[1] // 2
    for cr, ref in enumerate(pieces):
        pltpu.make_async_copy(ref.at[:, pl.ds(nu, no)], wo.at[:, columns(me, cr, no)], sem.at[0]).start()
    for cr, ref in enumerate(pieces):
        pltpu.make_async_copy(ref.at[:, pl.ds(0, nu)], wu.at[:, columns(me, cr, nu)], sem.at[1]).start()
    seq, d = x_ref.shape
    ff = wu.shape[1]
    gw = c_ref.shape[2]
    for src, dst, k in loads:
        pltpu.make_async_copy(src, dst, sem.at[k]).wait()
    wait_all(wo, sem.at[0])

    def rows_body(i, carry):
        rows = pl.ds(mult(i * rt, rt), rt)
        a = dotf(c_ref[0, rows, :], wo[:gw], 1, 0)
        a += dotf(c_ref[1, rows, :], wo[gw : 2 * gw], 1, 0)
        a += dotf(c_ref[2, rows, :], wo[2 * gw :], 1, 0)
        h = x_ref[rows, :].astype(F32) + (a + par_ref[2:3, :])
        cen = h - jnp.mean(h, axis=1, keepdims=True)
        r = lax.rsqrt(jnp.mean(cen * cen, axis=1, keepdims=True) + EPS)
        n = cen * r
        yt = n * par_ref[4:5, :] + par_ref[6:7, :]
        n1[rows, :] = n
        r1[rows, :] = jnp.broadcast_to(r, (rt, 128))
        y[rows, :] = yt
        yb[rows, :] = yt.astype(BF)
        return carry

    lax.fori_loop(0, seq // rt, rows_body, 0)
    wait_all(wu, sem.at[1])

    def product(i, slot):
        cs = pl.ds(mult(i * ft, ft), ft)
        us[slot] = dotf(yb[...], wu[:, cs], 1, 0)

    def finish(i, slot):
        cs = pl.ds(mult(i * ft, ft), ft)
        gt, gpt = gelu_parts(us[slot] + ub_ref[:, cs])
        g[:, cs] = gt.astype(BF)
        gp[:, cs] = gpt.astype(BF)

    last = ff // ft - 1
    product(0, 0)

    def cols_body(i, carry):
        product(2 * i + 1, 1)
        finish(2 * i, 0)
        product(lax.min(2 * i + 2, last), 0)
        finish(2 * i + 1, 1)
        return carry

    lax.fori_loop(0, ff // ft // 2, cols_body, 0)


def in_vmem(*arrays):
    return [pltpu.with_memory_space_constraint(a, pltpu.VMEM) for a in arrays]


def in_hbm(*arrays):
    return [pltpu.with_memory_space_constraint(a, pltpu.HBM) for a in arrays]


def mid_a(me, x, cs, par, ub, pieces):
    seq, d = x.shape
    ff = ub.shape[1]
    ft = 512
    shapes = [((seq, ff), BF), ((seq, ff), BF), ((seq, d), F32), ((seq, d), BF), ((seq, d), F32), ((seq, 128), F32)]
    shapes += [((d, d), BF), ((d, ff), BF)]
    return pl.pallas_call(
        functools.partial(mid_a_kernel, 256, ft),
        in_specs=[SM] + [VM] * 2 + [ANY] * 5,
        out_specs=[VM] * 8,
        out_shape=[pltpu.VMEM(*sh) for sh in shapes],
        scratch_shapes=[pltpu.VMEM((2, seq, ft), F32), pltpu.VMEM((seq, d), BF)]
        + [pltpu.VMEM((GROUPS, seq, d // GROUPS), BF), pltpu.SemaphoreType.DMA((5,))],
        compiler_params=pltpu.CompilerParams(vmem_limit_bytes=15 << 20),
        cost_estimate=pl.CostEstimate(
            flops=2 * seq * d * (d + ff), bytes_accessed=20 << 20, transcendentals=seq * ff
        ),
        name="mid_a",
    )(me, par, ub, *in_hbm(x, *cs, *pieces))


def mid_b_kernel(rt, ft, me_ref, len_ref, par_ref, y, g, gp, cot_hbm, *refs):
    wd_p, refs = refs[:8], refs[8:]
    out_hbm, dh2, du, keep_ref, send_ref, sm_ref, ubg_ref, cot, wd, dz, dw, sem, tsem = refs
    me = read_me(me_ref)
    load_pieces(me, wd_p, wd, sem.at[0])
    pltpu.make_async_copy(cot_hbm, cot, sem.at[1]).start()
    seq, d = y.shape
    ff = g.shape[1]
    tiles = seq // rt
    length = len_ref[0]
    sm_ref[...] = jnp.zeros_like(sm_ref)
    wait_all(wd, sem.at[0])
    pltpu.make_async_copy(cot_hbm, cot, sem.at[1]).wait()

    def rows_body(i, carry):
        rows = pl.ds(mult(i * rt, rt), rt)
        z = dotf(g[rows, :], wd[...], 1, 0) + par_ref[3:4, :]
        h = y[rows, :] + z
        cen = h - jnp.mean(h, axis=1, keepdims=True)
        r = lax.rsqrt(jnp.mean(cen * cen, axis=1, keepdims=True) + EPS)
        n = cen * r
        pos = lax.broadcasted_iota(jnp.int32, (rt, 1), 0) + i * rt
        valid = pos < length
        do = jnp.where(valid, cot[rows, :].astype(F32), 0.0)
        res = n * par_ref[5:6, :] + par_ref[7:8, :]
        cot[rows, :] = jnp.where(valid, res, 0.0).astype(BF)
        e = do * par_ref[5:6, :]
        me_ = jnp.mean(e, axis=1, keepdims=True)
        men = jnp.mean(e * n, axis=1, keepdims=True)
        dh = r * (e - me_ - n * men)
        dh2[rows, :] = dh
        dz[rows, :] = dh.astype(BF)
        sm_ref[0:1, :] += jnp.sum(do * n, axis=0, keepdims=True)
        sm_ref[1:2, :] += jnp.sum(do, axis=0, keepdims=True)
        sm_ref[2:3, :] += jnp.sum(dh, axis=0, keepdims=True)
        return carry

    lax.fori_loop(0, tiles, rows_body, 0)
    pltpu.make_async_copy(cot, out_hbm, sem.at[2]).start()
    n = d // 2
    part = ff // 32

    def dw_body(f, carry):
        rows = pl.ds(mult(f * 4 * part, part), 4 * part)
        dw[rows, :] = dotf(g[:, rows], dz[...], 0, 0).astype(BF)
        for cr, ref in ((1, send_ref), (0, keep_ref)):
            for j in range(4):
                at = dw.at[pl.ds(mult((f * 4 + j) * part, part), part), columns(me, cr, n)]
                to = ref.at[pl.ds(mult(f * part, part), part), pl.ds(j * n, n)]
                pltpu.make_async_copy(at, to, sem.at[3]).start()
        return carry

    lax.fori_loop(0, 8, dw_body, 0)

    def du_body(i, carry):
        cs = pl.ds(mult(i * 4 * part, 4 * part), 4 * part)
        dg = dotf(dz[...], wd[cs, :], 1, 1)
        dut = dg * gp[:, cs].astype(F32)
        ubg_ref[pl.ds(i, 1), :] = jnp.sum(dut, axis=0, keepdims=True)
        du[:, cs] = dut.astype(BF)
        return carry

    lax.fori_loop(0, 8, du_body, 0)
    pltpu.make_async_copy(cot, out_hbm, sem.at[2]).wait()
    wait_all(dw, sem.at[3])


def mid_b(me, length, y, cot, par, g, gp, wd_p):
    seq, d = y.shape
    ff = g.shape[1]
    rt = 256
    S = jax.ShapeDtypeStruct
    ps = pltpu.HBM((ff // 4, 2 * d), BF)
    return pl.pallas_call(
        functools.partial(mid_b_kernel, rt, 512),
        in_specs=[SM] * 2 + [VM] * 4 + [ANY] * 9,
        out_specs=[ANY] + [VM] * 2 + [ANY] * 2 + [VM] * 2,
        out_shape=[
            pltpu.HBM((seq, d), BF),
            pltpu.VMEM((seq, d), F32),
            pltpu.VMEM((seq, ff), BF),
            ps,
            ps,
            S((8, d), F32),
            S((8, ff // 8), F32),
        ],
        input_output_aliases={3: 1, 5: 2},
        scratch_shapes=[
            pltpu.VMEM((seq, d), BF),
            pltpu.VMEM((ff, d), BF),
            pltpu.VMEM((seq, d), BF),
            pltpu.VMEM((ff, d), BF),
            pltpu.SemaphoreType.DMA((4,)),
            pltpu.SemaphoreType.DMA((3, seq // rt)),
        ],
        compiler_params=pltpu.CompilerParams(vmem_limit_bytes=17 << 20),
        cost_estimate=pl.CostEstimate(flops=6 * seq * d * ff, bytes_accessed=20 << 20, transcendentals=seq),
        name="mid_b",
    )(me, length, par, *in_vmem(y, g, gp), *in_hbm(cot, *wd_p))


def mid_c_kernel(rt, ft, me_ref, par_ref, n1, r1, dh2, yb, wo, du, wu, *refs):
    c0_h, c12_h = refs[:2]
    dh1_h, dc_h, keep, send, sm_ref = refs[2:7]
    cs_, dwu, dwo, da, dc, dh1, sem = refs[7:]
    me = read_me(me_ref)
    seq, d = n1.shape
    ff = du.shape[1]
    gw = d // 3
    nu, no = ff // 2, d // 2
    steps = nu // ft
    for i in range(GROUPS):
        ref = c0_h.at[0] if i == 0 else c12_h.at[i - 1]
        pltpu.make_async_copy(ref, cs_.at[:, i * gw : (i + 1) * gw], sem.at[0]).start()
    sm_ref[...] = jnp.zeros_like(sm_ref)
    for cr, ref in ((1, send), (0, keep)):

        def dwu_body(j, carry):
            at = pl.ds(mult(lax.bitwise_xor(me[3], cr) * nu + j * ft, ft), ft)
            dwu[:, at] = dotf(yb[...], du[:, at], 0, 0).astype(BF)
            cut_pieces(me, dwu, at, ref, pl.ds(mult(j * ft, ft), ft), sem.at[1])
            return carry

        lax.fori_loop(0, steps, dwu_body, 0)

    def rows_body(i, carry):
        rows = pl.ds(mult(i * rt, rt), rt)
        dy = dh2[rows, :] + dotf(du[rows, :], wu[...], 1, 1)
        n = n1[rows, :]
        e = dy * par_ref[4:5, :]
        me_ = jnp.mean(e, axis=1, keepdims=True)
        men = jnp.mean(e * n, axis=1, keepdims=True)
        dh = r1[rows, 0:1] * (e - me_ - n * men)
        dh1[rows, :] = dh
        dat = dh.astype(BF)
        da[rows, :] = dat
        sm_ref[0:1, :] += jnp.sum(dy * n, axis=0, keepdims=True)
        sm_ref[1:2, :] += jnp.sum(dy, axis=0, keepdims=True)
        sm_ref[2:3, :] += jnp.sum(dh, axis=0, keepdims=True)
        dc[rows, :] = dotf(dat, wo[...], 1, 1).astype(BF)
        return carry

    lax.fori_loop(0, seq // rt, rows_body, 0)
    pltpu.make_async_copy(dh1, dh1_h, sem.at[2]).start()
    pltpu.make_async_copy(dc, dc_h, sem.at[3]).start()
    wait_all(cs_, sem.at[0])
    for cr, ref in ((1, send), (0, keep)):
        at = columns(me, cr, no)
        dwo[:, at] = dotf(cs_[...], da[:, at], 0, 0).astype(BF)
        cut_pieces(me, dwo, at, ref, pl.ds(nu, no), sem.at[4])
    pltpu.make_async_copy(dh1, dh1_h, sem.at[2]).wait()
    wait_all(dc, sem.at[3])
    wait_all(dwu, sem.at[1])
    wait_all(dwo, sem.at[4])


def mid_c(me, n1, r1, dh2, yb, cs, par, wo, du, wu):
    seq, d = n1.shape
    ff = du.shape[1]
    S = jax.ShapeDtypeStruct
    ps = pltpu.HBM(piece_shape(d, ff + d).shape, BF)
    dc = pltpu.HBM((seq, d), BF)
    ft = 512
    return pl.pallas_call(
        functools.partial(mid_c_kernel, 256, ft),
        in_specs=[SM] + [VM] * 8 + [ANY] * 2,
        out_specs=[ANY] * 4 + [VM],
        out_shape=[pltpu.HBM((seq, d), F32), dc, ps, ps, S((8, d), F32)],
        scratch_shapes=[
            pltpu.VMEM((seq, d), BF),
            pltpu.VMEM((d, ff), BF),
            pltpu.VMEM((d, d), BF),
            pltpu.VMEM((seq, d), BF),
            pltpu.VMEM((seq, d), BF),
            pltpu.VMEM((seq, d), F32),
            pltpu.SemaphoreType.DMA((5,)),
        ],
        compiler_params=pltpu.CompilerParams(vmem_limit_bytes=18 << 20),
        cost_estimate=pl.CostEstimate(flops=4 * seq * d * (ff + d), bytes_accessed=20 << 20, transcendentals=seq),
        name="mid_c",
    )(me, par, *in_vmem(n1, r1, dh2, yb, wo, du, wu), *in_hbm(*cs))


def input_grad_kernel(dh1_ref, m_ref, w0, w12, out_ref):
    acc = dh1_ref[...]
    for g in range(GROUPS):
        acc += dotf(m_ref[g], w0[0] if g == 0 else w12[g - 1], 1, 1)
    out_ref[...] = acc


def input_grad(dh1, dm, w0, w12):
    seq, d = dh1.shape
    n = dm.shape[2]
    rt = 256
    row = pl.BlockSpec((rt, d), lambda i: (i, 0))
    full = lambda k: pl.BlockSpec((k, d, n), lambda i: (0, 0, 0))
    return pl.pallas_call(
        input_grad_kernel,
        grid=(seq // rt,),
        in_specs=[row, pl.BlockSpec((GROUPS, rt, n), lambda i: (0, i, 0)), full(1), full(GROUPS - 1)],
        out_specs=row,
        out_shape=jax.ShapeDtypeStruct((seq, d), F32),
        compiler_params=pltpu.CompilerParams(vmem_limit_bytes=60 << 20),
        cost_estimate=pl.CostEstimate(flops=6 * seq * d * n, bytes_accessed=15 << 20, transcendentals=0),
        name="input_grad",
    )(dh1, dm, w0, w12)


def sum_kernel(*refs):
    out = refs[-1]
    first = 0
    for a, b in zip(refs[0:-1:2], refs[1:-1:2]):
        w = a.shape[1]
        out[:, first : first + w] = (a[...].astype(F32) + b[...].astype(F32)).astype(BF)
        first += w


def summed(*pairs):
    rows = pairs[0][0].shape[0]
    rt = rows // 8
    width = sum(a.shape[1] for a, _ in pairs)
    one = lambda w: pl.BlockSpec((rt, w), lambda i: (i, 0))
    arrays = [a for pair in pairs for a in pair]
    return pl.pallas_call(
        sum_kernel,
        grid=(8,),
        in_specs=[one(a.shape[1]) for a in arrays],
        out_specs=one(width),
        out_shape=jax.ShapeDtypeStruct((rows, width), BF),
        compiler_params=pltpu.CompilerParams(vmem_limit_bytes=16 << 20),
        cost_estimate=pl.CostEstimate(flops=rows * width, bytes_accessed=6 * rows * width, transcendentals=0),
        name="summed",
    )(*arrays)


def load_parts(parts, arrays, at, buf, sem):
    first = 0
    for array, group, w in parts:
        ref = arrays[array] if group is None else arrays[array].at[group]
        pltpu.make_async_copy(ref.at[at], buf.at[..., pl.ds(first, w)], sem).start()
        first += w


PLANE = ((0, 0), (0, 1), (1, 0), (1, 1))


def plane_kernel(parts, n, *refs):
    both, outs, (buf, sem) = (refs[:n], refs[n : 2 * n]), refs[2 * n : 2 * n + 4], refs[2 * n + 4 :]
    for j, at in enumerate(PLANE):
        for i, arrays in enumerate(both):
            load_parts(parts, arrays, at, buf.at[j, i], sem.at[j, i])
    for j in (1, 2, 3, 0):
        for i in range(2):
            wait_all(buf.at[j, i], sem.at[j, i])
        outs[j][...] = (buf[j, 0].astype(F32) + buf[j, 1].astype(F32)).astype(outs[j].dtype)


def line_kernel(stay, y, x, xy, *outs):
    for z, out in enumerate(outs):
        total = stay[z] + y[z].astype(F32) + x[z].astype(F32) + xy[z].astype(F32)
        out[...] = total.astype(out.dtype)


def plane_sums(parts, keeps, recvs):
    rows = keeps[0].shape[-2]
    width = sum(w for _, _, w in parts)
    shape = (4, rows, width)
    n = len(keeps)
    nbytes = 16 * rows * width * 10
    return pl.pallas_call(
        functools.partial(plane_kernel, parts, n),
        in_specs=[ANY] * (2 * n),
        out_specs=[VM] * 4,
        out_shape=[jax.ShapeDtypeStruct(shape, F32)] + [jax.ShapeDtypeStruct(shape, BF)] * 3,
        scratch_shapes=[pltpu.VMEM((4, 2) + shape, BF), pltpu.SemaphoreType.DMA((4, 2))],
        compiler_params=pltpu.CompilerParams(vmem_limit_bytes=12 << 20),
        cost_estimate=pl.CostEstimate(flops=nbytes, bytes_accessed=nbytes, transcendentals=0),
        name="plane_sums",
    )(*keeps, *recvs)


def line_sums(stay, y, x, xy):
    shape = stay.shape[1:]
    nbytes = 4 * stay.size * 4
    return pl.pallas_call(
        line_kernel,
        in_specs=[VM] * 4,
        out_specs=[VM] * 4,
        out_shape=[jax.ShapeDtypeStruct(shape, F32)] + [jax.ShapeDtypeStruct(shape, BF)] * 3,
        compiler_params=pltpu.CompilerParams(vmem_limit_bytes=8 << 20),
        cost_estimate=pl.CostEstimate(flops=nbytes, bytes_accessed=nbytes, transcendentals=0),
        name="line_sums",
    )(stay, y, x, xy)


def after(value, *others):
    return lax.optimization_barrier((value, *others))[0]


def added(*parts):
    return sum(p.astype(F32) for p in parts)


def flipped(array, bits, axes):
    for bit, axis in zip(bits, axes):
        array = jnp.where(bit == 1, jnp.flip(array, axis), array)
    return array


class Links:
    def __init__(self, mesh):
        r, f = mesh.shape["replica"], mesh.shape["fsdp"]
        self.direct = (r, f) == (4, 8)
        if self.direct:
            fi, ri = lax.axis_index("fsdp"), lax.axis_index("replica")
            self.me = jnp.stack([fi // 2, fi % 2, ri // 2, ri % 2]).astype(jnp.int32)
        else:
            self.me = jnp.zeros((4,), jnp.int32)

    def core(self, a):
        return lax.ppermute(a, "replica", [(i, i ^ 1) for i in range(4)])

    def x(self, a):
        return lax.ppermute(a, "replica", [(i, i ^ 2) for i in range(4)])

    def y(self, a):
        return lax.ppermute(a, "fsdp", [(i, i ^ 1) for i in range(8)])

    def z(self, a, d):
        return lax.ppermute(a, "fsdp", [(i, i ^ (2 * d)) for i in range(8)])

    def xy(self, a):
        both = ("replica", "fsdp")
        return lax.ppermute(a, both, [(i, i ^ 17) for i in range(32)])

    def to_plane(self, a):
        return [self.y(a), self.x(a), self.xy(a)]

    def to_z(self, own):
        return [self.z(own, d) for d in (1, 2, 3)]

    def across(self, sends):
        y, x, xy = sends
        return [self.y(y), self.x(x), self.xy(xy)]

    def down_z(self, sends):
        return [self.z(t, i + 1) for i, t in enumerate(sends)]

    def half(self, shard):
        n = shard.shape[-1] // 2
        return lax.dynamic_slice_in_dim(shard, self.me[3] * n, n, shard.ndim - 1)

    def quarter(self, shard):
        r = shard.shape[0] // 2
        return lax.dynamic_slice_in_dim(self.half(shard), self.me[2] * r, r, 0)

    def bits(self):
        z, y, x, c = (self.me[i] for i in range(4))
        return z // 2, z % 2, y, x, c

    def wide(self, own, other):
        c0 = self.me[3] == 0
        return jnp.concatenate([jnp.where(c0, own, other), jnp.where(c0, other, own)], axis=1)


def masks(length, chosen, seq):
    nb = chosen.shape[0]
    used = (length + BLK - 1) // BLK
    lane = jnp.arange(128, dtype=jnp.int32)[None, :]
    pos = jnp.arange(seq, dtype=jnp.int32)[:, None]
    kb = pos // BLK
    onehot = (kb == lane).astype(BF)
    picks = jnp.pad(chosen, ((0, 128 - nb), (0, 0)), constant_values=-1)
    allowed = (jnp.abs(lane - kb) <= 1) | (kb == 0) | (kb == used - 1) | (lane == 0) | (lane == used - 1)
    for i in range(chosen.shape[1]):
        allowed |= picks[:, i][None, :] == kb
    bias = jnp.where(allowed & (pos < length), 0.0, -1e9)
    return onehot, jnp.where(lane < nb, bias, 0.0).astype(BF)


def shards(mesh, tokens, lengths, random_blocks, qkv_weight, out_weight, up_weight, down_weight, proj_bias,
           up_bias, norm_gain, norm_bias, cotangent):
    links = Links(mesh)
    me = links.me
    direct = links.direct
    seq, d = tokens.shape
    gw = d // GROUPS
    hw = 3 * gw // 2
    f_size = mesh.shape["fsdp"]
    dl = proj_bias.shape[1]
    ul = up_bias.shape[0]
    n_up = ul // dl
    ff = ul * f_size
    nu, no = ff // 2, d // 2
    small = jnp.concatenate([proj_bias, norm_gain, norm_bias, up_bias.reshape(n_up, dl)], axis=0)

    groups = []
    for g in range(GROUPS):
        cut = [qkv_weight[:, j * d + g * gw : j * d + (g + 1) * gw] for j in range(3)]
        groups.append(jnp.concatenate(cut, axis=1))
    if direct:
        own0 = jnp.concatenate([links.half(groups[0]), jnp.pad(small.reshape(-1, hw), ((0, 8 - small.size // hw), (0, 0)))])
        own_m = jnp.concatenate([links.half(up_weight), links.half(out_weight)], axis=1)
        m_own = lax.all_gather(own_m, "fsdp", axis=0, tiled=True)
        own0 = after(own0, own_m)
        rows = groups[0].shape[0] // 2
        own12 = lax.dynamic_slice_in_dim(links.half(jnp.stack(groups[1:])), me[2] * rows, rows, 1)
        own12 = after(own12, own0)
        own_d = links.quarter(down_weight)
        z0 = links.to_z(own0)
        z12 = links.to_z(own12)
        b0 = jnp.stack([own0] + z0)
        by0 = links.y(b0)
        q0 = [b0, by0, links.core(b0), links.core(by0)]
        small = jnp.stack([b0[:, -8:], by0[:, -8:]], axis=1)
        small = small.reshape(2, 2, 2, -1)[..., : (8 + n_up) * dl]
        small = flipped(small, links.bits()[:3], (0, 1, 2)).reshape(f_size, 8 + n_up, dl)
    else:
        small = lax.all_gather(small, "fsdp", axis=0)
        every = [lax.all_gather(w, "fsdp", axis=0, tiled=True) for w in groups]
        q0 = every[0].reshape(4, 2, d // 8, 2, hw)
        q0 = [q0[:, y, :, c] for c in range(2) for y in range(2)]
        q12 = jnp.stack([w.reshape(4, 2, 2, d // 16, 2, hw) for w in every[1:]], axis=1)
        q12 = [q12[:, :, y, x, :, c] for c in range(2) for x in range(2) for y in range(2)]
        up_all = lax.all_gather(up_weight, "fsdp", axis=0, tiled=True)
        out_all = lax.all_gather(out_weight, "fsdp", axis=0, tiled=True)
        m_parts = [
            jnp.concatenate([up_all[:, c * nu : (c + 1) * nu], out_all[:, c * no : (c + 1) * no]], axis=1)
            for c in range(2)
        ]
        every = lax.all_gather(down_weight, "fsdp", axis=0, tiled=True).reshape(4, 2, 2, ff // 16, 2, d // 2)
        d_parts = [every[:, y, x, :, c] for c in range(2) for x in range(2) for y in range(2)]

    ub = small[:, 8:].reshape(1, ff).astype(F32)
    par = small[:, :8].transpose(1, 0, 2).reshape(8, d).astype(F32)
    onehot, bias = masks(lengths[0], random_blocks[0], seq)
    xt = tokens.T

    par3 = jnp.stack([par[:2, g * gw : (g + 1) * gw] for g in range(GROUPS)])
    one_rows = lambda m, refs, dst, sem: load_rows(m, [(ref, d // 8) for ref in refs], dst, sem)

    if direct:
        b12 = jnp.stack([own12] + z12)
        plane = links.to_plane(b12)
        z_d = links.to_z(after(own_d, b12))
        f0 = attn_fwd(me, after(tokens, xt, b12), par3, onehot, bias, q0, 0, 1, one_rows)
        plane, z_d = after((plane, z_d), f0[3])
        near = [b12] + plane
        q12 = near + [links.core(a) for a in near]
        b_d = jnp.stack([own_d] + z_d)
        plane = links.to_plane(b_d)
        core_b = links.core(b_d)
        f12 = attn_fwd(me, after(tokens, b_d), par3, onehot, bias, q12, 1, 2, load_pieces)
        m_own, core_b, *plane = after((m_own, core_b, *plane), f12[3])
        m_parts = [m_own, links.core(m_own)]
    else:
        f0 = attn_fwd(me, tokens, par3, onehot, bias, q0, 0, 1, one_rows)
        f12 = attn_fwd(me, tokens, par3, onehot, bias, q12, 1, 2, load_pieces)
    cs = [f0[3], f12[3]]
    gact, gp, y, yb, n1, r1, wo, wu = mid_a(me, tokens, cs, par, ub, m_parts)
    if direct:
        far = [links.core(a) for a in plane]
        d_parts = [b_d] + plane + [core_b] + list(after(tuple(far), y))
    result, dh2, du, dkeep, dsend, sm2, ubg = mid_b(me, lengths, y, cotangent, par, gact, gp, d_parts)
    dh1, dc, mkeep, msend, sm1 = mid_c(me, n1, r1, dh2, yb, cs, par, wo, du, wu)

    def backward(dc):
        return attn_bwd(me, xt, f0[:5], f12[:5], dc, onehot, bias, sm1, sm2, ubg)

    if direct:
        drecv = after(links.core(dsend), dc)
        mrecv = links.core(msend)
        total = summed((dkeep, drecv))
        part = lax.psum_scatter(total, "fsdp", scatter_dimension=0, tiled=True)
        mrecv = after(mrecv, total)
        m_stay, *m_sends = plane_sums(((0, None, mkeep.shape[-1]),), [mkeep], [mrecv])
        m_plane = links.across(m_sends)
        dm, keep, send, db, e = backward(after(dc, *m_sends))
        keep, send, e, m_plane = after((keep, send, e, m_plane), db)
        q_parts = tuple((0, g, hw) for g in range(GROUPS)) + ((1, None, 128),)
        q_stay, *q_sends = plane_sums(q_parts, [keep, e], [links.core(send), links.core(e)])
        q_plane = links.across(q_sends)
        m_base, *m_line = line_sums(m_stay, *m_plane)
        m_last = links.down_z(m_line)
        grad_in = input_grad(after(dh1, *q_sends, *m_line), dm, f0[5], f12[5])
        q_plane = after(tuple(q_plane), grad_in)
        q_base, *q_line = line_sums(q_stay, *q_plane)
        part, *q_line = after((part, *q_line), q_base)
        part_x = links.x(part)
        q_last = links.down_z(q_line)
        m_last = after(tuple(m_last), q_base)
        part, part_x = after((part, part_x), q_base)
        part = added(part, part_x).astype(BF)
        part_c = links.core(part)
        down = [p.reshape(-1, 4, no).transpose(1, 0, 2).reshape(-1, no) for p in (part, part_c)]
        down_grad = links.wide(*down).astype(F32)
        fin = jnp.concatenate([added(q_base, *q_last), added(m_base, *m_last)], axis=1).astype(BF)
        fx = links.x(fin)
        fc, fxc = links.core(fin), links.core(fx)
        quarters = (fin, fc, fx, fxc)
        x0, c0 = me[2] == 0, me[3] == 0

        def whole(first, w):
            cut = [q[:, first : first + w] for q in quarters]
            m, t = links.wide(*cut[:2]), links.wide(*cut[2:])
            return jnp.concatenate([jnp.where(x0, m, t), jnp.where(x0, t, m)], axis=0).astype(F32)

        qkv_cols = [whole(g * hw, hw) for g in range(GROUPS)]
        first = GROUPS * hw + 128
        up_grad, out_grad = whole(first, nu), whole(first + nu, no)
        cut = [q[: 8 + n_up, GROUPS * hw : GROUPS * hw + dl] for q in quarters]
        own = jnp.where(x0, jnp.where(c0, cut[0], cut[1]), jnp.where(c0, cut[2], cut[3])).astype(F32)
    else:

        def total(full):
            part = lax.psum_scatter(full.astype(F32), "fsdp", scatter_dimension=0, tiled=True)
            return lax.psum(part.astype(BF), "replica").astype(F32)

        def pieces_total(keep, send):
            full = jnp.stack([keep, send])
            c, x, y_, z, r, n = full.shape
            return total(full.transpose(3, 2, 1, 4, 0, 5).reshape(z * y_ * x * r, c * n))

        dm, keep, send, db, _ = backward(dc)
        grad_in = input_grad(dh1, dm, f0[5], f12[5])
        downs = jnp.stack([p.reshape(8, -1, 4, no).transpose(0, 2, 1, 3).reshape(ff, no) for p in (dkeep, dsend)], axis=1)
        down_grad = total(downs.reshape(ff, d))
        both_g = pieces_total(mkeep, msend)
        both_g = both_g.reshape(both_g.shape[0], 2, nu + no)
        up_grad = both_g[:, :, :nu].reshape(-1, ff)
        out_grad = both_g[:, :, nu:].reshape(-1, d)
        qkv_cols = [pieces_total(keep[g], send[g]) for g in range(GROUPS)]
        rows = jnp.stack([db[0], db[1], sm1[2], sm2[2], sm1[0], sm2[0], sm1[1], sm2[1]])
        rows = rows.reshape(8, f_size, dl).transpose(1, 0, 2)
        every = jnp.concatenate([rows, ubg.reshape(f_size, n_up, dl)], axis=1)
        every = lax.psum(every, ("replica", "fsdp"))
        own = lax.dynamic_index_in_dim(every, lax.axis_index("fsdp"), 0, keepdims=False)
    qkv_grad = jnp.concatenate(
        [qkv_cols[g][:, j * gw : (j + 1) * gw] for j in range(3) for g in range(GROUPS)], axis=1
    )
    return (
        result,
        grad_in,
        qkv_grad,
        out_grad,
        up_grad,
        down_grad,
        own[:4],
        own[8:].reshape(ul),
        own[4:6],
        own[6:8],
    )


def solution(mesh):
    both = ("replica", "fsdp")
    return jax.shard_map(
        functools.partial(shards, mesh),
        mesh=mesh,
        in_specs=(
            P(both, None),
            P(both),
            P(both, None, None),
            P("fsdp", None),
            P("fsdp", None),
            P("fsdp", None),
            P("fsdp", None),
            P(None, "fsdp"),
            P("fsdp"),
            P(None, "fsdp"),
            P(None, "fsdp"),
            P(both, None),
        ),
        out_specs=(
            P(both, None),
            P(both, None),
            P("fsdp", None),
            P("fsdp", None),
            P("fsdp", None),
            P("fsdp", None),
            P(None, "fsdp"),
            P("fsdp"),
            P(None, "fsdp"),
            P(None, "fsdp"),
        ),
        check_vma=False,
    )
```
